32 devices in a mesh: dp: 8 (over z, y), tensor: 4 (over x, core).
Axes of the slice: x: 2, y: 2, z: 4, core: 2. Of those that a mesh axis runs over, the one named last changes fastest.
Arguments:
- tokens: bfloat16 [12288, 1280], P('dp'), may hold values from -6 to 6
- clip_len: int32 [5], replicated, may hold values from 31 to 1500, as said below
- slot_clip: int32 [8], P('dp'), may hold values from -1 to 4, as said below
- w_qkv: bfloat16 [1280, 3, 1280], P(None, None, 'tensor'), may hold values from -0.15625 to 0.15625
- bias_q: float32 [1280], P('tensor'), may hold values from -1.5 to 1.5
- bias_v: float32 [1280], P('tensor'), may hold values from -1.5 to 1.5
- w_out: bfloat16 [1280, 1280], P('tensor'), may hold values from -0.625 to 0.625
- bias_out: float32 [1280], replicated, may hold values from -1.5 to 1.5
- w_up: bfloat16 [1280, 5120], P(None, 'tensor'), may hold values from -0.15625 to 0.15625
- bias_up: float32 [5120], P('tensor'), may hold values from -1.5 to 1.5
- w_down: bfloat16 [5120, 1280], P('tensor'), may hold values from -0.078125 to 0.078125
- bias_down: float32 [1280], replicated, may hold values from -1.5 to 1.5
- gain1: float32 [1280], replicated, may hold values from 0.1 to 1.9
- shift1: float32 [1280], replicated, may hold values from -1.5 to 1.5
- gain2: float32 [1280], replicated, may hold values from 0.1 to 1.9
- shift2: float32 [1280], replicated, may hold values from -1.5 to 1.5
- grad_out: bfloat16 [12288, 1280], P('dp')
Outputs:
- mixed: bfloat16 [12288, 1280], P('dp')
- grad_tokens: float32 [12288, 1280], P('dp')
- grad_qkv: float32 [1280, 3, 1280], P(None, None, 'tensor')
- grad_bias_q: float32 [1280], P('tensor')
- grad_bias_v: float32 [1280], P('tensor')
- grad_out_proj: float32 [1280, 1280], P('tensor')
- grad_out_bias: float32 [1280], replicated
- grad_up: float32 [1280, 5120], P(None, 'tensor')
- grad_up_bias: float32 [5120], P('tensor')
- grad_down: float32 [5120, 1280], P('tensor')
- grad_down_bias: float32 [1280], replicated
- grad_gain1: float32 [1280], replicated
- grad_shift1: float32 [1280], replicated
- grad_gain2: float32 [1280], replicated
- grad_shift2: float32 [1280], replicated
The draws below stay inside these ranges and needn't reach their ends.
Inputs may be any that keep to these rules, and one draw needn't show every extreme that they name: `clip_len`: some clip has exactly 1500 frames in every draw; short clips are far more common than long ones. `slot_clip`: every clip stands in exactly one slot; the other slots hold -1; each index of dp holds one slot; some slots are empty (-1), and the clip lengths in the filled slots vary widely.
All inputs are finite; a program needn't handle non-finite values.
Results may differ from the reference program's by a relative error of at most 0.022.
Values may be sent and summed in bfloat16 or wider, within the bound.
A program may use at most 256 MiB of HBM per device.

```python
import math
import jax
import jax.numpy as jnp
from jax import lax

H = 20
HD = 64
D = 1280
FF = 5120
MAXLEN = 1500
CAP = 1536
SLOTS = 1
CLIPS = 5
TOKENS = 12288
N_DP = 8
N_TENSOR = 4


def draw_clip_len(key, part):
    keys = jax.random.split(jax.random.fold_in(key, 3), 5)
    lowest = max(MAXLEN // 48, 1)
    shortest = jax.random.randint(keys[0], (CLIPS,), lowest, MAXLEN + 1)
    for index in range(1, 4):
        shortest = jnp.minimum(shortest, jax.random.randint(keys[index], (CLIPS,), lowest, MAXLEN + 1))
    longest = jax.random.randint(keys[4], (), 0, CLIPS)
    return jnp.where(jnp.arange(CLIPS) == longest, MAXLEN, shortest).astype(jnp.int32)


def draw_slot_clip(key, part):
    first, second = jax.random.split(jax.random.fold_in(key, 5))
    total = N_DP * SLOTS
    order_key = jax.random.permutation(first, total).astype(jnp.int32)
    full_device = jax.random.randint(second, (), 0, N_DP)
    slot_ids = jnp.arange(total, dtype=jnp.int32)
    priority = jnp.where(slot_ids // SLOTS == full_device, 0, 1).astype(jnp.int32) * total + order_key
    order = jnp.argsort(priority, stable=True).astype(jnp.int32)
    table = jnp.full((total,), -1, jnp.int32)
    return table.at[order[:CLIPS]].set(jnp.arange(CLIPS, dtype=jnp.int32))


def draw_grad_out(key, part):
    first, second = jax.random.split(jax.random.fold_in(key, 7))
    count = TOKENS // CAP
    scales = jnp.exp(jax.random.uniform(first, (count, 1, 1), jnp.float32, math.log(0.3), math.log(3.0)))
    base = jax.random.normal(second, (count, CAP, D), jnp.float32)
    return (base * scales).reshape(TOKENS, D).astype(jnp.bfloat16)


def block_levels(rng, dims, pieces, least, top_value):
    loudness = 1.0
    for position, blocks in pieces:
        heights = jax.random.uniform(jax.random.fold_in(jax.random.fold_in(rng, 6), position), (blocks,), jnp.float32, least / len(pieces), top_value / len(pieces))
        loudness = loudness * jnp.repeat(jnp.exp(heights), dims[position] // blocks).reshape((-1,) + (1,) * (len(dims) - 1 - position))
    return loudness


def noise(own_key, shape, spread, most, shards=(), held_as=jnp.bfloat16):
    entries = jax.random.normal(own_key, shape, jnp.float32) * spread
    if len(shards) > 0:
        entries = block_levels(own_key, shape, shards, -0.22, 0.18) * entries
    return jnp.clip(entries, min=-most, max=most).astype(held_as)


def setup_inputs(seed: int = 0) -> dict:
    splits = jax.random.split(jax.random.key(seed), 18)
    tokens = noise(splits[0], (TOKENS, D), 1.0, 6.0, ((0, 8),))
    clip_len = draw_clip_len(jax.random.fold_in(splits[17], 71), 0)
    slot_clip = draw_slot_clip(jax.random.fold_in(splits[17], 71), 0)
    w_qkv = noise(splits[3], (D, 3, D), D ** -0.5, 0.15625, ((2, 4),))
    bias_q = noise(splits[4], (D,), 0.3, 1.5, ((0, 4),), jnp.float32)
    bias_v = noise(splits[5], (D,), 0.3, 1.5, ((0, 4),), jnp.float32)
    w_out = noise(splits[6], (D, D), (D // 16) ** -0.5, 0.625, ((0, 4),))
    bias_out = noise(splits[7], (D,), 0.3, 1.5, (), jnp.float32)
    w_up = noise(splits[8], (D, FF), D ** -0.5, 0.15625, ((1, 4),))
    bias_up = noise(splits[9], (FF,), 0.3, 1.5, ((0, 4),), jnp.float32)
    w_down = noise(splits[10], (FF, D), FF ** -0.5, 0.078125, ((0, 4),))
    bias_down = noise(splits[11], (D,), 0.3, 1.5, (), jnp.float32)
    gain1 = jnp.clip(1.0 + 0.18 * jax.random.normal(splits[12], (D,), jnp.float32), 0.1, 1.9)
    shift1 = noise(splits[13], (D,), 0.3, 1.5, (), jnp.float32)
    gain2 = jnp.clip(1.0 + 0.18 * jax.random.normal(splits[14], (D,), jnp.float32), 0.1, 1.9)
    shift2 = noise(splits[15], (D,), 0.3, 1.5, (), jnp.float32)
    grad_out = draw_grad_out(jax.random.fold_in(splits[17], 71), 0)
    return dict(tokens=tokens, clip_len=clip_len, slot_clip=slot_clip, w_qkv=w_qkv, bias_q=bias_q, bias_v=bias_v, w_out=w_out, bias_out=bias_out, w_up=w_up, bias_up=bias_up, w_down=w_down, bias_down=bias_down, gain1=gain1, shift1=shift1, gain2=gain2, shift2=shift2, grad_out=grad_out)


EPS = 1e-05
NEG = -1e+30
HALF_ROOT = 0.7071067811865476
INV_ROOT_TAU = 0.3989422804014327

def bf16_round(value):
    return lax.optimization_barrier(value.astype(jnp.bfloat16)).astype(jnp.float32)

def layer_norm(value, gain, shift):
    center = value - lax.optimization_barrier(jnp.mean(value, -1, keepdims=True))
    rstd = lax.rsqrt(lax.optimization_barrier(jnp.mean(center * center, -1, keepdims=True)) + EPS)
    normed = center * rstd
    return (normed, rstd, normed * gain + shift)

def layer_norm_back(grad, normed, rstd, gain):
    scaled = grad * gain
    return rstd * (scaled - lax.optimization_barrier(jnp.mean(scaled, -1, keepdims=True)) - normed * lax.optimization_barrier(jnp.mean(scaled * normed, -1, keepdims=True)))

def gelu_pair(value):
    cdf = 0.5 * (1.0 + jax.scipy.special.erf(value * HALF_ROOT))
    return (value * cdf, cdf + value * jnp.exp(-0.5 * value * value) * INV_ROOT_TAU)

def contract_first(left, right):
    return lax.dot_general(left, right, (((0,), (0,)), ((), ())), preferred_element_type=jnp.float32)

def contract_last(left, right):
    return lax.dot_general(left, right, (((1,), (1,)), ((), ())), preferred_element_type=jnp.float32)

def grouped_sum(left, right, groups):
    rows = left.shape[0]
    left_g = left.astype(jnp.float32).reshape(rows, groups, -1)
    right_g = right.astype(jnp.float32).reshape(groups, -1, right.shape[1])
    parts = jnp.einsum('rgk,gkc->grc', left_g, right_g)
    return lax.optimization_barrier(jnp.sum(bf16_round(parts), 0))

def slot_lengths(slot_clip, clip_len):
    match = slot_clip[:, None] == jnp.arange(clip_len.shape[0], dtype=jnp.int32)[None, :]
    return lax.optimization_barrier(jnp.sum(jnp.where(match, clip_len[None, :], 0), 1)).astype(jnp.int32)

def reference(tokens, clip_len, slot_clip, w_qkv, bias_q, bias_v, w_out, bias_out, w_up, bias_up, w_down, bias_down, gain1, shift1, gain2, shift2, grad_out):
    groups = N_TENSOR
    width = tokens.shape[1]
    scale = HD ** (-0.5)
    slot_count = tokens.shape[0] // CAP
    joined = w_qkv.reshape(width, 3 * width)
    local = width // groups
    qkv_right = w_qkv.reshape(width, 3, groups, local).transpose(2, 1, 3, 0).reshape(3 * width, width)
    lengths = slot_lengths(slot_clip, clip_len)

    def clip_step(carry, inputs):
        x_clip, dy_clip, length = inputs
        positions = jnp.arange(CAP, dtype=jnp.int32)
        keep = positions < length
        valid = keep[:, None]
        source = x_clip.astype(jnp.float32)
        normed1, rstd1, pre1 = layer_norm(source, gain1, shift1)
        act1 = pre1.astype(jnp.bfloat16)
        proj = jnp.dot(act1, joined, preferred_element_type=jnp.float32)
        query = (proj[:, :width] + bias_q).astype(jnp.bfloat16)
        keys = proj[:, width:2 * width].astype(jnp.bfloat16)
        values = (proj[:, 2 * width:] + bias_v).astype(jnp.bfloat16)
        q_heads = query.astype(jnp.float32).reshape(CAP, H, HD)
        k_heads = keys.astype(jnp.float32).reshape(CAP, H, HD)
        v_heads = values.astype(jnp.float32).reshape(CAP, H, HD)
        raw = jnp.einsum('qhe,khe->hqk', q_heads, k_heads) * scale
        raw = jnp.where(keep[None, None, :], raw, NEG)
        top = lax.optimization_barrier(jnp.max(raw, -1, keepdims=True))
        lse = top + jnp.log(lax.optimization_barrier(jnp.sum(jnp.exp(raw - top), -1, keepdims=True)))
        probs_f = jnp.exp(raw - lse)
        probs = bf16_round(probs_f)
        context = jnp.einsum('hqk,khe->qhe', probs, v_heads).astype(jnp.bfloat16).reshape(CAP, width)
        attended = grouped_sum(context, w_out, groups)
        middle = source + attended + bias_out
        normed2, rstd2, pre2 = layer_norm(middle, gain2, shift2)
        act2 = pre2.astype(jnp.bfloat16)
        pre = jnp.dot(act2, w_up, preferred_element_type=jnp.float32) + bias_up
        hidden_f, slope = gelu_pair(pre)
        hidden = hidden_f.astype(jnp.bfloat16)
        branch = grouped_sum(hidden, w_down, groups)
        mixed = jnp.where(valid, middle + branch + bias_down, 0.0).astype(jnp.bfloat16)
        upstream = jnp.where(valid, dy_clip.astype(jnp.float32), 0.0)
        upstream_b = upstream.astype(jnp.bfloat16)
        g_down_bias = lax.optimization_barrier(jnp.sum(upstream, 0))
        g_down = contract_first(hidden, upstream_b)
        d_pre = contract_last(upstream_b, w_down) * slope
        g_up_bias = lax.optimization_barrier(jnp.sum(d_pre, 0))
        d_pre_b = d_pre.astype(jnp.bfloat16)
        g_up = contract_first(act2, d_pre_b)
        d_act2 = grouped_sum(d_pre_b, w_up.T, groups)
        g_gain2 = lax.optimization_barrier(jnp.sum(d_act2 * normed2, 0))
        g_shift2 = lax.optimization_barrier(jnp.sum(d_act2, 0))
        d_middle = upstream + layer_norm_back(d_act2, normed2, rstd2, gain2)
        g_out_bias = lax.optimization_barrier(jnp.sum(d_middle, 0))
        d_middle_b = d_middle.astype(jnp.bfloat16)
        g_out = contract_first(context, d_middle_b)
        d_context = contract_last(d_middle_b, w_out).astype(jnp.bfloat16)
        dc_heads = d_context.astype(jnp.float32).reshape(CAP, H, HD)
        c_heads = context.astype(jnp.float32).reshape(CAP, H, HD)
        d_probs = jnp.einsum('qhe,khe->hqk', dc_heads, v_heads)
        delta = lax.optimization_barrier(jnp.sum(dc_heads * c_heads, -1)).T[:, :, None]
        d_scores = bf16_round(probs_f * (d_probs - delta) * scale)
        d_query = jnp.einsum('hqk,khe->qhe', d_scores, k_heads).reshape(CAP, width)
        d_keys = jnp.einsum('hqk,qhe->khe', d_scores, q_heads).reshape(CAP, width)
        d_values = jnp.einsum('hqk,qhe->khe', probs, dc_heads).reshape(CAP, width)
        g_bias_q = lax.optimization_barrier(jnp.sum(d_query, 0))
        g_bias_v = lax.optimization_barrier(jnp.sum(d_values, 0))
        stacked = jnp.concatenate([d_query.astype(jnp.bfloat16), d_keys.astype(jnp.bfloat16), d_values.astype(jnp.bfloat16)], 1)
        g_qkv = contract_first(act1, stacked).reshape(width, 3, width)
        left = stacked.reshape(CAP, 3, groups, local).transpose(0, 2, 1, 3).reshape(CAP, 3 * width)
        d_act1 = grouped_sum(left, qkv_right, groups)
        g_gain1 = lax.optimization_barrier(jnp.sum(d_act1 * normed1, 0))
        g_shift1 = lax.optimization_barrier(jnp.sum(d_act1, 0))
        d_tokens = jnp.where(valid, d_middle + layer_norm_back(d_act1, normed1, rstd1, gain1), 0.0)
        terms = (g_qkv, g_bias_q, g_bias_v, g_out, g_out_bias, g_up, g_up_bias, g_down, g_down_bias, g_gain1, g_shift1, g_gain2, g_shift2)
        carry = tuple((total + term for total, term in zip(carry, terms)))
        return (carry, (mixed, d_tokens))
    start = (jnp.zeros((width, 3, width), jnp.float32), jnp.zeros((width,), jnp.float32), jnp.zeros((width,), jnp.float32), jnp.zeros((width, width), jnp.float32), jnp.zeros((width,), jnp.float32), jnp.zeros((width, FF), jnp.float32), jnp.zeros((FF,), jnp.float32), jnp.zeros((FF, width), jnp.float32), jnp.zeros((width,), jnp.float32), jnp.zeros((width,), jnp.float32), jnp.zeros((width,), jnp.float32), jnp.zeros((width,), jnp.float32), jnp.zeros((width,), jnp.float32))
    totals, (mixed, d_tokens) = lax.scan(clip_step, start, (tokens.reshape(slot_count, CAP, width), grad_out.reshape(slot_count, CAP, width), lengths))
    g_qkv, g_bias_q, g_bias_v, g_out, g_out_bias, g_up, g_up_bias, g_down, g_down_bias, g_gain1, g_shift1, g_gain2, g_shift2 = totals
    return (mixed.reshape(TOKENS, width), d_tokens.reshape(TOKENS, width), g_qkv, g_bias_q, g_bias_v, g_out, g_out_bias, g_up, g_up_bias, g_down, g_down_bias, g_gain1, g_shift1, g_gain2, g_shift2)
```

```python
import functools

import jax
import jax.numpy as jnp
from jax import lax
from jax.experimental import pallas as pl
from jax.experimental.pallas import tpu as pltpu
from jax.sharding import PartitionSpec as P

HD = 64


EPS = 1e-05
NEG = -1e30
HALF_ROOT = 0.7071067811865476
INV_ROOT_TAU = 0.3989422804014327


def layer_norm(value, gain, shift):
    center = value - jnp.mean(value, -1, keepdims=True)
    rstd = lax.rsqrt(jnp.mean(center * center, -1, keepdims=True) + EPS)
    normed = center * rstd
    return (normed, rstd, normed * gain + shift)


def layer_norm_back(grad, normed, rstd, gain):
    scaled = grad * gain
    return rstd * (
        scaled
        - jnp.mean(scaled, -1, keepdims=True)
        - normed * jnp.mean(scaled * normed, -1, keepdims=True)
    )


def gelu_pair(value):
    cdf = 0.5 * (1.0 + jax.scipy.special.erf(value * HALF_ROOT))
    return (value * cdf, cdf + value * jnp.exp(-0.5 * value * value) * INV_ROOT_TAU)


def contract_first(left, right):
    return lax.dot_general(
        left, right, (((0,), (0,)), ((), ())), preferred_element_type=jnp.float32
    )


def contract_last(left, right):
    return lax.dot_general(
        left, right, (((1,), (1,)), ((), ())), preferred_element_type=jnp.float32
    )


def masked_scores(query_clip, keys_clip, length, positions, scale):
    raw = (
        jnp.einsum("qhe,khe->hqk", query_clip, keys_clip, preferred_element_type=jnp.float32)
        * scale
    )
    return jnp.where((positions < length)[None, None, :], raw, NEG)


def plain(
    tokens,
    clip_len,
    slot_clip,
    w_qkv,
    bias_q,
    bias_v,
    w_out,
    bias_out,
    w_up,
    bias_up,
    w_down,
    bias_down,
    gain1,
    shift1,
    gain2,
    shift2,
    grad_out,
):
    rows, width = tokens.shape
    clips = slot_clip.shape[0]
    cap = rows // clips
    local = w_qkv.shape[2]
    heads = local // HD
    scale = HD ** (-0.5)
    positions = jnp.arange(cap, dtype=jnp.int32)
    match = slot_clip[:, None] == jnp.arange(clip_len.shape[0], dtype=jnp.int32)[None, :]
    lengths = jnp.sum(jnp.where(match, clip_len[None, :], 0), 1)
    valid = (positions[None, :] < lengths[:, None]).reshape(rows, 1)
    source = tokens.astype(jnp.float32)
    normed1, rstd1, pre1 = layer_norm(source, gain1, shift1)
    act1 = pre1.astype(jnp.bfloat16)
    joined = w_qkv.reshape(width, 3 * local)
    proj = jnp.dot(act1, joined, preferred_element_type=jnp.float32)
    query = (proj[:, :local] + bias_q).astype(jnp.bfloat16)
    keys = proj[:, local : 2 * local].astype(jnp.bfloat16)
    values = (proj[:, 2 * local :] + bias_v).astype(jnp.bfloat16)

    def per_clip(value):
        return value.reshape(clips, cap, heads, HD)

    def forward_clip(inputs):
        query_clip, keys_clip, values_clip, length = inputs
        raw = masked_scores(query_clip, keys_clip, length, positions, scale)
        top = jnp.max(raw, -1, keepdims=True)
        lse = top + jnp.log(jnp.sum(jnp.exp(raw - top), -1, keepdims=True))
        probs = jnp.exp(raw - lse).astype(jnp.bfloat16)
        context_clip = jnp.einsum(
            "hqk,khe->qhe", probs, values_clip, preferred_element_type=jnp.float32
        )
        return (context_clip.astype(jnp.bfloat16), lse)

    context_all, lse_all = lax.map(
        forward_clip, (per_clip(query), per_clip(keys), per_clip(values), lengths)
    )
    context = context_all.reshape(rows, local)
    attended = lax.psum(
        jnp.dot(context, w_out, preferred_element_type=jnp.float32).astype(jnp.bfloat16), "tensor"
    ).astype(jnp.float32)
    middle = source + attended + bias_out
    normed2, rstd2, pre2 = layer_norm(middle, gain2, shift2)
    act2 = pre2.astype(jnp.bfloat16)
    pre = jnp.dot(act2, w_up, preferred_element_type=jnp.float32) + bias_up
    hidden_f, slope = gelu_pair(pre)
    hidden = hidden_f.astype(jnp.bfloat16)
    branch = lax.psum(
        jnp.dot(hidden, w_down, preferred_element_type=jnp.float32).astype(jnp.bfloat16), "tensor"
    ).astype(jnp.float32)
    mixed = jnp.where(valid, middle + branch + bias_down, 0.0).astype(jnp.bfloat16)
    upstream = jnp.where(valid, grad_out.astype(jnp.float32), 0.0)
    upstream_b = upstream.astype(jnp.bfloat16)
    g_down_bias = jnp.sum(upstream, 0)
    g_down = contract_first(hidden, upstream_b)
    d_pre = contract_last(upstream_b, w_down) * slope
    g_up_bias = jnp.sum(d_pre, 0)
    d_pre_b = d_pre.astype(jnp.bfloat16)
    g_up = contract_first(act2, d_pre_b)
    d_act2 = lax.psum(contract_last(d_pre_b, w_up).astype(jnp.bfloat16), "tensor").astype(
        jnp.float32
    )
    g_gain2 = jnp.sum(d_act2 * normed2, 0)
    g_shift2 = jnp.sum(d_act2, 0)
    d_middle = upstream + layer_norm_back(d_act2, normed2, rstd2, gain2)
    g_out_bias = jnp.sum(d_middle, 0)
    d_middle_b = d_middle.astype(jnp.bfloat16)
    g_out = contract_first(context, d_middle_b)
    d_context = contract_last(d_middle_b, w_out).astype(jnp.bfloat16)

    def backward_clip(inputs):
        query_clip, keys_clip, values_clip, context_clip, dcontext_clip, lse, length = inputs
        raw = masked_scores(query_clip, keys_clip, length, positions, scale)
        probs_f = jnp.exp(raw - lse)
        probs = probs_f.astype(jnp.bfloat16)
        d_probs = jnp.einsum(
            "qhe,khe->hqk", dcontext_clip, values_clip, preferred_element_type=jnp.float32
        )
        delta = jnp.sum(dcontext_clip.astype(jnp.float32) * context_clip.astype(jnp.float32), -1).T[
            :, :, None
        ]
        d_scores = (probs_f * (d_probs - delta) * scale).astype(jnp.bfloat16)
        d_query_clip = jnp.einsum(
            "hqk,khe->qhe", d_scores, keys_clip, preferred_element_type=jnp.float32
        )
        d_keys_clip = jnp.einsum(
            "hqk,qhe->khe", d_scores, query_clip, preferred_element_type=jnp.float32
        )
        d_values_clip = jnp.einsum(
            "hqk,qhe->khe", probs, dcontext_clip, preferred_element_type=jnp.float32
        )
        return (d_query_clip, d_keys_clip, d_values_clip)

    d_query, d_keys, d_values = lax.map(
        backward_clip,
        (
            per_clip(query),
            per_clip(keys),
            per_clip(values),
            context_all,
            per_clip(d_context),
            lse_all,
            lengths,
        ),
    )
    d_query = d_query.reshape(rows, local)
    d_keys = d_keys.reshape(rows, local)
    d_values = d_values.reshape(rows, local)
    g_bias_q = jnp.sum(d_query, 0)
    g_bias_v = jnp.sum(d_values, 0)
    stacked = jnp.concatenate(
        [d_query.astype(jnp.bfloat16), d_keys.astype(jnp.bfloat16), d_values.astype(jnp.bfloat16)],
        1,
    )
    g_qkv = contract_first(act1, stacked).reshape(width, 3, local)
    d_act1 = lax.psum(contract_last(stacked, joined).astype(jnp.bfloat16), "tensor").astype(
        jnp.float32
    )
    g_gain1 = jnp.sum(d_act1 * normed1, 0)
    g_shift1 = jnp.sum(d_act1, 0)
    d_tokens = jnp.where(valid, d_middle + layer_norm_back(d_act1, normed1, rstd1, gain1), 0.0)
    (
        g_qkv,
        g_bias_q,
        g_bias_v,
        g_out,
        g_out_bias,
        g_up,
        g_up_bias,
        g_down,
        g_down_bias,
        g_gain1,
        g_shift1,
        g_gain2,
        g_shift2,
    ) = (
        lax.psum(g_qkv.astype(jnp.bfloat16), "dp").astype(jnp.float32),
        lax.psum(g_bias_q.astype(jnp.bfloat16), "dp").astype(jnp.float32),
        lax.psum(g_bias_v.astype(jnp.bfloat16), "dp").astype(jnp.float32),
        lax.psum(g_out.astype(jnp.bfloat16), "dp").astype(jnp.float32),
        lax.psum(g_out_bias.astype(jnp.bfloat16), "dp").astype(jnp.float32),
        lax.psum(g_up.astype(jnp.bfloat16), "dp").astype(jnp.float32),
        lax.psum(g_up_bias.astype(jnp.bfloat16), "dp").astype(jnp.float32),
        lax.psum(g_down.astype(jnp.bfloat16), "dp").astype(jnp.float32),
        lax.psum(g_down_bias.astype(jnp.bfloat16), "dp").astype(jnp.float32),
        lax.psum(g_gain1.astype(jnp.bfloat16), "dp").astype(jnp.float32),
        lax.psum(g_shift1.astype(jnp.bfloat16), "dp").astype(jnp.float32),
        lax.psum(g_gain2.astype(jnp.bfloat16), "dp").astype(jnp.float32),
        lax.psum(g_shift2.astype(jnp.bfloat16), "dp").astype(jnp.float32),
    )
    return (
        mixed,
        d_tokens,
        g_qkv,
        g_bias_q,
        g_bias_v,
        g_out,
        g_out_bias,
        g_up,
        g_up_bias,
        g_down,
        g_down_bias,
        g_gain1,
        g_shift1,
        g_gain2,
        g_shift2,
    )


MESH = pl.DeviceIdType.MESH
DMA = pltpu.SemaphoreType.DMA
ANY = pl.BlockSpec(memory_space=pl.ANY)
VMEM = pl.BlockSpec(memory_space=pltpu.VMEM)
SMEM = pl.BlockSpec(memory_space=pltpu.SMEM)
BLOCKS = (96,)
BQ = 256
BK = 256


def coords():
    dp = lax.axis_index("dp")
    t = lax.axis_index("tensor")
    return dp // 2, dp % 2, t // 2, t % 2


def device(z, y, x, c):
    return (z * 2 + y, x * 2 + c)


def greet(peers):
    barrier = pltpu.get_barrier_semaphore()
    for peer in peers:
        pl.semaphore_signal(barrier, inc=1, device_id=peer, device_id_type=MESH)
    pl.semaphore_wait(barrier, len(peers))


def greet_grid():
    z, y, x, c = coords()
    barrier = pltpu.get_barrier_semaphore()

    def signal(peer):
        pl.semaphore_signal(barrier, inc=1, device_id=peer, device_id_type=MESH)

    @pl.when(z > 0)
    def _():
        signal(device(z - 1, y, x, c))

    @pl.when(z < 3)
    def _():
        signal(device(z + 1, y, x, c))

    signal(device(z, 1 - y, x, c))
    signal(device(z, y, 1 - x, c))
    signal(device(z, y, x, 1 - c))

    pl.semaphore_wait(barrier, 3 + jnp.minimum(z, 1) + jnp.minimum(3 - z, 1))


GATHER_SEMS = [DMA, DMA((4,)), DMA((4,)), DMA((4,)), DMA((8,)), DMA((16,)), DMA((32,))]


def gather_steps(x_ref, o_ref, local_sem, right_sem, left_sem, u_sem, v_sem, core_sem, recv_sem):
    z, y, x, c = coords()
    size = x_ref.shape[0]

    def block(z, y, x, c):
        return (z * 2 + y) * 4 + x * 2 + c

    def rows(b):
        return o_ref.at[pl.ds(pl.multiple_of(b * size, size), size)]

    ux, uy = x + (1 - c) * (1 - 2 * x), y + c * (1 - 2 * y)
    vx, vy = x + c * (1 - 2 * x), y + (1 - c) * (1 - 2 * y)

    def copy(b, src, sem, peer):
        return pltpu.make_async_remote_copy(
            src_ref=src,
            dst_ref=rows(b),
            send_sem=sem,
            recv_sem=recv_sem.at[b],
            device_id=peer,
            device_id_type=MESH,
        )

    def send_right(b, src, i):
        copy(b, src, right_sem.at[i], device(z + 1, y, x, c)).start()

    def send_left(b, src, i):
        copy(b, src, left_sem.at[i], device(z - 1, y, x, c)).start()

    def send_u(b, src, i):
        copy(b, src, u_sem.at[i], device(z, uy, ux, c)).start()

    def send_v(b, src, i):
        copy(b, src, v_sem.at[i], device(z, vy, vx, c)).start()

    def send_core(b, src, i):
        copy(b, src, core_sem.at[i], device(z, y, x, 1 - c)).start()

    def arrived(b):
        copy(b, x_ref, core_sem.at[0], device(z, y, x, 1 - c)).wait_recv()

    own = block(z, y, x, c)
    local = pltpu.make_async_copy(x_ref, rows(own), local_sem)
    local.start()

    @pl.when(z < 3)
    def _():
        send_right(own, x_ref, z)

    @pl.when(z > 0)
    def _():
        send_left(own, x_ref, z)

    send_u(own, x_ref, z)
    send_v(own, x_ref, z)
    send_core(own, x_ref, z)

    def got_line(at):
        b = block(at, y, x, c)
        arrived(b)

        @pl.when((at < z) & (z < 3))
        def _():
            send_right(b, rows(b), at)

        @pl.when((at > z) & (z > 0))
        def _():
            send_left(b, rows(b), at)

        send_u(b, rows(b), at)
        send_v(b, rows(b), at)
        send_core(b, rows(b), at)

    def got_u(at):
        b = block(at, uy, ux, c)
        arrived(b)
        send_v(b, rows(b), 4 + at)
        send_core(b, rows(b), 4 + at)

    def got_v(at):
        b = block(at, vy, vx, c)
        arrived(b)
        send_core(b, rows(b), 8 + at)

    def got_uv(at):
        b = block(at, 1 - y, 1 - x, c)
        arrived(b)
        send_core(b, rows(b), 12 + at)

    def around(step, distance):
        for side in (-1, 1) if distance else (0,):
            at = z + side * distance
            pl.when((at >= 0) & (at < 4))(functools.partial(step, at))

    for distance in range(4):
        if distance:
            around(got_line, distance)
        around(got_u, distance)
    for distance in range(4):
        around(got_v, distance)
        around(got_uv, distance)

    @pl.loop(0, 16)
    def _(i):
        arrived((i // 2) * 4 + (i % 2) * 2 + 1 - c)

    local.wait()

    def sent(sem):
        copy(own, x_ref, sem, device(z, y, x, 1 - c)).wait_send()

    @pl.loop(0, 16)
    def _(i):
        sent(core_sem.at[i])

    @pl.loop(0, 8)
    def _(i):
        sent(v_sem.at[i])

    @pl.loop(0, 4)
    def _(i):
        sent(u_sem.at[i])

        @pl.when((i <= z) & (z < 3))
        def _():
            sent(right_sem.at[i])

        @pl.when((i >= z) & (z > 0))
        def _():
            sent(left_sem.at[i])


def gather_kernel(*refs):
    greet_grid()
    n = len(GATHER_SEMS)
    arrays = len(refs) // (n + 2)
    for a in range(arrays):
        gather_steps(refs[a], refs[arrays + a], *refs[2 * arrays + a * n : 2 * arrays + (a + 1) * n])


def gather32(arrays, spare, cid):
    return pl.pallas_call(
        gather_kernel,
        out_shape=[
            jax.ShapeDtypeStruct((32 * a.shape[0] + e, a.shape[1]), a.dtype)
            for a, e in zip(arrays, spare)
        ],
        in_specs=[ANY] * len(arrays),
        out_specs=[ANY] * len(arrays),
        scratch_shapes=GATHER_SEMS * len(arrays),
        compiler_params=pltpu.CompilerParams(collective_id=cid, has_side_effects=True),
        name="gather32",
    )(*arrays)


def table_kernel(x_ref, o_ref, send_sem, recv_sem):
    me = lax.axis_index("dp")
    t = lax.axis_index("tensor")
    peers = [(lax.rem(me + s, 8), t) for s in range(1, 8)]
    greet(peers)
    o_ref[me] = x_ref[...]
    copies = [
        pltpu.make_async_remote_copy(
            src_ref=x_ref,
            dst_ref=o_ref.at[me],
            send_sem=send_sem.at[s],
            recv_sem=recv_sem.at[s],
            device_id=peer,
            device_id_type=MESH,
        )
        for s, peer in enumerate(peers)
    ]
    for copy in copies:
        copy.start()
    for copy in copies:
        copy.wait()


def gather_table(value, cid):
    tile = jnp.broadcast_to(value.reshape(1, 1), (8, 128))
    out = pl.pallas_call(
        table_kernel,
        out_shape=jax.ShapeDtypeStruct((8, 8, 128), value.dtype),
        in_specs=[VMEM],
        out_specs=VMEM,
        scratch_shapes=[DMA((7,)), DMA((7,))],
        compiler_params=pltpu.CompilerParams(collective_id=cid, has_side_effects=True),
        name="table",
    )(tile)
    return out[:, 0, 0]


def pieces_kernel(size, info_ref, x_ref, u_ref, xo_ref, uo_ref, held, sems):
    t = lax.axis_index("tensor")
    cap = x_ref.shape[0]
    offset = info_ref[0]
    length = info_ref[1]
    loads = [
        pltpu.make_async_copy(src, held.at[i, pl.ds(size, cap)], sems.at[i])
        for i, src in enumerate((x_ref, u_ref))
    ]
    for load in loads:
        load.start()
    for i in (0, 1):
        held[i, 0:size, :] = jnp.zeros((size, held.shape[2]), held.dtype)
        held[i, size + cap :, :] = jnp.zeros((size, held.shape[2]), held.dtype)
    for i, out in enumerate((xo_ref, uo_ref)):
        loads[i].wait()

        @pl.loop(0, 8)
        def _(b):
            first = (b * 4 + t) * size - offset + size
            first = pl.multiple_of(jnp.clip(first, 0, cap + size), 16)
            row = lax.broadcasted_iota(jnp.int32, (size, 1), 0) + first - size
            value = held[i, pl.ds(first, size), :].astype(jnp.float32)
            value = jnp.where((row >= 0) & (row < length), value, 0.0)
            out[b] = value.astype(jnp.bfloat16)


def take_pieces(x, u, info, size):
    cap, width = x.shape
    shape = jax.ShapeDtypeStruct((8, size, width), jnp.bfloat16)
    return pl.pallas_call(
        functools.partial(pieces_kernel, size),
        out_shape=(shape, shape),
        in_specs=[SMEM, ANY, ANY],
        out_specs=(VMEM, VMEM),
        scratch_shapes=[pltpu.VMEM((2, cap + 2 * size, width), jnp.bfloat16), DMA((2,))],
        compiler_params=pltpu.CompilerParams(vmem_limit_bytes=40 << 20),
        name="pieces",
    )(info, x, u)


def pack_kernel(
    p_ref,
    o_ref,
    acc,
    own,
    y_out,
    y_in,
    r_out,
    r_in,
    l_out,
    l_in,
    ys,
    yr,
    rs,
    rr,
    ls,
    lr,
    *gather_sems,
):
    z, y, x, c = coords()
    greet_grid()

    def piece(zp, yp):
        return p_ref[zp * 2 + yp].astype(jnp.float32)

    def y_copy(i):
        return pltpu.make_async_remote_copy(
            src_ref=y_out.at[i],
            dst_ref=y_in.at[i],
            send_sem=ys.at[i],
            recv_sem=yr.at[i],
            device_id=device(z, 1 - y, x, c),
            device_id_type=MESH,
        )

    def r_copy(i):
        return pltpu.make_async_remote_copy(
            src_ref=r_out.at[i],
            dst_ref=r_in.at[i],
            send_sem=rs.at[i],
            recv_sem=rr.at[i],
            device_id=device(z + 1, y, x, c),
            device_id_type=MESH,
        )

    def l_copy(i):
        return pltpu.make_async_remote_copy(
            src_ref=l_out.at[i],
            dst_ref=l_in.at[i],
            send_sem=ls.at[i],
            recv_sem=lr.at[i],
            device_id=device(z - 1, y, x, c),
            device_id_type=MESH,
        )

    def add(ref, copy, i):
        copy(i).wait_recv()
        acc[...] += ref[i].astype(jnp.float32)

    def flow(zp, yp, first):
        i = zp * 2 + yp

        @pl.when(z < zp)
        def _():
            first()

            @pl.when(z > 0)
            def _():
                add(r_in, r_copy, i)

            r_out[i] = acc[...].astype(jnp.bfloat16)
            r_copy(i).start()

        @pl.when(z > zp)
        def _():
            first()

            @pl.when(z < 3)
            def _():
                add(l_in, l_copy, i)

            l_out[i] = acc[...].astype(jnp.bfloat16)
            l_copy(i).start()

    def land(yp):
        @pl.when(z > 0)
        def _():
            add(r_in, r_copy, z * 2 + yp)

        @pl.when(z < 3)
        def _():
            add(l_in, l_copy, z * 2 + yp)

    order = (0, 3, 1, 2)

    @pl.when(c == 0)
    def _():
        for zp in order:
            y_out[zp] = piece(zp, 1 - y).astype(jnp.bfloat16)
            y_copy(zp).start()
        for zp in order:

            def first(zp=zp):
                acc[...] = piece(zp, y)
                add(y_in, y_copy, zp)

            flow(zp, y, first)
        acc[...] = piece(z, y)
        add(y_in, y_copy, z)
        land(y)
        own[...] = acc[...].astype(jnp.bfloat16)
        for zp in order:
            y_copy(zp).wait_send()

    @pl.when(c == 1)
    def _():
        for zp in order:
            for yp in (0, 1):

                def first(zp=zp, yp=yp):
                    acc[...] = piece(zp, yp)

                flow(zp, yp, first)
        acc[...] = piece(z, 1 - y)
        land(1 - y)
        y_out[0] = acc[...].astype(jnp.bfloat16)
        y_copy(0).start()
        acc[...] = piece(z, y)
        land(y)
        add(y_in, y_copy, 0)
        own[...] = acc[...].astype(jnp.bfloat16)
        y_copy(0).wait_send()

    for zp in range(4):
        for yp in (0, 1):
            used = (c == 1) | (y == yp)

            @pl.when(used & (z < zp))
            def _(i=zp * 2 + yp):
                r_copy(i).wait_send()

            @pl.when(used & (z > zp))
            def _(i=zp * 2 + yp):
                l_copy(i).wait_send()

    gather_steps(own, o_ref, *gather_sems)


def pack_gather(parts, cid):
    _, size, width = parts.shape
    bf16 = jnp.bfloat16
    slots = pltpu.VMEM((8, size, width), bf16)
    quarter = pltpu.VMEM((4, size, width), bf16)
    return pl.pallas_call(
        pack_kernel,
        out_shape=jax.ShapeDtypeStruct((32 * size, width), bf16),
        in_specs=[VMEM],
        out_specs=ANY,
        scratch_shapes=[
            pltpu.VMEM((size, width), jnp.float32),
            pltpu.VMEM((size, width), bf16),
            quarter,
            quarter,
            slots,
            slots,
            slots,
            slots,
            DMA((4,)),
            DMA((4,)),
            DMA((8,)),
            DMA((8,)),
            DMA((8,)),
            DMA((8,)),
        ]
        + GATHER_SEMS,
        compiler_params=pltpu.CompilerParams(
            collective_id=cid, has_side_effects=True, vmem_limit_bytes=40 << 20
        ),
        name="pack_gather",
    )(parts)


def share_kernel(p_ref, o_ref, landed, send_sem, recv_sem):
    dp = lax.axis_index("dp")
    t = lax.axis_index("tensor")
    peers = [lax.rem(t + s, 4) for s in (2, 3, 1)]
    greet([(dp, peer) for peer in peers])
    copies = [
        pltpu.make_async_remote_copy(
            src_ref=p_ref.at[peer],
            dst_ref=landed.at[s],
            send_sem=send_sem.at[s],
            recv_sem=recv_sem.at[s],
            device_id=(dp, peer),
            device_id_type=MESH,
        )
        for s, peer in enumerate(peers)
    ]
    for copy in copies:
        copy.start()
    total = p_ref[t].astype(jnp.float32)
    for s, copy in enumerate(copies):
        copy.wait_recv()
        total += landed[s].astype(jnp.float32)
    o_ref[...] = total
    for copy in copies:
        copy.wait_send()


def share4(parts, cid):
    rows, width = parts.shape
    size = rows // 4
    return pl.pallas_call(
        share_kernel,
        out_shape=jax.ShapeDtypeStruct((size, width), jnp.float32),
        in_specs=[VMEM],
        out_specs=VMEM,
        scratch_shapes=[pltpu.VMEM((3, size, width), parts.dtype), DMA((3,)), DMA((3,))],
        compiler_params=pltpu.CompilerParams(
            collective_id=cid, has_side_effects=True, vmem_limit_bytes=24 << 20
        ),
        name="share4",
    )(parts.reshape(4, size, width))


def dot_nt(a, b):
    return lax.dot_general(a, b, (((1,), (1,)), ((), ())), preferred_element_type=jnp.float32)


def dot_nn(a, b):
    return lax.dot_general(a, b, (((1,), (0,)), ((), ())), preferred_element_type=jnp.float32)


def attend_kernel(heads, klo, khi, qkv_ref, vt_ref, seg_ref, ctx_ref, lse_ref, m_s, l_s, acc_s):
    i = pl.program_id(0)
    q0 = pl.multiple_of(i * BQ, BQ)
    local = heads * HD
    span = range(heads)
    start = seg_ref[0:1, pl.ds(q0, BQ)]
    end = seg_ref[1:2, pl.ds(q0, BQ)]
    m_s[...] = jnp.full_like(m_s, NEG)
    l_s[...] = jnp.zeros_like(l_s)
    acc_s[...] = jnp.zeros_like(acc_s)
    q = [qkv_ref[pl.ds(q0, BQ), h * HD : (h + 1) * HD] for h in span]

    def body(kb, carry):
        k0 = pl.multiple_of(kb * BK, BK)
        key = lax.broadcasted_iota(jnp.int32, (BK, BQ), 0) + k0
        mask = (key >= start) & (key < end)
        s = [
            jnp.where(
                mask,
                dot_nt(qkv_ref[pl.ds(k0, BK), local + h * HD : local + (h + 1) * HD], q[h]),
                NEG,
            )
            for h in span
        ]
        p, a = [], []
        for h in span:
            old = m_s[h]
            new = jnp.maximum(old, jnp.max(s[h], 0, keepdims=True))
            e = jnp.exp(s[h] - new)
            scale = jnp.exp(old - new)
            l_s[h] = scale * l_s[h] + jnp.sum(e, 0, keepdims=True)
            m_s[h] = new
            p.append(e.astype(jnp.bfloat16))
            a.append(scale)
        for h in span:
            vt = vt_ref[h * HD : (h + 1) * HD, pl.ds(k0, BK)]
            acc_s[h] = a[h] * acc_s[h] + dot_nn(vt, p[h])
        return carry

    lax.fori_loop(klo[i], khi[i], body, 0)
    for h in span:
        total = l_s[h]
        total = jnp.where(total == 0.0, 1.0, total)
        lse_ref[h : h + 1, :] = m_s[h] + jnp.log(total)
        out = acc_s[h] * (1.0 / total)
        ctx_ref[:, h * HD : (h + 1) * HD] = out.T.astype(jnp.bfloat16)


def whole(a):
    return pl.BlockSpec(a.shape, lambda i, *_: (0,) * len(a.shape), pipeline_mode=pl.Buffered(1))


def attend(qkv, vt, seg, klo, khi, heads):
    rows = qkv.shape[0]
    local = heads * HD
    row = pltpu.VMEM((heads, 1, BQ), jnp.float32)
    return pl.pallas_call(
        functools.partial(attend_kernel, heads),
        out_shape=(
            jax.ShapeDtypeStruct((rows, local), jnp.bfloat16),
            jax.ShapeDtypeStruct((8, rows), jnp.float32),
        ),
        grid_spec=pltpu.PrefetchScalarGridSpec(
            num_scalar_prefetch=2,
            grid=(rows // BQ,),
            in_specs=[whole(qkv), whole(vt), whole(seg)],
            out_specs=[
                pl.BlockSpec((BQ, local), lambda i, *_: (i, 0)),
                pl.BlockSpec((8, BQ), lambda i, *_: (0, i)),
            ],
            scratch_shapes=[row, row, pltpu.VMEM((heads, HD, BQ), jnp.float32)],
        ),
        compiler_params=pltpu.CompilerParams(vmem_limit_bytes=40 << 20),
        name="attend",
    )(klo, khi, qkv, vt, seg)


def attend_back_kernel(
    heads, klo, khi, qkv_ref, kt_ref, do_ref, ctx_ref, lse_ref, seg_ref, d_ref, dbq_ref, dbv_ref, dk_s, dv_s, dq_s
):
    i = pl.program_id(0)
    n = pl.num_programs(0)
    q0 = pl.multiple_of(i * BQ, BQ)
    local = heads * HD
    span = range(heads)

    @pl.when(i == 0)
    def _():
        dk_s[...] = jnp.zeros_like(dk_s)
        dv_s[...] = jnp.zeros_like(dv_s)
        dbq_ref[...] = jnp.zeros_like(dbq_ref)
        dbv_ref[...] = jnp.zeros_like(dbv_ref)

    start = seg_ref[0:1, pl.ds(q0, BQ)]
    end = seg_ref[1:2, pl.ds(q0, BQ)]
    dq_s[...] = jnp.zeros_like(dq_s)
    delta = []
    for h in span:
        sl = slice(h * HD, (h + 1) * HD)
        both = do_ref[pl.ds(q0, BQ), sl].astype(jnp.float32) * ctx_ref[pl.ds(q0, BQ), sl].astype(jnp.float32)
        delta.append(jnp.sum(both.T, 0, keepdims=True))

    def body(kb, carry):
        k0 = pl.multiple_of(kb * BK, BK)
        key = lax.broadcasted_iota(jnp.int32, (BK, BQ), 0) + k0
        mask = (key >= start) & (key < end)
        q = [qkv_ref[pl.ds(q0, BQ), h * HD : (h + 1) * HD] for h in span]
        do = [do_ref[pl.ds(q0, BQ), h * HD : (h + 1) * HD] for h in span]
        s = [
            dot_nt(qkv_ref[pl.ds(k0, BK), local + h * HD : local + (h + 1) * HD], q[h])
            for h in span
        ]
        dp = [
            dot_nt(qkv_ref[pl.ds(k0, BK), 2 * local + h * HD : 2 * local + (h + 1) * HD], do[h])
            for h in span
        ]
        p = [
            jnp.exp(jnp.where(mask, s[h], NEG) - lse_ref[h : h + 1, pl.ds(q0, BQ)]) for h in span
        ]
        ds = [(p[h] * (dp[h] - delta[h])).astype(jnp.bfloat16) for h in span]
        pb = [p[h].astype(jnp.bfloat16) for h in span]
        for h in span:
            dv_s[h, pl.ds(k0, BK), :] += dot_nn(pb[h], do[h])
        for h in span:
            dk_s[h, pl.ds(k0, BK), :] += dot_nn(ds[h], q[h])
        for h in span:
            dq_s[h] += dot_nn(kt_ref[h * HD : (h + 1) * HD, pl.ds(k0, BK)], ds[h])
        return carry

    lax.fori_loop(klo[i], khi[i], body, 0)
    for h in span:
        dq = dq_s[h].T * 0.125
        d_ref[pl.ds(q0, BQ), h * HD : (h + 1) * HD] = dq.astype(jnp.bfloat16)
        dbq_ref[h : h + 1, :] += jnp.sum(dq, 0, keepdims=True)

    @pl.when(i == n - 1)
    def _():
        for h in span:

            def finish(j, carry):
                r = pl.ds(pl.multiple_of(j * BK, BK), BK)
                dk = dk_s[h, r, :]
                dv = dv_s[h, r, :]
                d_ref[r, local + h * HD : local + (h + 1) * HD] = dk.astype(jnp.bfloat16)
                d_ref[r, 2 * local + h * HD : 2 * local + (h + 1) * HD] = dv.astype(jnp.bfloat16)
                return carry + jnp.sum(dv, 0, keepdims=True)

            dbv_ref[h : h + 1, :] = lax.fori_loop(0, n, finish, jnp.zeros((1, HD), jnp.float32))


def attend_back(qkv, kt, do, ctx, lse, seg, klo, khi, heads):
    rows = qkv.shape[0]
    local = heads * HD

    def const(shape):
        return pl.BlockSpec(shape, lambda i, *_: (0, 0), pipeline_mode=pl.Buffered(1))

    tall = pltpu.VMEM((heads, rows, HD), jnp.float32)
    return pl.pallas_call(
        functools.partial(attend_back_kernel, heads),
        out_shape=(
            jax.ShapeDtypeStruct((rows, 3 * local), jnp.bfloat16),
            jax.ShapeDtypeStruct((8, HD), jnp.float32),
            jax.ShapeDtypeStruct((8, HD), jnp.float32),
        ),
        grid_spec=pltpu.PrefetchScalarGridSpec(
            num_scalar_prefetch=2,
            grid=(rows // BQ,),
            in_specs=[whole(qkv), whole(kt), whole(do), whole(ctx), whole(lse), whole(seg)],
            out_specs=[const((rows, 3 * local)), const((8, HD)), const((8, HD))],
            scratch_shapes=[tall, tall, pltpu.VMEM((heads, HD, BQ), jnp.float32)],
        ),
        compiler_params=pltpu.CompilerParams(vmem_limit_bytes=60 << 20),
        name="attend_back",
    )(klo, khi, qkv, kt, do, ctx, lse, seg)


def packed_step(size, cids, offset, length, offsets, lengths, args):
    (
        tokens, _, _, w_qkv, bias_q, bias_v, w_out, bias_out, w_up, bias_up, w_down, bias_down,
        gain1, shift1, gain2, shift2, grad_out,
    ) = args
    f32, bf16 = jnp.float32, jnp.bfloat16
    cap, width = tokens.shape
    local = w_qkv.shape[2]
    heads = local // HD
    rows = 32 * size
    mine = 4 * size
    dp = lax.axis_index("dp")
    t = lax.axis_index("tensor")
    pack_id, gather_id, share_id, last_id = cids

    def own(value, count=mine, at=None):
        first = dp * mine if at is None else at
        return lax.dynamic_slice_in_dim(value, first, count, 0)

    at_block = (dp * 4 + t) * size
    info = jnp.stack([offset, length])
    x_parts, up_parts = take_pieces(tokens, grad_out, info, size)
    x_all = pack_gather(x_parts, pack_id)
    up_all = pack_gather(up_parts, pack_id)

    index = jnp.arange(rows, dtype=jnp.int32)
    inside = (index[None, :] >= offsets[:, None]) & (index[None, :] < (offsets + lengths)[:, None])
    start = jnp.sum(jnp.where(inside, offsets[:, None], 0), 0)
    end = jnp.sum(jnp.where(inside, (offsets + lengths)[:, None], 0), 0)
    seg = jnp.concatenate([start[None], end[None], jnp.zeros((6, rows), jnp.int32)], 0)
    taken = end > 0
    first_key = jnp.min(jnp.where(taken, start, rows).reshape(-1, BQ), 1)
    last_key = jnp.max(end.reshape(-1, BQ), 1)
    klo = jnp.where(last_key > 0, first_key // BK, 0)
    khi = (last_key + BK - 1) // BK

    _, _, pre1 = layer_norm(x_all.astype(f32), gain1, shift1)
    act1 = pre1.astype(bf16)
    joined = w_qkv.reshape(width, 3 * local)
    bias = jnp.concatenate([bias_q, jnp.zeros_like(bias_q), bias_v])
    scale = jnp.concatenate([jnp.full((local,), HD**-0.5, bf16), jnp.ones((2 * local,), bf16)])
    qkv = (jnp.dot(act1, joined, preferred_element_type=f32) + bias).astype(bf16) * scale
    context, lse = attend(qkv, qkv[:, 2 * local :].T, seg, klo, khi, heads)
    part = jnp.dot(own(context), w_out, preferred_element_type=f32).astype(bf16)
    attended = share4(part, share_id)
    source = own(x_all, size, at_block).astype(f32)
    middle = source + attended + bias_out
    normed2, rstd2, pre2 = layer_norm(middle, gain2, shift2)
    (act2,) = gather32([pre2.astype(bf16)], [cap], gather_id)
    act2 = act2[:rows]

    pre = jnp.dot(act2, w_up, preferred_element_type=f32) + bias_up
    hidden_f, slope = gelu_pair(pre)
    hidden = hidden_f.astype(bf16)
    d_pre = contract_last(up_all, w_down) * slope
    g_up_bias = jnp.sum(d_pre, 0)
    d_pre_b = d_pre.astype(bf16)
    d_act2 = share4(contract_last(own(d_pre_b), w_up).astype(bf16), share_id)
    upstream = own(up_all, size, at_block).astype(f32)
    d_middle = upstream + layer_norm_back(d_act2, normed2, rstd2, gain2)
    (d_middle_b,) = gather32([d_middle.astype(bf16)], [cap], gather_id)
    d_middle_b = d_middle_b[:rows]
    g_down = contract_first(hidden, up_all)
    g_up = contract_first(act2, d_pre_b)
    g_down_bias = jnp.sum(up_all.astype(f32), 0)
    branch = share4(
        jnp.dot(own(hidden), w_down, preferred_element_type=f32).astype(bf16), share_id
    )
    (mixed_all,) = gather32([(middle + branch + bias_down).astype(bf16)], [cap], gather_id)

    g_out_bias = jnp.sum(d_middle_b.astype(f32), 0)
    g_out = contract_first(context, d_middle_b)
    d_context = contract_last(d_middle_b, w_out).astype(bf16)
    d_qkv, dbq, dbv = attend_back(
        qkv, qkv[:, local : 2 * local].T, d_context, context, lse, seg, klo, khi, heads
    )
    g_bias_q = dbq[:heads].reshape(local)
    g_bias_v = dbv[:heads].reshape(local)
    g_qkv = contract_first(act1, d_qkv).reshape(width, 3, local)
    d_act1 = share4(contract_last(own(d_qkv), joined).astype(bf16), share_id)
    normed1, rstd1, _ = layer_norm(source, gain1, shift1)
    d_tokens = d_middle + layer_norm_back(d_act1, normed1, rstd1, gain1)
    vectors = jnp.stack(
        [
            jnp.sum(d_act1 * normed1, 0),
            jnp.sum(d_act1, 0),
            jnp.sum(d_act2 * normed2, 0),
            jnp.sum(d_act2, 0),
        ]
        + [jnp.zeros((width,), f32)] * 4
    )
    d_tokens_all, vectors_all = gather32([d_tokens.astype(bf16), vectors], [cap, 0], last_id)
    sums = jnp.sum(vectors_all.reshape(32, 8, width), 0)
    valid = (jnp.arange(cap, dtype=jnp.int32) < length)[:, None]

    def slot(value):
        return jnp.where(valid, own(value, cap, offset), jnp.zeros((), value.dtype))

    return (
        slot(mixed_all),
        slot(d_tokens_all).astype(f32),
        g_qkv,
        g_bias_q,
        g_bias_v,
        g_out,
        g_out_bias,
        g_up,
        g_up_bias,
        g_down,
        g_down_bias,
        sums[0],
        sums[1],
        sums[2],
        sums[3],
    )


def packed(*args):
    clip_len, slot_clip = args[1], args[2]
    clips = clip_len.shape[0]

    def padded(value):
        return (value + 15) // 16 * 16

    need = jnp.sum(padded(clip_len))
    table = gather_table(slot_clip[0], 0)
    match = table[:, None] == jnp.arange(clips, dtype=jnp.int32)[None, :]
    lengths = jnp.sum(jnp.where(match, clip_len[None, :], 0), 1)
    offsets = jnp.cumsum(padded(lengths)) - padded(lengths)
    dp = lax.axis_index("dp")
    length = lengths[dp]
    offset = offsets[dp]
    branches = [
        functools.partial(packed_step, size, [1 + 4 * n + i for i in range(4)])
        for n, size in enumerate(BLOCKS)
    ]
    pick = sum((need > 32 * size).astype(jnp.int32) for size in BLOCKS)

    def fallback(offset, length, offsets, lengths, args):
        return plain(*args)

    return lax.switch(pick, branches + [fallback], offset, length, offsets, lengths, args)


def solution(mesh):
    placed = (
        P("dp", None),
        P(),
        P("dp"),
        P(None, None, "tensor"),
        P("tensor"),
        P("tensor"),
        P("tensor", None),
        P(),
        P(None, "tensor"),
        P("tensor"),
        P("tensor", None),
        P(),
        P(),
        P(),
        P(),
        P(),
        P("dp", None),
    )
    fits = mesh.shape["dp"] == 8 and mesh.shape["tensor"] == 4
    return jax.shard_map(
        packed if fits else plain,
        mesh=mesh,
        in_specs=placed,
        out_specs=(
            P("dp", None),
            P("dp", None),
            P(None, None, "tensor"),
            P("tensor"),
            P("tensor"),
            P("tensor", None),
            P(),
            P(None, "tensor"),
            P("tensor"),
            P("tensor", None),
            P(),
            P(),
            P(),
            P(),
            P(),
        ),
        check_vma=False,
    )
```

```python
import functools

import jax
import jax.numpy as jnp
from jax import lax
from jax.experimental import pallas as pl
from jax.experimental.pallas import tpu as pltpu
from jax.sharding import PartitionSpec as P

HD = 64


EPS = 1e-05
NEG = -1e30
HALF_ROOT = 0.7071067811865476
INV_ROOT_TAU = 0.3989422804014327


def layer_norm(value, gain, shift):
    center = value - jnp.mean(value, -1, keepdims=True)
    rstd = lax.rsqrt(jnp.mean(center * center, -1, keepdims=True) + EPS)
    normed = center * rstd
    return (normed, rstd, normed * gain + shift)


def layer_norm_back(grad, normed, rstd, gain):
    scaled = grad * gain
    return rstd * (
        scaled
        - jnp.mean(scaled, -1, keepdims=True)
        - normed * jnp.mean(scaled * normed, -1, keepdims=True)
    )


def gelu_pair(value):
    cdf = 0.5 * (1.0 + jax.scipy.special.erf(value * HALF_ROOT))
    return (value * cdf, cdf + value * jnp.exp(-0.5 * value * value) * INV_ROOT_TAU)


def contract_first(left, right):
    return lax.dot_general(
        left, right, (((0,), (0,)), ((), ())), preferred_element_type=jnp.float32
    )


def contract_last(left, right):
    return lax.dot_general(
        left, right, (((1,), (1,)), ((), ())), preferred_element_type=jnp.float32
    )


def masked_scores(query_clip, keys_clip, length, positions, scale):
    raw = (
        jnp.einsum("qhe,khe->hqk", query_clip, keys_clip, preferred_element_type=jnp.float32)
        * scale
    )
    return jnp.where((positions < length)[None, None, :], raw, NEG)


def plain(
    tokens,
    clip_len,
    slot_clip,
    w_qkv,
    bias_q,
    bias_v,
    w_out,
    bias_out,
    w_up,
    bias_up,
    w_down,
    bias_down,
    gain1,
    shift1,
    gain2,
    shift2,
    grad_out,
):
    rows, width = tokens.shape
    clips = slot_clip.shape[0]
    cap = rows // clips
    local = w_qkv.shape[2]
    heads = local // HD
    scale = HD ** (-0.5)
    positions = jnp.arange(cap, dtype=jnp.int32)
    match = slot_clip[:, None] == jnp.arange(clip_len.shape[0], dtype=jnp.int32)[None, :]
    lengths = jnp.sum(jnp.where(match, clip_len[None, :], 0), 1)
    valid = (positions[None, :] < lengths[:, None]).reshape(rows, 1)
    source = tokens.astype(jnp.float32)
    normed1, rstd1, pre1 = layer_norm(source, gain1, shift1)
    act1 = pre1.astype(jnp.bfloat16)
    joined = w_qkv.reshape(width, 3 * local)
    proj = jnp.dot(act1, joined, preferred_element_type=jnp.float32)
    query = (proj[:, :local] + bias_q).astype(jnp.bfloat16)
    keys = proj[:, local : 2 * local].astype(jnp.bfloat16)
    values = (proj[:, 2 * local :] + bias_v).astype(jnp.bfloat16)

    def per_clip(value):
        return value.reshape(clips, cap, heads, HD)

    def forward_clip(inputs):
        query_clip, keys_clip, values_clip, length = inputs
        raw = masked_scores(query_clip, keys_clip, length, positions, scale)
        top = jnp.max(raw, -1, keepdims=True)
        lse = top + jnp.log(jnp.sum(jnp.exp(raw - top), -1, keepdims=True))
        probs = jnp.exp(raw - lse).astype(jnp.bfloat16)
        context_clip = jnp.einsum(
            "hqk,khe->qhe", probs, values_clip, preferred_element_type=jnp.float32
        )
        return (context_clip.astype(jnp.bfloat16), lse)

    context_all, lse_all = lax.map(
        forward_clip, (per_clip(query), per_clip(keys), per_clip(values), lengths)
    )
    context = context_all.reshape(rows, local)
    attended = lax.psum(
        jnp.dot(context, w_out, preferred_element_type=jnp.float32).astype(jnp.bfloat16), "tensor"
    ).astype(jnp.float32)
    middle = source + attended + bias_out
    normed2, rstd2, pre2 = layer_norm(middle, gain2, shift2)
    act2 = pre2.astype(jnp.bfloat16)
    pre = jnp.dot(act2, w_up, preferred_element_type=jnp.float32) + bias_up
    hidden_f, slope = gelu_pair(pre)
    hidden = hidden_f.astype(jnp.bfloat16)
    branch = lax.psum(
        jnp.dot(hidden, w_down, preferred_element_type=jnp.float32).astype(jnp.bfloat16), "tensor"
    ).astype(jnp.float32)
    mixed = jnp.where(valid, middle + branch + bias_down, 0.0).astype(jnp.bfloat16)
    upstream = jnp.where(valid, grad_out.astype(jnp.float32), 0.0)
    upstream_b = upstream.astype(jnp.bfloat16)
    g_down_bias = jnp.sum(upstream, 0)
    g_down = contract_first(hidden, upstream_b)
    d_pre = contract_last(upstream_b, w_down) * slope
    g_up_bias = jnp.sum(d_pre, 0)
    d_pre_b = d_pre.astype(jnp.bfloat16)
    g_up = contract_first(act2, d_pre_b)
    d_act2 = lax.psum(contract_last(d_pre_b, w_up).astype(jnp.bfloat16), "tensor").astype(
        jnp.float32
    )
    g_gain2 = jnp.sum(d_act2 * normed2, 0)
    g_shift2 = jnp.sum(d_act2, 0)
    d_middle = upstream + layer_norm_back(d_act2, normed2, rstd2, gain2)
    g_out_bias = jnp.sum(d_middle, 0)
    d_middle_b = d_middle.astype(jnp.bfloat16)
    g_out = contract_first(context, d_middle_b)
    d_context = contract_last(d_middle_b, w_out).astype(jnp.bfloat16)

    def backward_clip(inputs):
        query_clip, keys_clip, values_clip, context_clip, dcontext_clip, lse, length = inputs
        raw = masked_scores(query_clip, keys_clip, length, positions, scale)
        probs_f = jnp.exp(raw - lse)
        probs = probs_f.astype(jnp.bfloat16)
        d_probs = jnp.einsum(
            "qhe,khe->hqk", dcontext_clip, values_clip, preferred_element_type=jnp.float32
        )
        delta = jnp.sum(dcontext_clip.astype(jnp.float32) * context_clip.astype(jnp.float32), -1).T[
            :, :, None
        ]
        d_scores = (probs_f * (d_probs - delta) * scale).astype(jnp.bfloat16)
        d_query_clip = jnp.einsum(
            "hqk,khe->qhe", d_scores, keys_clip, preferred_element_type=jnp.float32
        )
        d_keys_clip = jnp.einsum(
            "hqk,qhe->khe", d_scores, query_clip, preferred_element_type=jnp.float32
        )
        d_values_clip = jnp.einsum(
            "hqk,qhe->khe", probs, dcontext_clip, preferred_element_type=jnp.float32
        )
        return (d_query_clip, d_keys_clip, d_values_clip)

    d_query, d_keys, d_values = lax.map(
        backward_clip,
        (
            per_clip(query),
            per_clip(keys),
            per_clip(values),
            context_all,
            per_clip(d_context),
            lse_all,
            lengths,
        ),
    )
    d_query = d_query.reshape(rows, local)
    d_keys = d_keys.reshape(rows, local)
    d_values = d_values.reshape(rows, local)
    g_bias_q = jnp.sum(d_query, 0)
    g_bias_v = jnp.sum(d_values, 0)
    stacked = jnp.concatenate(
        [d_query.astype(jnp.bfloat16), d_keys.astype(jnp.bfloat16), d_values.astype(jnp.bfloat16)],
        1,
    )
    g_qkv = contract_first(act1, stacked).reshape(width, 3, local)
    d_act1 = lax.psum(contract_last(stacked, joined).astype(jnp.bfloat16), "tensor").astype(
        jnp.float32
    )
    g_gain1 = jnp.sum(d_act1 * normed1, 0)
    g_shift1 = jnp.sum(d_act1, 0)
    d_tokens = jnp.where(valid, d_middle + layer_norm_back(d_act1, normed1, rstd1, gain1), 0.0)
    (
        g_qkv,
        g_bias_q,
        g_bias_v,
        g_out,
        g_out_bias,
        g_up,
        g_up_bias,
        g_down,
        g_down_bias,
        g_gain1,
        g_shift1,
        g_gain2,
        g_shift2,
    ) = (
        lax.psum(g_qkv.astype(jnp.bfloat16), "dp").astype(jnp.float32),
        lax.psum(g_bias_q.astype(jnp.bfloat16), "dp").astype(jnp.float32),
        lax.psum(g_bias_v.astype(jnp.bfloat16), "dp").astype(jnp.float32),
        lax.psum(g_out.astype(jnp.bfloat16), "dp").astype(jnp.float32),
        lax.psum(g_out_bias.astype(jnp.bfloat16), "dp").astype(jnp.float32),
        lax.psum(g_up.astype(jnp.bfloat16), "dp").astype(jnp.float32),
        lax.psum(g_up_bias.astype(jnp.bfloat16), "dp").astype(jnp.float32),
        lax.psum(g_down.astype(jnp.bfloat16), "dp").astype(jnp.float32),
        lax.psum(g_down_bias.astype(jnp.bfloat16), "dp").astype(jnp.float32),
        lax.psum(g_gain1.astype(jnp.bfloat16), "dp").astype(jnp.float32),
        lax.psum(g_shift1.astype(jnp.bfloat16), "dp").astype(jnp.float32),
        lax.psum(g_gain2.astype(jnp.bfloat16), "dp").astype(jnp.float32),
        lax.psum(g_shift2.astype(jnp.bfloat16), "dp").astype(jnp.float32),
    )
    return (
        mixed,
        d_tokens,
        g_qkv,
        g_bias_q,
        g_bias_v,
        g_out,
        g_out_bias,
        g_up,
        g_up_bias,
        g_down,
        g_down_bias,
        g_gain1,
        g_shift1,
        g_gain2,
        g_shift2,
    )


MESH = pl.DeviceIdType.MESH
DMA = pltpu.SemaphoreType.DMA
ANY = pl.BlockSpec(memory_space=pl.ANY)
VMEM = pl.BlockSpec(memory_space=pltpu.VMEM)
SMEM = pl.BlockSpec(memory_space=pltpu.SMEM)
BLOCKS = (96,)
BQ = 256
BK = 256


def cost(us):
    return pl.CostEstimate(flops=int(us * 1e9), bytes_accessed=int(us * 3e6), transcendentals=0)


def coords():
    dp = lax.axis_index("dp")
    t = lax.axis_index("tensor")
    return dp // 2, dp % 2, t // 2, t % 2


def device(z, y, x, c):
    return (z * 2 + y, x * 2 + c)


def greet(peers):
    barrier = pltpu.get_barrier_semaphore()
    for peer in peers:
        pl.semaphore_signal(barrier, inc=1, device_id=peer, device_id_type=MESH)
    pl.semaphore_wait(barrier, len(peers))


def greet_grid():
    z, y, x, c = coords()
    barrier = pltpu.get_barrier_semaphore()

    def signal(peer):
        pl.semaphore_signal(barrier, inc=1, device_id=peer, device_id_type=MESH)

    @pl.when(z > 0)
    def _():
        signal(device(z - 1, y, x, c))

    @pl.when(z < 3)
    def _():
        signal(device(z + 1, y, x, c))

    signal(device(z, 1 - y, x, c))
    signal(device(z, y, 1 - x, c))
    signal(device(z, y, x, 1 - c))

    pl.semaphore_wait(barrier, 3 + jnp.minimum(z, 1) + jnp.minimum(3 - z, 1))


GATHER_SEMS = [DMA, DMA((4,)), DMA((4,)), DMA((4,)), DMA((8,)), DMA((16,)), DMA((32,))]


def gather_steps(x_refs, o_refs, sems, work=None, ahead=None):
    z, y, x, c = coords()
    n = len(GATHER_SEMS)
    arrays = [(a, o) + tuple(sems[n * i : n * i + n]) for i, (a, o) in enumerate(zip(x_refs, o_refs))]

    def block(z, y, x, c):
        return (z * 2 + y) * 4 + x * 2 + c

    ux, uy = x + (1 - c) * (1 - 2 * x), y + c * (1 - 2 * y)
    vx, vy = x + c * (1 - 2 * x), y + (1 - c) * (1 - 2 * y)
    own = block(z, y, x, c)
    core = device(z, y, x, 1 - c)

    def rows(array, b):
        size = array[0].shape[0]
        return array[1].at[pl.ds(pl.multiple_of(b * size, size), size)]

    def copy(array, b, kind, i, peer):
        return pltpu.make_async_remote_copy(
            src_ref=rows(array, b),
            dst_ref=rows(array, b),
            send_sem=array[kind].at[i],
            recv_sem=array[8].at[b],
            device_id=peer,
            device_id_type=MESH,
        )

    def send(b, kind, i, peer, first=False):
        for array in arrays:
            if first:
                pltpu.make_async_remote_copy(
                    src_ref=array[0],
                    dst_ref=rows(array, b),
                    send_sem=array[kind].at[i],
                    recv_sem=array[8].at[b],
                    device_id=peer,
                    device_id_type=MESH,
                ).start()
            else:
                copy(array, b, kind, i, peer).start()

    def arrived(b):
        for array in arrays:
            copy(array, b, 7, 0, core).wait_recv()

    right, left = device(z + 1, y, x, c), device(z - 1, y, x, c)
    u, v = device(z, uy, ux, c), device(z, vy, vx, c)
    locals_ = [pltpu.make_async_copy(a[0], rows(a, own), a[2]) for a in arrays]

    @pl.when(z < 3)
    def _():
        send(own, 3, z, right, True)

    @pl.when(z > 0)
    def _():
        send(own, 4, z, left, True)

    send(own, 5, z, u, True)
    send(own, 6, z, v, True)
    send(own, 7, z, core, True)
    for local in locals_:
        local.start()

    def near(step):
        def from_low(low):
            return jnp.where((low == 1) & (step < 2), 1 - step, step)

        return jnp.where(z < 2, from_low(z), 3 - from_low(3 - z))

    def got_line(at):
        b = block(at, y, x, c)
        arrived(b)

        @pl.when((at < z) & (z < 3))
        def _():
            send(b, 3, at, right)

        @pl.when((at > z) & (z > 0))
        def _():
            send(b, 4, at, left)

        send(b, 5, at, u)
        send(b, 6, at, v)
        send(b, 7, at, core)

    def got_u(at):
        b = block(at, uy, ux, c)
        arrived(b)
        send(b, 6, 4 + at, v)
        send(b, 7, 4 + at, core)

    def got_v(at):
        b = block(at, vy, vx, c)
        arrived(b)
        send(b, 7, 8 + at, core)

    def got_uv(at):
        b = block(at, 1 - y, 1 - x, c)
        arrived(b)
        send(b, 7, 12 + at, core)

    def meanwhile(step):
        if ahead is not None:
            ahead(step)

    def around(event, distance):
        for side in (-1, 1) if distance else (0,):
            at = z + side * distance
            pl.when((at >= 0) & (at < 4))(functools.partial(event, at))

    for distance in range(1, 4):
        around(got_line, distance)
        meanwhile(2 * distance - 2)
        around(got_u, distance - 1)
        meanwhile(2 * distance - 1)
    around(got_u, 3)
    meanwhile(6)
    for local in locals_:
        local.wait()

    @pl.loop(0, 4)
    def _(step):
        at = near(step)
        got_v(at)
        meanwhile(7 + 3 * step)
        got_uv(at)
        meanwhile(8 + 3 * step)

        @pl.loop(0, 4)
        def _(i):
            arrived(at * 8 + i * 2 + 1 - c)

        meanwhile(9 + 3 * step)

        if work is not None:
            work(at)

    def sent(kind, i):
        for array in arrays:
            copy(array, own, kind, i, core).wait_send()

    @pl.loop(0, 16)
    def _(i):
        sent(7, i)

    @pl.loop(0, 8)
    def _(i):
        sent(6, i)

    @pl.loop(0, 4)
    def _(i):
        sent(5, i)

        @pl.when((i <= z) & (z < 3))
        def _():
            sent(3, i)

        @pl.when((i >= z) & (z > 0))
        def _():
            sent(4, i)


def table_kernel(x_ref, o_ref, send_sem, recv_sem):
    me = lax.axis_index("dp")
    t = lax.axis_index("tensor")
    peers = [(lax.rem(me + s, 8), t) for s in range(1, 8)]
    greet(peers)
    o_ref[me] = x_ref[...]
    copies = [
        pltpu.make_async_remote_copy(
            src_ref=x_ref,
            dst_ref=o_ref.at[me],
            send_sem=send_sem.at[s],
            recv_sem=recv_sem.at[s],
            device_id=peer,
            device_id_type=MESH,
        )
        for s, peer in enumerate(peers)
    ]
    for copy in copies:
        copy.start()
    for copy in copies:
        copy.wait()


def gather_table(value, cid):
    tile = jnp.broadcast_to(value.reshape(1, 1), (8, 128))
    out = pl.pallas_call(
        table_kernel,
        out_shape=jax.ShapeDtypeStruct((8, 8, 128), value.dtype),
        in_specs=[VMEM],
        out_specs=VMEM,
        scratch_shapes=[DMA((7,)), DMA((7,))],
        compiler_params=pltpu.CompilerParams(collective_id=cid, has_side_effects=True),
        name="table",
    )(tile)
    return out[:, 0, 0]


def pieces_kernel(size, info_ref, x_ref, u_ref, xo_ref, uo_ref, held, sems):
    t = lax.axis_index("tensor")
    cap = x_ref.shape[0]
    offset = info_ref[0]
    length = info_ref[1]
    loads = [
        pltpu.make_async_copy(src, held.at[i, pl.ds(size, cap)], sems.at[i])
        for i, src in enumerate((x_ref, u_ref))
    ]
    for load in loads:
        load.start()
    for i in (0, 1):
        held[i, 0:size, :] = jnp.zeros((size, held.shape[2]), held.dtype)
        held[i, size + cap :, :] = jnp.zeros((size, held.shape[2]), held.dtype)
    for i, out in enumerate((xo_ref, uo_ref)):
        loads[i].wait()

        @pl.loop(0, 8)
        def _(b):
            first = (b * 4 + t) * size - offset + size
            first = pl.multiple_of(jnp.clip(first, 0, cap + size), 16)
            row = lax.broadcasted_iota(jnp.int32, (size, 1), 0) + first - size
            value = held[i, pl.ds(first, size), :].astype(jnp.float32)
            value = jnp.where((row >= 0) & (row < length), value, 0.0)
            out[b] = value.astype(jnp.bfloat16)


def take_pieces(x, u, info, size):
    cap, width = x.shape
    shape = jax.ShapeDtypeStruct((8, size, width), jnp.bfloat16)
    return pl.pallas_call(
        functools.partial(pieces_kernel, size),
        out_shape=(shape, shape),
        in_specs=[SMEM, ANY, ANY],
        out_specs=(VMEM, VMEM),
        scratch_shapes=[pltpu.VMEM((2, cap + 2 * size, width), jnp.bfloat16), DMA((2,))],
        compiler_params=pltpu.CompilerParams(vmem_limit_bytes=40 << 20),
        name="pieces",
    )(info, x, u)


def pack_kernel(
    p_ref,
    w_ref,
    wt_ref,
    bias_ref,
    bias_t_ref,
    gain_ref,
    shift_ref,
    own,
    act_ref,
    kv_ref,
    qkvt_ref,
    x_all,
    acc,
    y_out,
    y_in,
    r_out,
    r_in,
    l_out,
    l_in,
    ys,
    yr,
    rs,
    rr,
    ls,
    lr,
    *gather_sems,
):
    z, y, x, c = coords()
    size = own.shape[0]
    local = kv_ref.shape[1] // 2
    greet_grid()

    def piece(zp, yp):
        return p_ref[zp * 2 + yp].astype(jnp.float32)

    def project(at):
        @pl.loop(0, 8)
        def _(i):
            r = pl.ds(pl.multiple_of(at * 8 * size + i * size, size), size)
            _, _, pre = layer_norm(x_all[r, :].astype(jnp.float32), gain_ref[...], shift_ref[...])
            act_ref[r, :] = pre.astype(jnp.bfloat16)

        @pl.loop(0, 2)
        def _(i):
            r = pl.ds(pl.multiple_of(at * 8 * size + i * 4 * size, 4 * size), 4 * size)
            act = act_ref[r, :]
            kv_ref[r, :] = (dot_nn(act, w_ref[:, local:]) + bias_ref[:, local:]).astype(jnp.bfloat16)
            for j in range(3):
                cols = slice(j * local, (j + 1) * local)
                out = (dot_nt(wt_ref[cols, :], act) + bias_t_ref[cols, :]).astype(jnp.bfloat16)
                qkvt_ref[cols, r] = out * jnp.bfloat16(HD**-0.5) if j == 0 else out

    def y_copy(i):
        return pltpu.make_async_remote_copy(
            src_ref=y_out.at[i],
            dst_ref=y_in.at[i],
            send_sem=ys.at[i],
            recv_sem=yr.at[i],
            device_id=device(z, 1 - y, x, c),
            device_id_type=MESH,
        )

    def r_copy(i):
        return pltpu.make_async_remote_copy(
            src_ref=r_out.at[i],
            dst_ref=r_in.at[i],
            send_sem=rs.at[i],
            recv_sem=rr.at[i],
            device_id=device(z + 1, y, x, c),
            device_id_type=MESH,
        )

    def l_copy(i):
        return pltpu.make_async_remote_copy(
            src_ref=l_out.at[i],
            dst_ref=l_in.at[i],
            send_sem=ls.at[i],
            recv_sem=lr.at[i],
            device_id=device(z - 1, y, x, c),
            device_id_type=MESH,
        )

    def add(ref, copy, i):
        copy(i).wait_recv()
        acc[...] += ref[i].astype(jnp.float32)

    def flow(zp, yp, first):
        i = zp * 2 + yp

        @pl.when(z < zp)
        def _():
            first()

            @pl.when(z > 0)
            def _():
                add(r_in, r_copy, i)

            r_out[i] = acc[...].astype(jnp.bfloat16)
            r_copy(i).start()

        @pl.when(z > zp)
        def _():
            first()

            @pl.when(z < 3)
            def _():
                add(l_in, l_copy, i)

            l_out[i] = acc[...].astype(jnp.bfloat16)
            l_copy(i).start()

    def land(yp):
        @pl.when(z > 0)
        def _():
            add(r_in, r_copy, z * 2 + yp)

        @pl.when(z < 3)
        def _():
            add(l_in, l_copy, z * 2 + yp)

    order = (0, 3, 1, 2)

    @pl.when(c == 0)
    def _():
        for zp in order:
            y_out[zp] = piece(zp, 1 - y).astype(jnp.bfloat16)
            y_copy(zp).start()
        for zp in order:

            def first(zp=zp):
                acc[...] = piece(zp, y)
                add(y_in, y_copy, zp)

            flow(zp, y, first)
        acc[...] = piece(z, y)
        add(y_in, y_copy, z)
        land(y)
        own[...] = acc[...].astype(jnp.bfloat16)
        for zp in order:
            y_copy(zp).wait_send()

    @pl.when(c == 1)
    def _():
        for zp in order:
            for yp in (0, 1):

                def first(zp=zp, yp=yp):
                    acc[...] = piece(zp, yp)

                flow(zp, yp, first)
        acc[...] = piece(z, 1 - y)
        land(1 - y)
        y_out[0] = acc[...].astype(jnp.bfloat16)
        y_copy(0).start()
        acc[...] = piece(z, y)
        land(y)
        add(y_in, y_copy, 0)
        own[...] = acc[...].astype(jnp.bfloat16)
        y_copy(0).wait_send()

    for zp in range(4):
        for yp in (0, 1):
            used = (c == 1) | (y == yp)

            @pl.when(used & (z < zp))
            def _(i=zp * 2 + yp):
                r_copy(i).wait_send()

            @pl.when(used & (z > zp))
            def _(i=zp * 2 + yp):
                l_copy(i).wait_send()

    gather_steps([own], [x_all], gather_sems, project)


def pack_gather(parts, joined, bias, gain, shift, cid):
    _, size, width = parts.shape
    bf16 = jnp.bfloat16
    rows = 32 * size
    total = joined.shape[1]
    slots = pltpu.VMEM((8, size, width), bf16)
    quarter = pltpu.VMEM((4, size, width), bf16)
    return pl.pallas_call(
        pack_kernel,
        out_shape=(
            jax.ShapeDtypeStruct((size, width), bf16),
            jax.ShapeDtypeStruct((rows, width), bf16),
            jax.ShapeDtypeStruct((rows, total // 3 * 2), bf16),
            jax.ShapeDtypeStruct((total, rows), bf16),
        ),
        in_specs=[VMEM] * 7,
        out_specs=[VMEM] * 4,
        scratch_shapes=[
            pltpu.VMEM((rows, width), bf16),
            pltpu.VMEM((size, width), jnp.float32),
            quarter,
            quarter,
            slots,
            slots,
            slots,
            slots,
            DMA((4,)),
            DMA((4,)),
            DMA((8,)),
            DMA((8,)),
            DMA((8,)),
            DMA((8,)),
        ]
        + GATHER_SEMS,
        compiler_params=pltpu.CompilerParams(
            collective_id=cid, has_side_effects=True, vmem_limit_bytes=58 << 20
        ),
        cost_estimate=cost(90),
        name="pack_gather",
    )(parts, joined, joined.T, bias[None], bias[:, None], gain[None], shift[None])


def greet_all():
    z, y, x, c = coords()
    barrier = pltpu.get_barrier_semaphore()

    def signal(peer):
        pl.semaphore_signal(barrier, inc=1, device_id=peer, device_id_type=MESH)

    @pl.when(z > 0)
    def _():
        signal(device(z - 1, y, x, c))

    @pl.when(z < 3)
    def _():
        signal(device(z + 1, y, x, c))

    signal(device(z, 1 - y, x, c))
    for peer in (device(z, y, 1 - x, c), device(z, y, x, 1 - c), device(z, y, 1 - x, 1 - c)):
        signal(peer)
    pl.semaphore_wait(barrier, 4 + jnp.minimum(z, 1) + jnp.minimum(3 - z, 1))


def share_start(p_ref, landed, send_sem, recv_sem):
    dp = lax.axis_index("dp")
    t = lax.axis_index("tensor")
    copies = [
        pltpu.make_async_remote_copy(
            src_ref=p_ref.at[peer],
            dst_ref=landed.at[s],
            send_sem=send_sem.at[s],
            recv_sem=recv_sem.at[s],
            device_id=(dp, peer),
            device_id_type=MESH,
        )
        for s, peer in enumerate([lax.rem(t + s, 4) for s in (2, 3, 1)])
    ]
    for copy in copies:
        copy.start()
    return copies


def share_sum(p_ref, landed, copies):
    total = p_ref[lax.axis_index("tensor")].astype(jnp.float32)
    for s, copy in enumerate(copies):
        copy.wait_recv()
        total += landed[s].astype(jnp.float32)
    for copy in copies:
        copy.wait_send()
    return total


def share_scratch(size, width):
    return [pltpu.VMEM((3, size, width), jnp.bfloat16), DMA((3,)), DMA((3,))]


def load_all(sources, targets, sems):
    copies = [
        pltpu.make_async_copy(a, b, sems.at[i]) for i, (a, b) in enumerate(zip(sources, targets))
    ]
    for copy in copies:
        copy.start()
    return copies


def products(units):
    total = sum(count for _, count in units)
    each = (total + 9) // 10

    def ahead(step):
        @pl.when(step < 10)
        def _():
            @pl.loop(0, each)
            def _(i):
                job = step * each + i
                before = 0
                for unit, count in units:
                    pl.when((job >= before) & (job < before + count))(
                        functools.partial(unit, job - before)
                    )
                    before += count

    return ahead


def outer_unit(a, b, out, tall, wide):
    across = b.shape[1] // wide

    def unit(job):
        n = pl.ds(pl.multiple_of(lax.rem(job, across) * wide, 128), wide)
        if tall == a.shape[1]:
            out[:, n] = dot_tn(a[...], b[:, n])
        else:
            m = pl.ds(pl.multiple_of(job // across * tall, 128), tall)
            out[m, n] = dot_tn(a[:, m], b[:, n])

    return unit, a.shape[1] // tall * across


def first_kernel(p_ref, x_ref, bias_ref, gain_ref, shift_ref, mid_ref, o_ref, own, landed, ss, sr, *sems):
    greet_all()
    copies = share_start(p_ref, landed, ss, sr)
    middle = x_ref[...].astype(jnp.float32) + share_sum(p_ref, landed, copies) + bias_ref[...]
    mid_ref[...] = middle
    _, _, pre = layer_norm(middle, gain_ref[...], shift_ref[...])
    own[...] = pre.astype(jnp.bfloat16)
    gather_steps([own], [o_ref], sems)


def first_exchange(part, source, bias_out, gain2, shift2, cid):
    size, width = source.shape
    return pl.pallas_call(
        first_kernel,
        out_shape=(
            jax.ShapeDtypeStruct((size, width), jnp.float32),
            jax.ShapeDtypeStruct((32 * size, width), jnp.bfloat16),
        ),
        in_specs=[VMEM] * 5,
        out_specs=[VMEM, ANY],
        scratch_shapes=[pltpu.VMEM((size, width), jnp.bfloat16)]
        + share_scratch(size, width)
        + GATHER_SEMS,
        compiler_params=pltpu.CompilerParams(
            collective_id=cid, has_side_effects=True, vmem_limit_bytes=24 << 20
        ),
        cost_estimate=cost(60),
        name="first_exchange",
    )(part.reshape(4, size, width), source, bias_out[None], gain2[None], shift2[None])


def second_kernel(
    p_ref, b_ref, mid_ref, up_ref, gain_ref, bias_ref, wout_ref, act_ref, hid_ref, dpre_ref, upall_ref,
    dmid_ref, mixed_ref, vec_ref, o_ref, gup_ref, gdown_ref, dctx_ref, gbias_ref,
    own, landed, ss, sr, landed2, ss2, sr2, some, act, hid, dpre, upall, load_sem, *sems,
):
    loads = load_all((act_ref, dpre_ref, hid_ref, upall_ref), (act, dpre, hid, upall), load_sem)
    greet_all()
    copies = share_start(p_ref, landed, ss, sr)
    branch_copies = share_start(b_ref, landed2, ss2, sr2)
    grad = share_sum(p_ref, landed, copies)
    middle = mid_ref[...]
    normed, rstd, _ = layer_norm(middle, 1.0, 0.0)
    d_middle = up_ref[...].astype(jnp.float32) + layer_norm_back(grad, normed, rstd, gain_ref[...])
    own[...] = d_middle.astype(jnp.bfloat16)
    dmid_ref[...] = d_middle
    vec_ref[...] = jnp.concatenate(
        [
            jnp.sum(grad * normed, 0, keepdims=True),
            jnp.sum(grad, 0, keepdims=True),
            jnp.zeros((6, grad.shape[1]), jnp.float32),
        ],
        0,
    )
    work = products([outer_unit(act, dpre, gup_ref, 256, 1280), outer_unit(hid, upall, gdown_ref, 256, 1280)])

    def ahead(step):
        @pl.when(step == 0)
        def _():
            branch = share_sum(b_ref, landed2, branch_copies)
            mixed_ref[...] = (mid_ref[...] + branch + bias_ref[...]).astype(jnp.bfloat16)
            for load in loads:
                load.wait()

        work(step)

    size = own.shape[0]
    gbias_ref[...] = jnp.zeros_like(gbias_ref)

    def context_grad(at):
        @pl.loop(0, 2)
        def _(i):
            r = pl.ds(pl.multiple_of(at * 8 * size + i * 4 * size, 4 * size), 4 * size)
            pltpu.sync_copy(o_ref.at[r], some)
            dctx_ref[:, r] = dot_nt(wout_ref[...], some[...]).astype(jnp.bfloat16)
            gbias_ref[0:1, :] += jnp.sum(some[...].astype(jnp.float32), 0, keepdims=True)

    gather_steps([own], [o_ref], sems, context_grad, ahead)


def second_exchange(part, branch, middle, upstream, gain2, bias_down, w_out, act2, hidden, d_pre, up_all, cid):
    size, width = middle.shape
    f32, bf16 = jnp.float32, jnp.bfloat16
    rows, inner = hidden.shape
    return pl.pallas_call(
        second_kernel,
        out_shape=(
            jax.ShapeDtypeStruct((size, width), f32),
            jax.ShapeDtypeStruct((size, width), bf16),
            jax.ShapeDtypeStruct((8, width), f32),
            jax.ShapeDtypeStruct((rows, width), bf16),
            jax.ShapeDtypeStruct((width, inner), f32),
            jax.ShapeDtypeStruct((inner, width), f32),
            jax.ShapeDtypeStruct((w_out.shape[0], rows), bf16),
            jax.ShapeDtypeStruct((8, width), f32),
        ),
        in_specs=[VMEM] * 7 + [ANY] * 4,
        out_specs=[VMEM, VMEM, VMEM, ANY, VMEM, VMEM, VMEM, VMEM],
        scratch_shapes=[pltpu.VMEM((size, width), bf16)]
        + share_scratch(size, width) * 2
        + [pltpu.VMEM((4 * size, width), bf16)]
        + [pltpu.VMEM((rows, n), bf16) for n in (width, inner, inner, width)]
        + [DMA((4,))]
        + GATHER_SEMS,
        compiler_params=pltpu.CompilerParams(
            collective_id=cid, has_side_effects=True, vmem_limit_bytes=60 << 20
        ),
        cost_estimate=cost(80),
        name="second_exchange",
    )(
        part.reshape(4, size, width), branch.reshape(4, size, width), middle, upstream,
        gain2[None], bias_down[None], w_out, act2, hidden, d_pre, up_all,
    )


def third_kernel(
    p_ref, x_ref, dmid_ref, gain_ref, vec_ref, act_ref, dt_ref, ctx_ref, dmall_ref,
    o_ref, vo_ref, gqkv_ref, gout_ref,
    own, vec, landed, ss, sr, act, dt, ctx, dmall, load_sem, *sems,
):
    loads = load_all((act_ref, dt_ref, ctx_ref, dmall_ref), (act, dt, ctx, dmall), load_sem)
    greet_all()
    copies = share_start(p_ref, landed, ss, sr)
    grad = share_sum(p_ref, landed, copies)
    normed, rstd, _ = layer_norm(x_ref[...].astype(jnp.float32), 1.0, 0.0)
    own[...] = (dmid_ref[...] + layer_norm_back(grad, normed, rstd, gain_ref[...])).astype(jnp.bfloat16)
    vec[...] = jnp.concatenate(
        [
            vec_ref[0:2, :],
            jnp.sum(grad * normed, 0, keepdims=True),
            jnp.sum(grad, 0, keepdims=True),
            jnp.zeros((4, grad.shape[1]), jnp.float32),
        ],
        0,
    )
    part = dt.shape[0] // 3

    def project(job):
        m = pl.ds(pl.multiple_of(job // 3 * 256, 256), 256)
        k = lax.rem(job, 3)
        gqkv_ref[k, m, :] = dot_nn(dt[pl.ds(pl.multiple_of(k * part, 64), part), :], act[:, m]).T

    work = products([(project, act.shape[1] // 256 * 3), outer_unit(ctx, dmall, gout_ref, part, 640)])

    def ahead(step):
        @pl.when(step == 0)
        def _():
            for load in loads:
                load.wait()

        work(step)

    gather_steps([own, vec], [o_ref, vo_ref], sems, ahead=ahead)


def third_exchange(part, source, d_middle, gain1, vec, act1, d_qkv, context, d_middle_all, cid):
    size, width = d_middle.shape
    f32, bf16 = jnp.float32, jnp.bfloat16
    rows = act1.shape[0]
    total = d_qkv.shape[0]
    return pl.pallas_call(
        third_kernel,
        out_shape=(
            jax.ShapeDtypeStruct((rows, width), bf16),
            jax.ShapeDtypeStruct((256, width), f32),
            jax.ShapeDtypeStruct((3, width, total // 3), f32),
            jax.ShapeDtypeStruct((total // 3, width), f32),
        ),
        in_specs=[VMEM] * 5 + [ANY] * 4,
        out_specs=[ANY, ANY, VMEM, VMEM],
        scratch_shapes=[pltpu.VMEM((size, width), bf16), pltpu.VMEM((8, width), f32)]
        + share_scratch(size, width)
        + [pltpu.VMEM(a.shape, bf16) for a in (act1, d_qkv, context, d_middle_all)]
        + [DMA((4,))]
        + GATHER_SEMS * 2,
        compiler_params=pltpu.CompilerParams(
            collective_id=cid, has_side_effects=True, vmem_limit_bytes=60 << 20
        ),
        cost_estimate=cost(60),
        name="third_exchange",
    )(
        part.reshape(4, size, width), source, d_middle, gain1[None], vec,
        act1, d_qkv, context, d_middle_all,
    )


def dot_nt(a, b):
    return lax.dot_general(a, b, (((1,), (1,)), ((), ())), preferred_element_type=jnp.float32)


def dot_nn(a, b):
    return lax.dot_general(a, b, (((1,), (0,)), ((), ())), preferred_element_type=jnp.float32)


def dot_tn(a, b):
    return lax.dot_general(a, b, (((0,), (0,)), ((), ())), preferred_element_type=jnp.float32)


def spans(offset_ref, length_ref, first, count):
    row = lax.broadcasted_iota(jnp.int32, (1, count), 1) + first
    start = jnp.zeros((1, count), jnp.int32)
    end = jnp.zeros((1, count), jnp.int32)
    low, high = 1 << 20, 0
    for i in range(offset_ref.shape[0]):
        a = offset_ref[i]
        b = a + length_ref[i]
        inside = (row >= a) & (row < b)
        start = jnp.where(inside, a, start)
        end = jnp.where(inside, b, end)
        used = (a < first + count) & (b > first) & (b > a)
        low = jnp.where(used, jnp.minimum(low, a // BK), low)
        high = jnp.where(used, jnp.maximum(high, (b + BK - 1) // BK), high)
    return start, end, low, high


def attend_kernel(heads, offset_ref, length_ref, qkvt_ref, kv_ref, ctx_ref, lse_ref, m_s, l_s, acc_s):
    rows = ctx_ref.shape[0]
    local = heads * HD
    span = range(heads)
    first = lax.axis_index("dp") * rows
    mine = pl.ds(pl.multiple_of(first, 128), rows)
    start, end, low, high = spans(offset_ref, length_ref, first, rows)
    m_s[...] = jnp.full_like(m_s, NEG)
    l_s[...] = jnp.zeros_like(l_s)
    acc_s[...] = jnp.zeros_like(acc_s)
    q = [qkvt_ref[h * HD : (h + 1) * HD, mine] for h in span]

    def body(kb, carry):
        k0 = pl.multiple_of(kb * BK, BK)
        key = lax.broadcasted_iota(jnp.int32, (BK, rows), 0) + k0
        mask = (key >= start) & (key < end)
        s = [
            jnp.where(
                mask,
                dot_nn(kv_ref[pl.ds(k0, BK), h * HD : (h + 1) * HD], q[h]),
                NEG,
            )
            for h in span
        ]
        p, a = [], []
        for h in span:
            old = m_s[h]
            new = jnp.maximum(old, jnp.max(s[h], 0, keepdims=True))
            e = jnp.exp(s[h] - new)
            scale = jnp.exp(old - new)
            l_s[h] = scale * l_s[h] + jnp.sum(e, 0, keepdims=True)
            m_s[h] = new
            p.append(e.astype(jnp.bfloat16))
            a.append(scale)
        for h in span:
            vt = qkvt_ref[2 * local + h * HD : 2 * local + (h + 1) * HD, pl.ds(k0, BK)]
            acc_s[h] = a[h] * acc_s[h] + dot_nn(vt, p[h])
        return carry

    lax.fori_loop(low, high, body, 0)
    parts = [[], [], []]
    for h in span:
        total = l_s[h]
        total = jnp.where(total == 0.0, 1.0, total)
        rest = m_s[h] + jnp.log(total)
        for part in parts:
            part.append(rest.astype(jnp.bfloat16).astype(jnp.float32))
            rest = rest - part[-1]
        out = acc_s[h] * (1.0 / total)
        ctx_ref[:, h * HD : (h + 1) * HD] = out.T.astype(jnp.bfloat16)
    blank = [jnp.zeros((128 - 3 * heads, rows), jnp.float32)]
    lse_ref[...] = jnp.concatenate(parts[0] + parts[1] + parts[2] + blank, 0).T.astype(jnp.bfloat16)


def whole(a):
    return pl.BlockSpec(a.shape, lambda i, *_: (0,) * len(a.shape), pipeline_mode=pl.Buffered(1))


def attend(qkvt, kv, offsets, lengths, heads):
    rows = kv.shape[0] // 8
    local = heads * HD
    row = pltpu.VMEM((heads, 1, rows), jnp.float32)
    return pl.pallas_call(
        functools.partial(attend_kernel, heads),
        out_shape=(
            jax.ShapeDtypeStruct((rows, local), jnp.bfloat16),
            jax.ShapeDtypeStruct((rows, 128), jnp.bfloat16),
        ),
        in_specs=[SMEM, SMEM] + [VMEM] * 2,
        out_specs=[VMEM, VMEM],
        scratch_shapes=[row, row, pltpu.VMEM((heads, HD, rows), jnp.float32)],
        compiler_params=pltpu.CompilerParams(vmem_limit_bytes=40 << 20),
        cost_estimate=cost(10),
        name="attend",
    )(offsets, lengths, qkvt, kv)


def attend_back_kernel(
    heads, offset_ref, length_ref, kv_ref, qkt_ref, dot_ref, ctxt_ref, lse_ref, d_ref, dk_s, dv_s, dq_s
):
    i = pl.program_id(0)
    local = heads * HD
    span = range(heads)
    sl = [slice(h * HD, (h + 1) * HD) for h in span]
    at_q = pl.ds(pl.multiple_of(i * BQ, BQ), BQ)

    @pl.when(i == 0)
    def _():
        dk_s[...] = jnp.zeros_like(dk_s)
        dv_s[...] = jnp.zeros_like(dv_s)

    start, end, low, high = spans(offset_ref, length_ref, i * BQ, BQ)
    dq_s[...] = jnp.zeros_like(dq_s)
    delta = []
    for h in span:
        both = dot_ref[sl[h], at_q].astype(jnp.float32) * ctxt_ref[sl[h], at_q].astype(jnp.float32)
        delta.append(jnp.sum(both, 0, keepdims=True))

    def body(kb, carry):
        at_k = pl.ds(pl.multiple_of(kb * BK, BK), BK)
        key = lax.broadcasted_iota(jnp.int32, (BK, BQ), 0) + kb * BK
        mask = (key >= start) & (key < end)

        def products(h):
            s = dot_nn(kv_ref[at_k, sl[h]], qkt_ref[sl[h], at_q])
            dp = dot_nn(kv_ref[at_k, local + h * HD : local + (h + 1) * HD], dot_ref[sl[h], at_q])
            return s, dp

        def scores(h, s, dp):
            p = jnp.exp(jnp.where(mask, s, NEG) - lse_ref[h : h + 1, at_q])
            ds = (p * (dp - delta[h])).astype(jnp.bfloat16)
            return p.astype(jnp.bfloat16), ds

        def gradients(h, p, ds):
            dv_s[h, :, at_k] += dot_nt(dot_ref[sl[h], at_q], p)
            dk_s[h, :, at_k] += dot_nt(qkt_ref[sl[h], at_q], ds)
            dq_s[h] += dot_nn(qkt_ref[local + h * HD : local + (h + 1) * HD, at_k], ds)

        now = products(0)
        held = None
        for h in span:
            later = products(h + 1) if h + 1 < heads else None
            done = scores(h, *now)
            if held is not None:
                gradients(h - 1, *held)
            held, now = done, later
        gradients(heads - 1, *held)
        return carry

    lax.fori_loop(low, high, body, 0)
    for h in span:
        d_ref[sl[h], at_q] = (dq_s[h] * HD**-0.5).astype(jnp.bfloat16)

    @pl.when(i == pl.num_programs(0) - 1)
    def _():
        for h in span:
            d_ref[local + h * HD : local + (h + 1) * HD, :] = dk_s[h].astype(jnp.bfloat16)
            d_ref[2 * local + h * HD : 2 * local + (h + 1) * HD, :] = dv_s[h].astype(jnp.bfloat16)


def attend_back(kv, qkt, dot, ctxt, lse, offsets, lengths, heads):
    rows = kv.shape[0]
    local = heads * HD
    tall = pltpu.VMEM((heads, HD, rows), jnp.float32)
    return pl.pallas_call(
        functools.partial(attend_back_kernel, heads),
        out_shape=jax.ShapeDtypeStruct((3 * local, rows), jnp.bfloat16),
        grid_spec=pltpu.PrefetchScalarGridSpec(
            num_scalar_prefetch=2,
            grid=(rows // BQ,),
            in_specs=[whole(a) for a in (kv, qkt, dot, ctxt, lse)],
            out_specs=pl.BlockSpec(
                (3 * local, rows), lambda i, *_: (0, 0), pipeline_mode=pl.Buffered(1)
            ),
            scratch_shapes=[tall, tall, pltpu.VMEM((heads, HD, BQ), jnp.float32)],
        ),
        compiler_params=pltpu.CompilerParams(vmem_limit_bytes=48 << 20),
        cost_estimate=cost(60),
        name="attend_back",
    )(offsets, lengths, kv, qkt, dot, ctxt, lse)


def unpack_kernel(info_ref, m_ref, d_ref, mo_ref, do_ref, m, d, sems):
    cap = mo_ref.shape[0]
    rows = m_ref.shape[0]
    offset = info_ref[0]
    length = info_ref[1]
    first = pl.multiple_of(jnp.minimum(offset, rows - cap), 16)
    loads = [
        pltpu.make_async_copy(src.at[pl.ds(first, cap)], dst.at[pl.ds(0, cap)], sems.at[i])
        for i, (src, dst) in enumerate(((m_ref, m), (d_ref, d)))
    ]
    for load in loads:
        load.start()
    for load, src, dst in zip(loads, (m, d), (mo_ref, do_ref)):
        load.wait()

        @pl.loop(0, cap // 128)
        def _(i):
            at = pl.multiple_of(jnp.minimum(offset - first + i * 128, cap), 16)
            row = lax.broadcasted_iota(jnp.int32, (128, 1), 0) + i * 128
            value = jnp.where(row < length, src[pl.ds(at, 128), :].astype(jnp.float32), 0.0)
            dst[pl.ds(pl.multiple_of(i * 128, 128), 128), :] = value.astype(dst.dtype)


def unpack(info, mixed, d_tokens, cap):
    width = mixed.shape[1]
    held = pltpu.VMEM((cap + 128, width), jnp.bfloat16)
    return pl.pallas_call(
        unpack_kernel,
        out_shape=(
            jax.ShapeDtypeStruct((cap, width), jnp.bfloat16),
            jax.ShapeDtypeStruct((cap, width), jnp.float32),
        ),
        in_specs=[SMEM, ANY, ANY],
        out_specs=[VMEM, VMEM],
        scratch_shapes=[held, held, DMA((2,))],
        compiler_params=pltpu.CompilerParams(vmem_limit_bytes=40 << 20),
        name="unpack",
    )(info, mixed, d_tokens)


def packed_step(size, cids, offset, length, offsets, lengths, args):
    (
        tokens, _, _, w_qkv, bias_q, bias_v, w_out, bias_out, w_up, bias_up, w_down, bias_down,
        gain1, shift1, gain2, shift2, grad_out,
    ) = args
    f32, bf16 = jnp.float32, jnp.bfloat16
    cap, width = tokens.shape
    local = w_qkv.shape[2]
    heads = local // HD
    rows = 32 * size
    mine = 4 * size
    dp = lax.axis_index("dp")
    pack_id, first_id, second_id, third_id = cids

    def own(value):
        return lax.dynamic_slice_in_dim(value, dp * mine, mine, 0)

    info = jnp.stack([offset, length])
    x_parts, up_parts = take_pieces(tokens, grad_out, info, size)
    joined = w_qkv.reshape(width, 3 * local)
    bias = jnp.concatenate([bias_q, jnp.zeros_like(bias_q), bias_v])
    source, act1, kv, qkvt = pack_gather(x_parts, joined, bias, gain1, shift1, pack_id)
    up_own = lax.psum_scatter(up_parts, "dp", scatter_dimension=0, tiled=True)
    up_own, source = lax.optimization_barrier((up_own, source))
    up_all = lax.all_gather(up_own.reshape(size, width), ("dp", "tensor"), tiled=True)

    context_own, lse_own = attend(
        qkvt, kv, offsets, lengths, heads
    )
    part = jnp.dot(context_own, w_out, preferred_element_type=f32).astype(bf16)
    sent = jnp.concatenate([context_own, lse_own], 1)
    sent = lax.all_gather(sent, "dp", tiled=True)
    context = sent[:, :local]
    lse = jnp.sum(sent[:, local : local + 3 * heads].astype(f32).reshape(rows, 3, heads), 1).T
    lse = jnp.concatenate([lse, jnp.zeros((8 - heads, rows), f32)], 0)
    middle, act2 = first_exchange(part, source, bias_out, gain2, shift2, first_id)

    pre = jnp.dot(act2, w_up, preferred_element_type=f32) + bias_up
    hidden_f, slope = gelu_pair(pre)
    hidden = hidden_f.astype(bf16)
    d_pre = contract_last(up_all, w_down) * slope
    g_up_bias = jnp.sum(d_pre, 0)
    d_pre_b = d_pre.astype(bf16)
    d_part = contract_last(own(d_pre_b), w_up).astype(bf16)
    branch = jnp.dot(own(hidden), w_down, preferred_element_type=f32).astype(bf16)
    d_middle, mixed, vec, d_middle_b, g_up, g_down, d_context, g_out_bias = second_exchange(
        d_part, branch, middle, up_own.reshape(size, width), gain2, bias_down,
        w_out, act2, hidden, d_pre_b, up_all, second_id,
    )
    g_down_bias = jnp.sum(up_all.astype(f32), 0)
    mixed_all = lax.all_gather(mixed, ("dp", "tensor"), tiled=True)
    d_qkv = attend_back(
        kv, qkvt, d_context, context.T, lse, offsets, lengths, heads
    )
    g_bias_q = jnp.sum(d_qkv[:local].astype(f32), 1)
    g_bias_v = jnp.sum(d_qkv[2 * local :].astype(f32), 1)
    d_own = lax.dynamic_slice_in_dim(d_qkv, dp * mine, mine, 1)
    d_act1 = jnp.einsum("kr,dk->rd", d_own, joined, preferred_element_type=f32).astype(bf16)
    d_tokens_all, vectors_all, g_qkv, g_out = third_exchange(
        d_act1, source, d_middle, gain1, vec, act1, d_qkv, context, d_middle_b, third_id
    )
    g_qkv = g_qkv.transpose(1, 0, 2)
    sums = jnp.sum(vectors_all.reshape(32, 8, width), 0)
    mixed, d_tokens = unpack(info, mixed_all, d_tokens_all, cap)

    return (
        mixed,
        d_tokens,
        g_qkv,
        g_bias_q,
        g_bias_v,
        g_out,
        g_out_bias[0],
        g_up,
        g_up_bias,
        g_down,
        g_down_bias,
        sums[2],
        sums[3],
        sums[0],
        sums[1],
    )


def packed(*args):
    clip_len, slot_clip = args[1], args[2]
    clips = clip_len.shape[0]

    def padded(value):
        return (value + 15) // 16 * 16

    need = jnp.sum(padded(clip_len))
    table = gather_table(slot_clip[0], 0)
    match = table[:, None] == jnp.arange(clips, dtype=jnp.int32)[None, :]
    lengths = jnp.sum(jnp.where(match, clip_len[None, :], 0), 1)
    slots = jnp.arange(8, dtype=jnp.int32)
    ahead = (lengths[None, :] > lengths[:, None]) | (
        (lengths[None, :] == lengths[:, None]) & (slots[None, :] < slots[:, None])
    )
    offsets = jnp.sum(jnp.where(ahead, padded(lengths)[None, :], 0), 1)
    dp = lax.axis_index("dp")
    length = lengths[dp]
    offset = offsets[dp]
    branches = [
        functools.partial(packed_step, size, [1 + 4 * n + i for i in range(4)])
        for n, size in enumerate(BLOCKS)
    ]
    pick = sum((need > 32 * size).astype(jnp.int32) for size in BLOCKS)

    def fallback(offset, length, offsets, lengths, args):
        return plain(*args)

    return lax.switch(pick, branches + [fallback], offset, length, offsets, lengths, args)


def solution(mesh):
    placed = (
        P("dp", None),
        P(),
        P("dp"),
        P(None, None, "tensor"),
        P("tensor"),
        P("tensor"),
        P("tensor", None),
        P(),
        P(None, "tensor"),
        P("tensor"),
        P("tensor", None),
        P(),
        P(),
        P(),
        P(),
        P(),
        P("dp", None),
    )
    fits = mesh.shape["dp"] == 8 and mesh.shape["tensor"] == 4
    return jax.shard_map(
        packed if fits else plain,
        mesh=mesh,
        in_specs=placed,
        out_specs=(
            P("dp", None),
            P("dp", None),
            P(None, None, "tensor"),
            P("tensor"),
            P("tensor"),
            P("tensor", None),
            P(),
            P(None, "tensor"),
            P("tensor"),
            P("tensor", None),
            P(),
            P(),
            P(),
            P(),
            P(),
        ),
        check_vma=False,
    )
```

```python
import functools

import jax
import jax.numpy as jnp
from jax import lax
from jax.experimental import pallas as pl
from jax.experimental.pallas import tpu as pltpu
from jax.sharding import PartitionSpec as P

HD = 64


EPS = 1e-05
NEG = -1e30
HALF_ROOT = 0.7071067811865476
INV_ROOT_TAU = 0.3989422804014327


def layer_norm(value, gain, shift):
    center = value - jnp.mean(value, -1, keepdims=True)
    rstd = lax.rsqrt(jnp.mean(center * center, -1, keepdims=True) + EPS)
    normed = center * rstd
    return (normed, rstd, normed * gain + shift)


def layer_norm_back(grad, normed, rstd, gain):
    scaled = grad * gain
    return rstd * (
        scaled
        - jnp.mean(scaled, -1, keepdims=True)
        - normed * jnp.mean(scaled * normed, -1, keepdims=True)
    )


def gelu_pair(value):
    cdf = 0.5 * (1.0 + jax.scipy.special.erf(value * HALF_ROOT))
    return (value * cdf, cdf + value * jnp.exp(-0.5 * value * value) * INV_ROOT_TAU)


def contract_first(left, right):
    return lax.dot_general(
        left, right, (((0,), (0,)), ((), ())), preferred_element_type=jnp.float32
    )


def contract_last(left, right):
    return lax.dot_general(
        left, right, (((1,), (1,)), ((), ())), preferred_element_type=jnp.float32
    )


def masked_scores(query_clip, keys_clip, length, positions, scale):
    raw = (
        jnp.einsum("qhe,khe->hqk", query_clip, keys_clip, preferred_element_type=jnp.float32)
        * scale
    )
    return jnp.where((positions < length)[None, None, :], raw, NEG)


def plain(
    tokens,
    clip_len,
    slot_clip,
    w_qkv,
    bias_q,
    bias_v,
    w_out,
    bias_out,
    w_up,
    bias_up,
    w_down,
    bias_down,
    gain1,
    shift1,
    gain2,
    shift2,
    grad_out,
):
    rows, width = tokens.shape
    clips = slot_clip.shape[0]
    cap = rows // clips
    local = w_qkv.shape[2]
    heads = local // HD
    scale = HD ** (-0.5)
    positions = jnp.arange(cap, dtype=jnp.int32)
    match = slot_clip[:, None] == jnp.arange(clip_len.shape[0], dtype=jnp.int32)[None, :]
    lengths = jnp.sum(jnp.where(match, clip_len[None, :], 0), 1)
    valid = (positions[None, :] < lengths[:, None]).reshape(rows, 1)
    source = tokens.astype(jnp.float32)
    normed1, rstd1, pre1 = layer_norm(source, gain1, shift1)
    act1 = pre1.astype(jnp.bfloat16)
    joined = w_qkv.reshape(width, 3 * local)
    proj = jnp.dot(act1, joined, preferred_element_type=jnp.float32)
    query = (proj[:, :local] + bias_q).astype(jnp.bfloat16)
    keys = proj[:, local : 2 * local].astype(jnp.bfloat16)
    values = (proj[:, 2 * local :] + bias_v).astype(jnp.bfloat16)

    def per_clip(value):
        return value.reshape(clips, cap, heads, HD)

    def forward_clip(inputs):
        query_clip, keys_clip, values_clip, length = inputs
        raw = masked_scores(query_clip, keys_clip, length, positions, scale)
        top = jnp.max(raw, -1, keepdims=True)
        lse = top + jnp.log(jnp.sum(jnp.exp(raw - top), -1, keepdims=True))
        probs = jnp.exp(raw - lse).astype(jnp.bfloat16)
        context_clip = jnp.einsum(
            "hqk,khe->qhe", probs, values_clip, preferred_element_type=jnp.float32
        )
        return (context_clip.astype(jnp.bfloat16), lse)

    context_all, lse_all = lax.map(
        forward_clip, (per_clip(query), per_clip(keys), per_clip(values), lengths)
    )
    context = context_all.reshape(rows, local)
    attended = lax.psum(
        jnp.dot(context, w_out, preferred_element_type=jnp.float32).astype(jnp.bfloat16), "tensor"
    ).astype(jnp.float32)
    middle = source + attended + bias_out
    normed2, rstd2, pre2 = layer_norm(middle, gain2, shift2)
    act2 = pre2.astype(jnp.bfloat16)
    pre = jnp.dot(act2, w_up, preferred_element_type=jnp.float32) + bias_up
    hidden_f, slope = gelu_pair(pre)
    hidden = hidden_f.astype(jnp.bfloat16)
    branch = lax.psum(
        jnp.dot(hidden, w_down, preferred_element_type=jnp.float32).astype(jnp.bfloat16), "tensor"
    ).astype(jnp.float32)
    mixed = jnp.where(valid, middle + branch + bias_down, 0.0).astype(jnp.bfloat16)
    upstream = jnp.where(valid, grad_out.astype(jnp.float32), 0.0)
    upstream_b = upstream.astype(jnp.bfloat16)
    g_down_bias = jnp.sum(upstream, 0)
    g_down = contract_first(hidden, upstream_b)
    d_pre = contract_last(upstream_b, w_down) * slope
    g_up_bias = jnp.sum(d_pre, 0)
    d_pre_b = d_pre.astype(jnp.bfloat16)
    g_up = contract_first(act2, d_pre_b)
    d_act2 = lax.psum(contract_last(d_pre_b, w_up).astype(jnp.bfloat16), "tensor").astype(
        jnp.float32
    )
    g_gain2 = jnp.sum(d_act2 * normed2, 0)
    g_shift2 = jnp.sum(d_act2, 0)
    d_middle = upstream + layer_norm_back(d_act2, normed2, rstd2, gain2)
    g_out_bias = jnp.sum(d_middle, 0)
    d_middle_b = d_middle.astype(jnp.bfloat16)
    g_out = contract_first(context, d_middle_b)
    d_context = contract_last(d_middle_b, w_out).astype(jnp.bfloat16)

    def backward_clip(inputs):
        query_clip, keys_clip, values_clip, context_clip, dcontext_clip, lse, length = inputs
        raw = masked_scores(query_clip, keys_clip, length, positions, scale)
        probs_f = jnp.exp(raw - lse)
        probs = probs_f.astype(jnp.bfloat16)
        d_probs = jnp.einsum(
            "qhe,khe->hqk", dcontext_clip, values_clip, preferred_element_type=jnp.float32
        )
        delta = jnp.sum(dcontext_clip.astype(jnp.float32) * context_clip.astype(jnp.float32), -1).T[
            :, :, None
        ]
        d_scores = (probs_f * (d_probs - delta) * scale).astype(jnp.bfloat16)
        d_query_clip = jnp.einsum(
            "hqk,khe->qhe", d_scores, keys_clip, preferred_element_type=jnp.float32
        )
        d_keys_clip = jnp.einsum(
            "hqk,qhe->khe", d_scores, query_clip, preferred_element_type=jnp.float32
        )
        d_values_clip = jnp.einsum(
            "hqk,qhe->khe", probs, dcontext_clip, preferred_element_type=jnp.float32
        )
        return (d_query_clip, d_keys_clip, d_values_clip)

    d_query, d_keys, d_values = lax.map(
        backward_clip,
        (
            per_clip(query),
            per_clip(keys),
            per_clip(values),
            context_all,
            per_clip(d_context),
            lse_all,
            lengths,
        ),
    )
    d_query = d_query.reshape(rows, local)
    d_keys = d_keys.reshape(rows, local)
    d_values = d_values.reshape(rows, local)
    g_bias_q = jnp.sum(d_query, 0)
    g_bias_v = jnp.sum(d_values, 0)
    stacked = jnp.concatenate(
        [d_query.astype(jnp.bfloat16), d_keys.astype(jnp.bfloat16), d_values.astype(jnp.bfloat16)],
        1,
    )
    g_qkv = contract_first(act1, stacked).reshape(width, 3, local)
    d_act1 = lax.psum(contract_last(stacked, joined).astype(jnp.bfloat16), "tensor").astype(
        jnp.float32
    )
    g_gain1 = jnp.sum(d_act1 * normed1, 0)
    g_shift1 = jnp.sum(d_act1, 0)
    d_tokens = jnp.where(valid, d_middle + layer_norm_back(d_act1, normed1, rstd1, gain1), 0.0)
    (
        g_qkv,
        g_bias_q,
        g_bias_v,
        g_out,
        g_out_bias,
        g_up,
        g_up_bias,
        g_down,
        g_down_bias,
        g_gain1,
        g_shift1,
        g_gain2,
        g_shift2,
    ) = (
        lax.psum(g_qkv.astype(jnp.bfloat16), "dp").astype(jnp.float32),
        lax.psum(g_bias_q.astype(jnp.bfloat16), "dp").astype(jnp.float32),
        lax.psum(g_bias_v.astype(jnp.bfloat16), "dp").astype(jnp.float32),
        lax.psum(g_out.astype(jnp.bfloat16), "dp").astype(jnp.float32),
        lax.psum(g_out_bias.astype(jnp.bfloat16), "dp").astype(jnp.float32),
        lax.psum(g_up.astype(jnp.bfloat16), "dp").astype(jnp.float32),
        lax.psum(g_up_bias.astype(jnp.bfloat16), "dp").astype(jnp.float32),
        lax.psum(g_down.astype(jnp.bfloat16), "dp").astype(jnp.float32),
        lax.psum(g_down_bias.astype(jnp.bfloat16), "dp").astype(jnp.float32),
        lax.psum(g_gain1.astype(jnp.bfloat16), "dp").astype(jnp.float32),
        lax.psum(g_shift1.astype(jnp.bfloat16), "dp").astype(jnp.float32),
        lax.psum(g_gain2.astype(jnp.bfloat16), "dp").astype(jnp.float32),
        lax.psum(g_shift2.astype(jnp.bfloat16), "dp").astype(jnp.float32),
    )
    return (
        mixed,
        d_tokens,
        g_qkv,
        g_bias_q,
        g_bias_v,
        g_out,
        g_out_bias,
        g_up,
        g_up_bias,
        g_down,
        g_down_bias,
        g_gain1,
        g_shift1,
        g_gain2,
        g_shift2,
    )


MESH = pl.DeviceIdType.MESH
DMA = pltpu.SemaphoreType.DMA
ANY = pl.BlockSpec(memory_space=pl.ANY)
VMEM = pl.BlockSpec(memory_space=pltpu.VMEM)
SMEM = pl.BlockSpec(memory_space=pltpu.SMEM)
BLOCKS = (80, 96, 112)
BQ = 256
BK = 256


def cost(us):
    return pl.CostEstimate(flops=int(us * 1e9), bytes_accessed=int(us * 3e6), transcendentals=0)


def coords():
    dp = lax.axis_index("dp")
    t = lax.axis_index("tensor")
    return dp // 2, dp % 2, t // 2, t % 2


def device(z, y, x, c):
    return (z * 2 + y, x * 2 + c)


def greet(peers):
    barrier = pltpu.get_barrier_semaphore()
    for peer in peers:
        pl.semaphore_signal(barrier, inc=1, device_id=peer, device_id_type=MESH)
    pl.semaphore_wait(barrier, len(peers))


def greet_grid():
    z, y, x, c = coords()
    barrier = pltpu.get_barrier_semaphore()

    def signal(peer):
        pl.semaphore_signal(barrier, inc=1, device_id=peer, device_id_type=MESH)

    @pl.when(z > 0)
    def _():
        signal(device(z - 1, y, x, c))

    @pl.when(z < 3)
    def _():
        signal(device(z + 1, y, x, c))

    signal(device(z, 1 - y, x, c))
    signal(device(z, y, 1 - x, c))
    signal(device(z, y, x, 1 - c))

    pl.semaphore_wait(barrier, 3 + jnp.minimum(z, 1) + jnp.minimum(3 - z, 1))


GATHER_SEMS = [DMA, DMA((4,)), DMA((4,)), DMA((4,)), DMA((8,)), DMA((16,)), DMA((32,))]


def gather_steps(x_refs, o_refs, sems, work=None, ahead=None):
    z, y, x, c = coords()
    n = len(GATHER_SEMS)
    arrays = [(a, o) + tuple(sems[n * i : n * i + n]) for i, (a, o) in enumerate(zip(x_refs, o_refs))]

    def block(z, y, x, c):
        return (z * 2 + y) * 4 + x * 2 + c

    ux, uy = x + (1 - c) * (1 - 2 * x), y + c * (1 - 2 * y)
    vx, vy = x + c * (1 - 2 * x), y + (1 - c) * (1 - 2 * y)
    own = block(z, y, x, c)
    core = device(z, y, x, 1 - c)

    def rows(array, b):
        size = array[0].shape[0]
        return array[1].at[pl.ds(pl.multiple_of(b * size, size), size)]

    def copy(array, b, kind, i, peer):
        return pltpu.make_async_remote_copy(
            src_ref=rows(array, b),
            dst_ref=rows(array, b),
            send_sem=array[kind].at[i],
            recv_sem=array[8].at[b],
            device_id=peer,
            device_id_type=MESH,
        )

    def send(b, kind, i, peer, first=False):
        for array in arrays:
            if first:
                pltpu.make_async_remote_copy(
                    src_ref=array[0],
                    dst_ref=rows(array, b),
                    send_sem=array[kind].at[i],
                    recv_sem=array[8].at[b],
                    device_id=peer,
                    device_id_type=MESH,
                ).start()
            else:
                copy(array, b, kind, i, peer).start()

    def arrived(b):
        for array in arrays:
            copy(array, b, 7, 0, core).wait_recv()

    right, left = device(z + 1, y, x, c), device(z - 1, y, x, c)
    u, v = device(z, uy, ux, c), device(z, vy, vx, c)
    locals_ = [pltpu.make_async_copy(a[0], rows(a, own), a[2]) for a in arrays]

    @pl.when(z < 3)
    def _():
        send(own, 3, z, right, True)

    @pl.when(z > 0)
    def _():
        send(own, 4, z, left, True)

    send(own, 5, z, u, True)
    send(own, 6, z, v, True)
    send(own, 7, z, core, True)
    for local in locals_:
        local.start()

    def near(step):
        def from_low(low):
            return jnp.where((low == 1) & (step < 2), 1 - step, step)

        return jnp.where(z < 2, from_low(z), 3 - from_low(3 - z))

    def got_line(at):
        b = block(at, y, x, c)
        arrived(b)

        @pl.when((at < z) & (z < 3))
        def _():
            send(b, 3, at, right)

        @pl.when((at > z) & (z > 0))
        def _():
            send(b, 4, at, left)

        send(b, 5, at, u)
        send(b, 6, at, v)
        send(b, 7, at, core)

    def got_u(at):
        b = block(at, uy, ux, c)
        arrived(b)
        send(b, 6, 4 + at, v)
        send(b, 7, 4 + at, core)

    def got_v(at):
        b = block(at, vy, vx, c)
        arrived(b)
        send(b, 7, 8 + at, core)

    def got_uv(at):
        b = block(at, 1 - y, 1 - x, c)
        arrived(b)
        send(b, 7, 12 + at, core)

    def meanwhile(step):
        if ahead is not None:
            ahead(step)

    def around(event, distance):
        for side in (-1, 1) if distance else (0,):
            at = z + side * distance
            pl.when((at >= 0) & (at < 4))(functools.partial(event, at))

    for distance in range(1, 4):
        around(got_line, distance)
        meanwhile(2 * distance - 2)
        around(got_u, distance - 1)
        meanwhile(2 * distance - 1)
    around(got_u, 3)
    meanwhile(6)
    for local in locals_:
        local.wait()

    @pl.loop(0, 4)
    def _(step):
        at = near(step)
        got_v(at)
        meanwhile(7 + 3 * step)
        got_uv(at)
        meanwhile(8 + 3 * step)

        @pl.loop(0, 4)
        def _(i):
            arrived(at * 8 + i * 2 + 1 - c)

        meanwhile(9 + 3 * step)

        if work is not None:
            work(at)

    def sent(kind, i):
        for array in arrays:
            copy(array, own, kind, i, core).wait_send()

    @pl.loop(0, 16)
    def _(i):
        sent(7, i)

    @pl.loop(0, 8)
    def _(i):
        sent(6, i)

    @pl.loop(0, 4)
    def _(i):
        sent(5, i)

        @pl.when((i <= z) & (z < 3))
        def _():
            sent(3, i)

        @pl.when((i >= z) & (z > 0))
        def _():
            sent(4, i)


def table_kernel(x_ref, o_ref, send_sem, recv_sem):
    me = lax.axis_index("dp")
    t = lax.axis_index("tensor")
    peers = [(lax.rem(me + s, 8), t) for s in range(1, 8)]
    greet(peers)
    o_ref[me] = x_ref[...]
    copies = [
        pltpu.make_async_remote_copy(
            src_ref=x_ref,
            dst_ref=o_ref.at[me],
            send_sem=send_sem.at[s],
            recv_sem=recv_sem.at[s],
            device_id=peer,
            device_id_type=MESH,
        )
        for s, peer in enumerate(peers)
    ]
    for copy in copies:
        copy.start()
    for copy in copies:
        copy.wait()


def gather_table(value, cid):
    tile = jnp.broadcast_to(value.reshape(1, 1), (8, 128))
    out = pl.pallas_call(
        table_kernel,
        out_shape=jax.ShapeDtypeStruct((8, 8, 128), value.dtype),
        in_specs=[VMEM],
        out_specs=VMEM,
        scratch_shapes=[DMA((7,)), DMA((7,))],
        compiler_params=pltpu.CompilerParams(collective_id=cid, has_side_effects=True),
        name="table",
    )(tile)
    return out[:, 0, 0]


def pieces_kernel(size, table_ref, clip_ref, x_ref, u_ref, xo_ref, uo_ref, offset_ref, length_ref, held, sems):
    t = lax.axis_index("tensor")
    dp = lax.axis_index("dp")
    cap = x_ref.shape[0]
    loads = [
        pltpu.make_async_copy(src, held.at[i, pl.ds(size, cap)], sems.at[i])
        for i, src in enumerate((x_ref, u_ref))
    ]
    for load in loads:
        load.start()
    lengths = []
    for s in range(8):
        clip = table_ref[s]
        lengths.append(jnp.where(clip >= 0, clip_ref[jnp.maximum(clip, 0)], 0))
    offset = length = 0
    for s in range(8):
        before = 0
        for o in range(8):
            if o != s:
                ahead = lengths[o] >= lengths[s] if o < s else lengths[o] > lengths[s]
                before += jnp.where(ahead, (lengths[o] + 15) // 16 * 16, 0)
        offset_ref[s] = before
        length_ref[s] = lengths[s]
        offset = jnp.where(dp == s, before, offset)
        length = jnp.where(dp == s, lengths[s], length)
    offset_ref[8] = offset
    length_ref[8] = length
    for i in (0, 1):
        held[i, 0:size, :] = jnp.zeros((size, held.shape[2]), held.dtype)
        held[i, size + cap :, :] = jnp.zeros((size, held.shape[2]), held.dtype)
    for i, out in enumerate((xo_ref, uo_ref)):
        loads[i].wait()

        @pl.loop(0, 8)
        def _(b):
            first = (b * 4 + t) * size - offset + size
            first = pl.multiple_of(jnp.clip(first, 0, cap + size), 16)
            row = lax.broadcasted_iota(jnp.int32, (size, 1), 0) + first - size
            value = held[i, pl.ds(first, size), :].astype(jnp.float32)
            value = jnp.where((row >= 0) & (row < length), value, 0.0)
            out[b] = value.astype(jnp.bfloat16)


def take_pieces(x, u, table, clip_len, size):
    cap, width = x.shape
    shape = jax.ShapeDtypeStruct((8, size, width), jnp.bfloat16)
    ints = jax.ShapeDtypeStruct((9,), jnp.int32)
    return pl.pallas_call(
        functools.partial(pieces_kernel, size),
        out_shape=(shape, shape, ints, ints),
        in_specs=[SMEM, SMEM, ANY, ANY],
        out_specs=(VMEM, VMEM, SMEM, SMEM),
        scratch_shapes=[pltpu.VMEM((2, cap + 2 * size, width), jnp.bfloat16), DMA((2,))],
        compiler_params=pltpu.CompilerParams(vmem_limit_bytes=60 << 20),
        name="pieces",
    )(table, clip_len, x, u)


def pack_kernel(
    p_ref,
    wt_ref,
    bias_ref,
    gain_ref,
    shift_ref,
    own,
    act_ref,
    k_ref,
    vt_ref,
    qt_ref,
    x_all,
    acc,
    y_out,
    y_in,
    r_out,
    r_in,
    l_out,
    l_in,
    ys,
    yr,
    rs,
    rr,
    ls,
    lr,
    *gather_sems,
):
    z, y, x, c = coords()
    size = own.shape[0]
    local = k_ref.shape[1]
    greet_grid()

    def piece(zp, yp):
        return p_ref[zp * 2 + yp].astype(jnp.float32)

    def project(at):
        @pl.loop(0, 8)
        def _(i):
            r = pl.ds(pl.multiple_of(at * 8 * size + i * size, size), size)
            _, _, pre = layer_norm(x_all[r, :].astype(jnp.float32), gain_ref[...], shift_ref[...])
            act_ref[r, :] = pre.astype(jnp.bfloat16)

        r = pl.ds(pl.multiple_of(at * 8 * size, 8 * size), 8 * size)
        k_ref[r, :] = dot_nt(act_ref[r, :], wt_ref[local : 2 * local, :]).astype(jnp.bfloat16)
        vt = dot_nt(wt_ref[2 * local :, :], act_ref[r, :]) + bias_ref[2 * local :, :]
        vt_ref[:, r] = vt.astype(jnp.bfloat16)

        @pl.when(at == z)
        def _():
            qt = dot_nt(wt_ref[:local, :], act_ref[r, :]) + bias_ref[:local, :]
            qt_ref[...] = qt.astype(jnp.bfloat16) * jnp.bfloat16(HD**-0.5)

    def y_copy(i):
        return pltpu.make_async_remote_copy(
            src_ref=y_out.at[i],
            dst_ref=y_in.at[i],
            send_sem=ys.at[i],
            recv_sem=yr.at[i],
            device_id=device(z, 1 - y, x, c),
            device_id_type=MESH,
        )

    def r_copy(i):
        return pltpu.make_async_remote_copy(
            src_ref=r_out.at[i],
            dst_ref=r_in.at[i],
            send_sem=rs.at[i],
            recv_sem=rr.at[i],
            device_id=device(z + 1, y, x, c),
            device_id_type=MESH,
        )

    def l_copy(i):
        return pltpu.make_async_remote_copy(
            src_ref=l_out.at[i],
            dst_ref=l_in.at[i],
            send_sem=ls.at[i],
            recv_sem=lr.at[i],
            device_id=device(z - 1, y, x, c),
            device_id_type=MESH,
        )

    def add(ref, copy, i):
        copy(i).wait_recv()
        acc[...] += ref[i].astype(jnp.float32)

    def flow(zp, yp, first):
        i = zp * 2 + yp

        @pl.when(z < zp)
        def _():
            first()

            @pl.when(z > 0)
            def _():
                add(r_in, r_copy, i)

            r_out[i] = acc[...].astype(jnp.bfloat16)
            r_copy(i).start()

        @pl.when(z > zp)
        def _():
            first()

            @pl.when(z < 3)
            def _():
                add(l_in, l_copy, i)

            l_out[i] = acc[...].astype(jnp.bfloat16)
            l_copy(i).start()

    def land(yp):
        @pl.when(z > 0)
        def _():
            add(r_in, r_copy, z * 2 + yp)

        @pl.when(z < 3)
        def _():
            add(l_in, l_copy, z * 2 + yp)

    order = (0, 3, 1, 2)

    @pl.when(c == 0)
    def _():
        for zp in order:
            y_out[zp] = piece(zp, 1 - y).astype(jnp.bfloat16)
            y_copy(zp).start()
        for zp in order:

            def first(zp=zp):
                acc[...] = piece(zp, y)
                add(y_in, y_copy, zp)

            flow(zp, y, first)
        acc[...] = piece(z, y)
        add(y_in, y_copy, z)
        land(y)
        own[...] = acc[...].astype(jnp.bfloat16)
        for zp in order:
            y_copy(zp).wait_send()

    @pl.when(c == 1)
    def _():
        for zp in order:
            for yp in (0, 1):

                def first(zp=zp, yp=yp):
                    acc[...] = piece(zp, yp)

                flow(zp, yp, first)
        acc[...] = piece(z, 1 - y)
        land(1 - y)
        y_out[0] = acc[...].astype(jnp.bfloat16)
        y_copy(0).start()
        acc[...] = piece(z, y)
        land(y)
        add(y_in, y_copy, 0)
        own[...] = acc[...].astype(jnp.bfloat16)
        y_copy(0).wait_send()

    for zp in range(4):
        for yp in (0, 1):
            used = (c == 1) | (y == yp)

            @pl.when(used & (z < zp))
            def _(i=zp * 2 + yp):
                r_copy(i).wait_send()

            @pl.when(used & (z > zp))
            def _(i=zp * 2 + yp):
                l_copy(i).wait_send()

    gather_steps([own], [x_all], gather_sems, project)


def pack_gather(parts, wt, bias, gain, shift, cid):
    _, size, width = parts.shape
    bf16 = jnp.bfloat16
    rows = 32 * size
    local = wt.shape[0] // 3
    slots = pltpu.VMEM((8, size, width), bf16)
    quarter = pltpu.VMEM((4, size, width), bf16)
    return pl.pallas_call(
        pack_kernel,
        out_shape=(
            jax.ShapeDtypeStruct((size, width), bf16),
            jax.ShapeDtypeStruct((rows, width), bf16),
            jax.ShapeDtypeStruct((rows, local), bf16),
            jax.ShapeDtypeStruct((local, rows), bf16),
            jax.ShapeDtypeStruct((local, 8 * size), bf16),
        ),
        in_specs=[VMEM] * 5,
        out_specs=[VMEM] * 5,
        scratch_shapes=[
            pltpu.VMEM((rows, width), bf16),
            pltpu.VMEM((size, width), jnp.float32),
            quarter,
            quarter,
            slots,
            slots,
            slots,
            slots,
            DMA((4,)),
            DMA((4,)),
            DMA((8,)),
            DMA((8,)),
            DMA((8,)),
            DMA((8,)),
        ]
        + GATHER_SEMS,
        compiler_params=pltpu.CompilerParams(
            collective_id=cid, has_side_effects=True, vmem_limit_bytes=60 << 20
        ),
        cost_estimate=cost(90),
        name="pack_gather",
    )(parts, wt, bias[:, None], gain[None], shift[None])


def greet_all():
    z, y, x, c = coords()
    barrier = pltpu.get_barrier_semaphore()

    def signal(peer):
        pl.semaphore_signal(barrier, inc=1, device_id=peer, device_id_type=MESH)

    @pl.when(z > 0)
    def _():
        signal(device(z - 1, y, x, c))

    @pl.when(z < 3)
    def _():
        signal(device(z + 1, y, x, c))

    signal(device(z, 1 - y, x, c))
    for peer in (device(z, y, 1 - x, c), device(z, y, x, 1 - c), device(z, y, 1 - x, 1 - c)):
        signal(peer)
    pl.semaphore_wait(barrier, 4 + jnp.minimum(z, 1) + jnp.minimum(3 - z, 1))


def share_start(p_ref, landed, send_sem, recv_sem):
    dp = lax.axis_index("dp")
    t = lax.axis_index("tensor")
    copies = [
        pltpu.make_async_remote_copy(
            src_ref=p_ref.at[peer],
            dst_ref=landed.at[s],
            send_sem=send_sem.at[s],
            recv_sem=recv_sem.at[s],
            device_id=(dp, peer),
            device_id_type=MESH,
        )
        for s, peer in enumerate([lax.rem(t + s, 4) for s in (2, 3, 1)])
    ]
    for copy in copies:
        copy.start()
    return copies


def share_sum(p_ref, landed, copies):
    total = p_ref[lax.axis_index("tensor")].astype(jnp.float32)
    for s, copy in enumerate(copies):
        copy.wait_recv()
        total += landed[s].astype(jnp.float32)
    for copy in copies:
        copy.wait_send()
    return total


def share_scratch(size, width):
    return [pltpu.VMEM((3, size, width), jnp.bfloat16), DMA((3,)), DMA((3,))]


def load_all(sources, targets, sems):
    copies = [
        pltpu.make_async_copy(a, b, sems.at[i]) for i, (a, b) in enumerate(zip(sources, targets))
    ]
    for copy in copies:
        copy.start()
    return copies


def products(units, early):
    total = sum(count for _, count in units)
    each = (total - early + 9) // 10

    def run(job):
        before = 0
        for unit, count in units:
            pl.when((job >= before) & (job < before + count))(functools.partial(unit, job - before))
            before += count

    def now():
        pl.loop(0, early)(run)

    def ahead(step):
        @pl.when(step < 10)
        def _():
            pl.loop(0, each)(lambda i: run(early + step * each + i))

    return now, ahead


def outer_unit(a, b, out, tall, wide):
    across = b.shape[1] // wide

    def unit(job):
        n = pl.ds(pl.multiple_of(lax.rem(job, across) * wide, 128), wide)
        if tall == out.shape[0]:
            out[:, n] = dot_tn(a[:, :tall], b[:, n]).astype(out.dtype)
        else:
            m = pl.ds(pl.multiple_of(job // across * tall, 128), tall)
            out[m, n] = dot_tn(a[:, m], b[:, n]).astype(out.dtype)

    return unit, out.shape[0] // tall * across


def first_kernel(
    p_ref, x_ref, bias_ref, gain_ref, shift_ref, wt_ref, wbias_ref, act_ref,
    mid_ref, o_ref, qkt_ref, v_ref,
    own, act, load_sem, landed, ss, sr, *sems,
):
    (load,) = load_all((act_ref,), (act,), load_sem)
    greet_all()
    copies = share_start(p_ref, landed, ss, sr)
    local = v_ref.shape[1]
    chunk = act.shape[0] // 4
    load.wait()

    def project(job):
        r = pl.ds(pl.multiple_of(job // 3 * chunk, 128), chunk)
        kind = lax.rem(job, 3)

        @pl.when(kind == 0)
        def _():
            qt = dot_nt(wt_ref[:local, :], act[r, :]) + wbias_ref[:local, :]
            qkt_ref[:local, r] = qt.astype(jnp.bfloat16) * jnp.bfloat16(HD**-0.5)

        @pl.when(kind == 1)
        def _():
            kt = dot_nt(wt_ref[local : 2 * local, :], act[r, :])
            qkt_ref[local:, r] = kt.astype(jnp.bfloat16)

        @pl.when(kind == 2)
        def _():
            v = dot_nt(act[r, :], wt_ref[2 * local :, :]) + wbias_ref[2 * local :, :].T
            v_ref[r, :] = v.astype(jnp.bfloat16)

    project(0)
    project(1)
    middle = x_ref[...].astype(jnp.float32) + share_sum(p_ref, landed, copies) + bias_ref[...]
    mid_ref[...] = middle
    _, _, pre = layer_norm(middle, gain_ref[...], shift_ref[...])
    own[...] = pre.astype(jnp.bfloat16)

    def ahead(step):
        pl.when(step < 10)(functools.partial(project, step + 2))

    gather_steps([own], [o_ref], sems, ahead=ahead)


def first_exchange(part, source, bias_out, gain2, shift2, wt, bias, act1, cid):
    size, width = source.shape
    rows = 32 * size
    local = wt.shape[0] // 3
    bf16 = jnp.bfloat16
    return pl.pallas_call(
        first_kernel,
        out_shape=(
            jax.ShapeDtypeStruct((size, width), jnp.float32),
            jax.ShapeDtypeStruct((rows, width), bf16),
            jax.ShapeDtypeStruct((2 * local, rows), bf16),
            jax.ShapeDtypeStruct((rows, local), bf16),
        ),
        in_specs=[VMEM] * 7 + [ANY],
        out_specs=[VMEM, ANY, VMEM, VMEM],
        scratch_shapes=[pltpu.VMEM((size, width), bf16), pltpu.VMEM((rows, width), bf16), DMA((1,))]
        + share_scratch(size, width)
        + GATHER_SEMS,
        compiler_params=pltpu.CompilerParams(
            collective_id=cid, has_side_effects=True, vmem_limit_bytes=60 << 20
        ),
        cost_estimate=cost(60),
        name="first_exchange",
    )(
        part.reshape(4, size, width), source, bias_out[None], gain2[None], shift2[None],
        wt, bias[:, None], act1,
    )


def second_kernel(
    p_ref, b_ref, mid_ref, up_ref, gain_ref, bias_ref, wout_ref, act_ref, hid_ref, dpre_ref, upall_ref,
    dmid_ref, mixed_ref, vec_ref, o_ref, gup_ref, gdown_ref, dctx_ref,
    own, landed, ss, sr, landed2, ss2, sr2, some, act, hid, dpre, upall, load_sem, *sems,
):
    loads = load_all((act_ref, dpre_ref, hid_ref, upall_ref), (act, dpre, hid, upall), load_sem)
    greet_all()
    copies = share_start(p_ref, landed, ss, sr)
    branch_copies = share_start(b_ref, landed2, ss2, sr2)
    now, work = products(
        [outer_unit(act, dpre, gup_ref, 256, 1280), outer_unit(hid, upall, gdown_ref, 256, 1280)], 2
    )
    for load in loads:
        load.wait()
    now()
    grad = share_sum(p_ref, landed, copies)
    middle = mid_ref[...]
    normed, rstd, _ = layer_norm(middle, 1.0, 0.0)
    d_middle = up_ref[...].astype(jnp.float32) + layer_norm_back(grad, normed, rstd, gain_ref[...])
    own[...] = d_middle.astype(jnp.bfloat16)
    dmid_ref[...] = d_middle
    vec_ref[...] = jnp.concatenate(
        [
            jnp.sum(grad * normed, 0, keepdims=True),
            jnp.sum(grad, 0, keepdims=True),
            jnp.sum(up_ref[...].astype(jnp.float32), 0, keepdims=True),
            jnp.sum(d_middle, 0, keepdims=True),
            jnp.zeros((4, grad.shape[1]), jnp.float32),
        ],
        0,
    )
    def ahead(step):
        @pl.when(step == 0)
        def _():
            branch = share_sum(b_ref, landed2, branch_copies)
            mixed_ref[...] = (mid_ref[...] + branch + bias_ref[...]).astype(jnp.bfloat16)

        work(step)

    size = own.shape[0]

    def context_grad(at):
        r = pl.ds(pl.multiple_of(at * 8 * size, 8 * size), 8 * size)
        pltpu.sync_copy(o_ref.at[r], some)
        dctx_ref[:, r] = dot_nt(wout_ref[...], some[...]).astype(jnp.bfloat16)

    gather_steps([own], [o_ref], sems, context_grad, ahead)


def second_exchange(part, branch, middle, upstream, gain2, bias_down, w_out, act2, hidden, d_pre, up_all, cid):
    size, width = middle.shape
    f32, bf16 = jnp.float32, jnp.bfloat16
    rows, inner = hidden.shape
    return pl.pallas_call(
        second_kernel,
        out_shape=(
            jax.ShapeDtypeStruct((size, width), f32),
            jax.ShapeDtypeStruct((size, width), bf16),
            jax.ShapeDtypeStruct((8, width), f32),
            jax.ShapeDtypeStruct((rows, width), bf16),
            jax.ShapeDtypeStruct((width, inner), bf16),
            jax.ShapeDtypeStruct((inner, width), bf16),
            jax.ShapeDtypeStruct((w_out.shape[0], rows), bf16),
        ),
        in_specs=[VMEM] * 7 + [ANY] * 4,
        out_specs=[VMEM, VMEM, VMEM, ANY, VMEM, VMEM, VMEM],
        scratch_shapes=[pltpu.VMEM((size, width), bf16)]
        + share_scratch(size, width) * 2
        + [pltpu.VMEM((8 * size, width), bf16)]
        + [pltpu.VMEM((rows, n), bf16) for n in (width, inner, inner, width)]
        + [DMA((4,))]
        + GATHER_SEMS,
        compiler_params=pltpu.CompilerParams(
            collective_id=cid, has_side_effects=True, vmem_limit_bytes=60 << 20
        ),
        cost_estimate=cost(80),
        name="second_exchange",
    )(
        part.reshape(4, size, width), branch.reshape(4, size, width), middle, upstream,
        gain2[None], bias_down[None], w_out, act2, hidden, d_pre, up_all,
    )


def third_kernel(
    p_ref, x_ref, dmid_ref, gain_ref, vec_ref, act_ref, dt_ref, ctx_ref, dmall_ref,
    o_ref, vo_ref, gqkv_ref, gout_ref,
    own, vec, landed, ss, sr, act, dt, ctx, dmall, load_sem, *sems,
):
    loads = load_all((act_ref, dt_ref, ctx_ref, dmall_ref), (act, dt, ctx, dmall), load_sem)
    greet_all()
    copies = share_start(p_ref, landed, ss, sr)
    part = dt.shape[0] // 3

    def project(job):
        k = pl.ds(pl.multiple_of(job // 2 * part, 64), part)
        m = pl.ds(pl.multiple_of(lax.rem(job, 2) * 640, 128), 640)
        gqkv_ref[k, m] = dot_nn(dt[k, :], act[:, m]).astype(jnp.bfloat16)

    now, work = products([(project, 6), outer_unit(ctx, dmall, gout_ref, part, 640)], 2)
    for load in loads:
        load.wait()
    now()
    grad = share_sum(p_ref, landed, copies)
    normed, rstd, _ = layer_norm(x_ref[...].astype(jnp.float32), 1.0, 0.0)
    own[...] = (dmid_ref[...] + layer_norm_back(grad, normed, rstd, gain_ref[...])).astype(jnp.bfloat16)
    vec[...] = jnp.concatenate(
        [
            vec_ref[0:4, :],
            jnp.sum(grad * normed, 0, keepdims=True),
            jnp.sum(grad, 0, keepdims=True),
            jnp.zeros((2, grad.shape[1]), jnp.float32),
        ],
        0,
    )
    gather_steps([own, vec], [o_ref, vo_ref], sems, ahead=work)


def third_exchange(part, source, d_middle, gain1, vec, act1, d_qkv, context, d_middle_all, cid):
    size, width = d_middle.shape
    f32, bf16 = jnp.float32, jnp.bfloat16
    rows = act1.shape[0]
    total = d_qkv.shape[0]
    return pl.pallas_call(
        third_kernel,
        out_shape=(
            jax.ShapeDtypeStruct((rows, width), bf16),
            jax.ShapeDtypeStruct((256, width), f32),
            jax.ShapeDtypeStruct((total, width), bf16),
            jax.ShapeDtypeStruct((total // 3, width), bf16),
        ),
        in_specs=[VMEM] * 5 + [ANY] * 4,
        out_specs=[ANY, ANY, VMEM, VMEM],
        scratch_shapes=[pltpu.VMEM((size, width), bf16), pltpu.VMEM((8, width), f32)]
        + share_scratch(size, width)
        + [pltpu.VMEM(a.shape, bf16) for a in (act1, d_qkv, context, d_middle_all)]
        + [DMA((4,))]
        + GATHER_SEMS * 2,
        compiler_params=pltpu.CompilerParams(
            collective_id=cid, has_side_effects=True, vmem_limit_bytes=60 << 20
        ),
        cost_estimate=cost(60),
        name="third_exchange",
    )(
        part.reshape(4, size, width), source, d_middle, gain1[None], vec,
        act1, d_qkv, context, d_middle_all,
    )


def dot_nt(a, b):
    return lax.dot_general(a, b, (((1,), (1,)), ((), ())), preferred_element_type=jnp.float32)


def dot_nn(a, b):
    return lax.dot_general(a, b, (((1,), (0,)), ((), ())), preferred_element_type=jnp.float32)


def dot_tn(a, b):
    return lax.dot_general(a, b, (((0,), (0,)), ((), ())), preferred_element_type=jnp.float32)


def spans(offset_ref, length_ref, first, count):
    row = lax.broadcasted_iota(jnp.int32, (1, count), 1) + first
    start = jnp.zeros((1, count), jnp.int32)
    end = jnp.zeros((1, count), jnp.int32)
    low, high = 1 << 20, 0
    for i in range(8):
        a = offset_ref[i]
        b = a + length_ref[i]
        inside = (row >= a) & (row < b)
        start = jnp.where(inside, a, start)
        end = jnp.where(inside, b, end)
        used = (a < first + count) & (b > first) & (b > a)
        low = jnp.where(used, jnp.minimum(low, a // BK), low)
        high = jnp.where(used, jnp.maximum(high, (b + BK - 1) // BK), high)
    return start, end, low, high


def attend_kernel(heads, offset_ref, length_ref, qt_ref, k_ref, vt_ref, sent_ref, m_s, l_s, acc_s, win):
    mine = sent_ref.shape[0]
    rows = win.shape[0]
    local = heads * HD
    span = range(heads)
    dp = lax.axis_index("dp")
    skip = lax.rem(dp, 2) * (mine % 128)
    first = dp * mine - skip
    window = pl.ds(pl.multiple_of(lax.rem(dp, 2) * mine - skip, 128), rows)
    start, end, low, high = spans(offset_ref, length_ref, first, rows)
    m_s[...] = jnp.full_like(m_s, NEG)
    l_s[...] = jnp.zeros_like(l_s)
    acc_s[...] = jnp.zeros_like(acc_s)
    q = [qt_ref[h * HD : (h + 1) * HD, window] for h in span]

    def body(kb, carry):
        k0 = pl.multiple_of(kb * BK, BK)
        key = lax.broadcasted_iota(jnp.int32, (BK, rows), 0) + k0
        mask = (key >= start) & (key < end)
        s = [
            jnp.where(
                mask,
                dot_nn(k_ref[pl.ds(k0, BK), h * HD : (h + 1) * HD], q[h]),
                NEG,
            )
            for h in span
        ]
        p, a = [], []
        for h in span:
            old = m_s[h]
            new = jnp.maximum(old, jnp.max(s[h], 0, keepdims=True))
            e = jnp.exp(s[h] - new)
            scale = jnp.exp(old - new)
            l_s[h] = scale * l_s[h] + jnp.sum(e, 0, keepdims=True)
            m_s[h] = new
            p.append(e.astype(jnp.bfloat16))
            a.append(scale)
        for h in span:
            vt = vt_ref[h * HD : (h + 1) * HD, pl.ds(k0, BK)]
            acc_s[h] = a[h] * acc_s[h] + dot_nn(vt, p[h])
        return carry

    lax.fori_loop(low, high, body, 0)
    parts = [[], [], []]
    for h in span:
        total = l_s[h]
        total = jnp.where(total == 0.0, 1.0, total)
        rest = m_s[h] + jnp.log(total)
        for part in parts:
            part.append(rest.astype(jnp.bfloat16).astype(jnp.float32))
            rest = rest - part[-1]
        out = acc_s[h] * (1.0 / total)
        win[:, h * HD : (h + 1) * HD] = out.T
    blank = [jnp.zeros((win.shape[1] - local - 3 * heads, rows), jnp.float32)]
    win[:, local:] = jnp.concatenate(parts[0] + parts[1] + parts[2] + blank, 0).T
    sent_ref[...] = win[pl.ds(pl.multiple_of(skip, 16), mine), :].astype(jnp.bfloat16)


def whole(a):
    return pl.BlockSpec(a.shape, lambda i, *_: (0,) * len(a.shape), pipeline_mode=pl.Buffered(1))


def attend(qt, k, vt, offsets, lengths, heads):
    mine = k.shape[0] // 8
    rows = (mine + mine % 128 + 127) // 128 * 128
    local = heads * HD
    wide = (local + 3 * heads + 127) // 128 * 128
    row = pltpu.VMEM((heads, 1, rows), jnp.float32)
    return pl.pallas_call(
        functools.partial(attend_kernel, heads),
        out_shape=jax.ShapeDtypeStruct((mine, wide), jnp.bfloat16),
        in_specs=[SMEM, SMEM, VMEM, VMEM, VMEM],
        out_specs=VMEM,
        scratch_shapes=[
            row,
            row,
            pltpu.VMEM((heads, HD, rows), jnp.float32),
            pltpu.VMEM((rows, wide), jnp.float32),
        ],
        compiler_params=pltpu.CompilerParams(vmem_limit_bytes=60 << 20),
        cost_estimate=cost(10),
        name="attend",
    )(offsets, lengths, qt, k, vt)


def attend_back_kernel(
    heads, offset_ref, length_ref, k_ref, v_ref, qkt_ref, dot_ref, sent_ref, d_ref, sum_ref, dk_s, dv_s, dq_s
):
    i = pl.program_id(0)
    local = heads * HD
    span = range(heads)
    sl = [slice(h * HD, (h + 1) * HD) for h in span]
    at_q = pl.ds(pl.multiple_of(i * BQ, BQ), BQ)

    @pl.when(i == 0)
    def _():
        dk_s[...] = jnp.zeros_like(dk_s)
        dv_s[...] = jnp.zeros_like(dv_s)
        sum_ref[...] = jnp.zeros_like(sum_ref)

    start, end, low, high = spans(offset_ref, length_ref, i * BQ, BQ)
    dq_s[...] = jnp.zeros_like(dq_s)
    sent = sent_ref[at_q, :].astype(jnp.float32).T
    lse, delta = [], []
    for h in span:
        a = local + h
        lse.append(
            sent[a : a + 1] + sent[a + heads : a + heads + 1] + sent[a + 2 * heads : a + 2 * heads + 1]
        )
        delta.append(jnp.sum(dot_ref[sl[h], at_q].astype(jnp.float32) * sent[sl[h]], 0, keepdims=True))

    def body(kb, carry):
        at_k = pl.ds(pl.multiple_of(kb * BK, BK), BK)
        key = lax.broadcasted_iota(jnp.int32, (BK, BQ), 0) + kb * BK
        mask = (key >= start) & (key < end)

        def products(h):
            s = dot_nn(k_ref[at_k, sl[h]], qkt_ref[sl[h], at_q])
            dp = dot_nn(v_ref[at_k, sl[h]], dot_ref[sl[h], at_q])
            return s, dp

        def scores(h, s, dp):
            p = jnp.exp(jnp.where(mask, s, NEG) - lse[h])
            ds = (p * (dp - delta[h])).astype(jnp.bfloat16)
            return p.astype(jnp.bfloat16), ds

        def gradients(h, p, ds):
            dv_s[h, :, at_k] += dot_nt(dot_ref[sl[h], at_q], p)
            dk_s[h, :, at_k] += dot_nt(qkt_ref[sl[h], at_q], ds)
            dq_s[h] += dot_nn(qkt_ref[local + h * HD : local + (h + 1) * HD, at_k], ds)

        now = products(0)
        held = None
        for h in span:
            later = products(h + 1) if h + 1 < heads else None
            done = scores(h, *now)
            if held is not None:
                gradients(h - 1, *held)
            held, now = done, later
        gradients(heads - 1, *held)
        return carry

    lax.fori_loop(low, high, body, 0)
    for h in span:
        dq = dq_s[h] * HD**-0.5
        d_ref[sl[h], at_q] = dq.astype(jnp.bfloat16)
        sum_ref[sl[h], :] += dq[:, :128] + dq[:, 128:]

    @pl.when(i == pl.num_programs(0) - 1)
    def _():
        for h in span:
            d_ref[local + h * HD : local + (h + 1) * HD, :] = dk_s[h].astype(jnp.bfloat16)
            d_ref[2 * local + h * HD : 2 * local + (h + 1) * HD, :] = dv_s[h].astype(jnp.bfloat16)
            total = dv_s[h, :, 0:128]
            for n in range(1, dv_s.shape[2] // 128):
                total += dv_s[h, :, n * 128 : (n + 1) * 128]
            sum_ref[local + h * HD : local + (h + 1) * HD, :] = total


def attend_back(k, v, qkt, dot, sent, offsets, lengths, heads):
    rows = k.shape[0]
    local = heads * HD
    tall = pltpu.VMEM((heads, HD, rows), jnp.float32)

    def const(shape):
        return pl.BlockSpec(shape, lambda i, *_: (0, 0), pipeline_mode=pl.Buffered(1))

    return pl.pallas_call(
        functools.partial(attend_back_kernel, heads),
        out_shape=(
            jax.ShapeDtypeStruct((3 * local, rows), jnp.bfloat16),
            jax.ShapeDtypeStruct((2 * local, 128), jnp.float32),
        ),
        grid_spec=pltpu.PrefetchScalarGridSpec(
            num_scalar_prefetch=2,
            grid=(rows // BQ,),
            in_specs=[whole(a) for a in (k, v, qkt, dot, sent)],
            out_specs=[const((3 * local, rows)), const((2 * local, 128))],
            scratch_shapes=[tall, tall, pltpu.VMEM((heads, HD, BQ), jnp.float32)],
        ),
        compiler_params=pltpu.CompilerParams(vmem_limit_bytes=60 << 20),
        cost_estimate=cost(60),
        name="attend_back",
    )(offsets, lengths, k, v, qkt, dot, sent)


def widen_kernel(*refs):
    for src, dst in zip(refs[:4], refs[4:]):
        dst[...] = src[...].astype(jnp.float32)


def widen(*grads):
    specs = [pl.BlockSpec((a.shape[0] // 10, a.shape[1]), lambda i: (i, 0)) for a in grads]
    return pl.pallas_call(
        widen_kernel,
        grid=(10,),
        out_shape=[jax.ShapeDtypeStruct(a.shape, jnp.float32) for a in grads],
        in_specs=specs,
        out_specs=specs,
        compiler_params=pltpu.CompilerParams(vmem_limit_bytes=60 << 20),
        name="widen",
    )(*grads)


def unpack_kernel(offset_ref, length_ref, m_ref, d_ref, mo_ref, do_ref, m, d, sems):
    cap = mo_ref.shape[0]
    rows = m_ref.shape[0]
    offset = offset_ref[8]
    length = length_ref[8]
    first = pl.multiple_of(jnp.minimum(offset, rows - cap), 16)
    loads = [
        pltpu.make_async_copy(src.at[pl.ds(first, cap)], dst.at[pl.ds(0, cap)], sems.at[i])
        for i, (src, dst) in enumerate(((m_ref, m), (d_ref, d)))
    ]
    for load in loads:
        load.start()
    for load, src, dst in zip(loads, (m, d), (mo_ref, do_ref)):
        load.wait()

        @pl.loop(0, cap // 128)
        def _(i):
            at = pl.multiple_of(jnp.minimum(offset - first + i * 128, cap), 16)
            row = lax.broadcasted_iota(jnp.int32, (128, 1), 0) + i * 128
            value = jnp.where(row < length, src[pl.ds(at, 128), :].astype(jnp.float32), 0.0)
            dst[pl.ds(pl.multiple_of(i * 128, 128), 128), :] = value.astype(dst.dtype)


def unpack(offsets, lengths, mixed, d_tokens, cap):
    width = mixed.shape[1]
    held = pltpu.VMEM((cap + 128, width), jnp.bfloat16)
    return pl.pallas_call(
        unpack_kernel,
        out_shape=(
            jax.ShapeDtypeStruct((cap, width), jnp.bfloat16),
            jax.ShapeDtypeStruct((cap, width), jnp.float32),
        ),
        in_specs=[SMEM, SMEM, ANY, ANY],
        out_specs=[VMEM, VMEM],
        scratch_shapes=[held, held, DMA((2,))],
        compiler_params=pltpu.CompilerParams(vmem_limit_bytes=60 << 20),
        name="unpack",
    )(offsets, lengths, mixed, d_tokens)


def packed_step(size, cids, table, args):
    (
        tokens, clip_len, _, w_qkv, bias_q, bias_v, w_out, bias_out, w_up, bias_up, w_down, bias_down,
        gain1, shift1, gain2, shift2, grad_out,
    ) = args
    f32, bf16 = jnp.float32, jnp.bfloat16
    cap, width = tokens.shape
    local = w_qkv.shape[2]
    heads = local // HD
    rows = 32 * size
    mine = 4 * size
    dp = lax.axis_index("dp")
    pack_id, first_id, second_id, third_id = cids

    def own(value):
        return lax.dynamic_slice_in_dim(value, dp * mine, mine, 0)

    x_parts, up_parts, offsets, lengths = take_pieces(tokens, grad_out, table, clip_len, size)
    wt = w_qkv.transpose(1, 2, 0).reshape(3 * local, width)
    bias = jnp.concatenate([bias_q, jnp.zeros_like(bias_q), bias_v])
    source, act1, k, vt, qt = pack_gather(x_parts, wt, bias, gain1, shift1, pack_id)
    up_own = lax.psum_scatter(up_parts, "dp", scatter_dimension=0, tiled=True)
    up_own, source = lax.optimization_barrier((up_own, source))
    up_all = lax.all_gather(up_own.reshape(size, width), ("dp", "tensor"), tiled=True)

    sent_own = attend(qt, k, vt, offsets, lengths, heads)
    part = jnp.dot(sent_own[:, :local], w_out, preferred_element_type=f32).astype(bf16)
    sent = lax.all_gather(sent_own, "dp", tiled=True)
    middle, act2, qkt, v = first_exchange(
        part, source, bias_out, gain2, shift2, wt, bias, act1, first_id
    )

    pre = jnp.dot(act2, w_up, preferred_element_type=f32) + bias_up
    hidden_f, slope = gelu_pair(pre)
    hidden = hidden_f.astype(bf16)
    d_pre = contract_last(up_all, w_down) * slope
    g_up_bias = jnp.sum(d_pre, 0)
    d_pre_b = d_pre.astype(bf16)
    d_part = contract_last(own(d_pre_b), w_up).astype(bf16)
    branch = jnp.dot(own(hidden), w_down, preferred_element_type=f32).astype(bf16)
    d_middle, mixed, vec, d_middle_b, g_up, g_down, d_context = second_exchange(
        d_part, branch, middle, up_own.reshape(size, width), gain2, bias_down,
        w_out, act2, hidden, d_pre_b, up_all, second_id,
    )
    mixed_all = lax.all_gather(mixed, ("dp", "tensor"), tiled=True)
    d_qkv, column = attend_back(k, v, qkt, d_context, sent, offsets, lengths, heads)
    column = jnp.sum(column, 1)
    d_own = lax.dynamic_slice_in_dim(d_qkv, dp * mine, mine, 1)
    d_act1 = jnp.einsum("kr,kd->rd", d_own, wt, preferred_element_type=f32).astype(bf16)
    d_tokens_all, vectors_all, g_qkv, g_out = third_exchange(
        d_act1, source, d_middle, gain1, vec, act1, d_qkv, sent, d_middle_b, third_id
    )
    g_up, g_down, g_qkv, g_out = widen(g_up, g_down, g_qkv, g_out)
    g_qkv = g_qkv.reshape(3, local, width).transpose(2, 0, 1)
    sums = jnp.sum(vectors_all.reshape(32, 8, width), 0)
    mixed, d_tokens = unpack(offsets, lengths, mixed_all, d_tokens_all, cap)

    return (
        mixed,
        d_tokens,
        g_qkv,
        column[:local],
        column[local:],
        g_out,
        sums[3],
        g_up,
        g_up_bias,
        g_down,
        sums[2],
        sums[4],
        sums[5],
        sums[0],
        sums[1],
    )


def packed(*args):
    clip_len, slot_clip = args[1], args[2]

    def padded(value):
        return (value + 15) // 16 * 16

    need = jnp.sum(padded(clip_len))
    table = gather_table(slot_clip[0], 0)
    branches = [
        functools.partial(packed_step, size, [1 + 4 * n + i for i in range(4)])
        for n, size in enumerate(BLOCKS)
    ]
    pick = sum((need > 32 * size).astype(jnp.int32) for size in BLOCKS)

    def fallback(table, args):
        return plain(*args)

    return lax.switch(pick, branches + [fallback], table, args)


def solution(mesh):
    placed = (
        P("dp", None),
        P(),
        P("dp"),
        P(None, None, "tensor"),
        P("tensor"),
        P("tensor"),
        P("tensor", None),
        P(),
        P(None, "tensor"),
        P("tensor"),
        P("tensor", None),
        P(),
        P(),
        P(),
        P(),
        P(),
        P("dp", None),
    )
    fits = mesh.shape["dp"] == 8 and mesh.shape["tensor"] == 4
    return jax.shard_map(
        packed if fits else plain,
        mesh=mesh,
        in_specs=placed,
        out_specs=(
            P("dp", None),
            P("dp", None),
            P(None, None, "tensor"),
            P("tensor"),
            P("tensor"),
            P("tensor", None),
            P(),
            P(None, "tensor"),
            P("tensor"),
            P("tensor", None),
            P(),
            P(),
            P(),
            P(),
            P(),
        ),
        check_vma=False,
    )
```

```python
import functools

import jax
import jax.numpy as jnp
from jax import lax
from jax.experimental import pallas as pl
from jax.experimental.pallas import tpu as pltpu
from jax.sharding import PartitionSpec as P

HD = 64


EPS = 1e-05
NEG = -1e30
HALF_ROOT = 0.7071067811865476
INV_ROOT_TAU = 0.3989422804014327


def layer_norm(value, gain, shift):
    center = value - jnp.mean(value, -1, keepdims=True)
    rstd = lax.rsqrt(jnp.mean(center * center, -1, keepdims=True) + EPS)
    normed = center * rstd
    return (normed, rstd, normed * gain + shift)


def layer_norm_back(grad, normed, rstd, gain):
    scaled = grad * gain
    return rstd * (
        scaled
        - jnp.mean(scaled, -1, keepdims=True)
        - normed * jnp.mean(scaled * normed, -1, keepdims=True)
    )


def gelu_pair(value):
    cdf = 0.5 * (1.0 + jax.scipy.special.erf(value * HALF_ROOT))
    return (value * cdf, cdf + value * jnp.exp(-0.5 * value * value) * INV_ROOT_TAU)


def contract_first(left, right):
    return lax.dot_general(
        left, right, (((0,), (0,)), ((), ())), preferred_element_type=jnp.float32
    )


def contract_last(left, right):
    return lax.dot_general(
        left, right, (((1,), (1,)), ((), ())), preferred_element_type=jnp.float32
    )


def masked_scores(query_clip, keys_clip, length, positions, scale):
    raw = (
        jnp.einsum("qhe,khe->hqk", query_clip, keys_clip, preferred_element_type=jnp.float32)
        * scale
    )
    return jnp.where((positions < length)[None, None, :], raw, NEG)


def plain(
    tokens,
    clip_len,
    slot_clip,
    w_qkv,
    bias_q,
    bias_v,
    w_out,
    bias_out,
    w_up,
    bias_up,
    w_down,
    bias_down,
    gain1,
    shift1,
    gain2,
    shift2,
    grad_out,
):
    rows, width = tokens.shape
    clips = slot_clip.shape[0]
    cap = rows // clips
    local = w_qkv.shape[2]
    heads = local // HD
    scale = HD ** (-0.5)
    positions = jnp.arange(cap, dtype=jnp.int32)
    match = slot_clip[:, None] == jnp.arange(clip_len.shape[0], dtype=jnp.int32)[None, :]
    lengths = jnp.sum(jnp.where(match, clip_len[None, :], 0), 1)
    valid = (positions[None, :] < lengths[:, None]).reshape(rows, 1)
    source = tokens.astype(jnp.float32)
    normed1, rstd1, pre1 = layer_norm(source, gain1, shift1)
    act1 = pre1.astype(jnp.bfloat16)
    joined = w_qkv.reshape(width, 3 * local)
    proj = jnp.dot(act1, joined, preferred_element_type=jnp.float32)
    query = (proj[:, :local] + bias_q).astype(jnp.bfloat16)
    keys = proj[:, local : 2 * local].astype(jnp.bfloat16)
    values = (proj[:, 2 * local :] + bias_v).astype(jnp.bfloat16)

    def per_clip(value):
        return value.reshape(clips, cap, heads, HD)

    def forward_clip(inputs):
        query_clip, keys_clip, values_clip, length = inputs
        raw = masked_scores(query_clip, keys_clip, length, positions, scale)
        top = jnp.max(raw, -1, keepdims=True)
        lse = top + jnp.log(jnp.sum(jnp.exp(raw - top), -1, keepdims=True))
        probs = jnp.exp(raw - lse).astype(jnp.bfloat16)
        context_clip = jnp.einsum(
            "hqk,khe->qhe", probs, values_clip, preferred_element_type=jnp.float32
        )
        return (context_clip.astype(jnp.bfloat16), lse)

    context_all, lse_all = lax.map(
        forward_clip, (per_clip(query), per_clip(keys), per_clip(values), lengths)
    )
    context = context_all.reshape(rows, local)
    attended = lax.psum(
        jnp.dot(context, w_out, preferred_element_type=jnp.float32).astype(jnp.bfloat16), "tensor"
    ).astype(jnp.float32)
    middle = source + attended + bias_out
    normed2, rstd2, pre2 = layer_norm(middle, gain2, shift2)
    act2 = pre2.astype(jnp.bfloat16)
    pre = jnp.dot(act2, w_up, preferred_element_type=jnp.float32) + bias_up
    hidden_f, slope = gelu_pair(pre)
    hidden = hidden_f.astype(jnp.bfloat16)
    branch = lax.psum(
        jnp.dot(hidden, w_down, preferred_element_type=jnp.float32).astype(jnp.bfloat16), "tensor"
    ).astype(jnp.float32)
    mixed = jnp.where(valid, middle + branch + bias_down, 0.0).astype(jnp.bfloat16)
    upstream = jnp.where(valid, grad_out.astype(jnp.float32), 0.0)
    upstream_b = upstream.astype(jnp.bfloat16)
    g_down_bias = jnp.sum(upstream, 0)
    g_down = contract_first(hidden, upstream_b)
    d_pre = contract_last(upstream_b, w_down) * slope
    g_up_bias = jnp.sum(d_pre, 0)
    d_pre_b = d_pre.astype(jnp.bfloat16)
    g_up = contract_first(act2, d_pre_b)
    d_act2 = lax.psum(contract_last(d_pre_b, w_up).astype(jnp.bfloat16), "tensor").astype(
        jnp.float32
    )
    g_gain2 = jnp.sum(d_act2 * normed2, 0)
    g_shift2 = jnp.sum(d_act2, 0)
    d_middle = upstream + layer_norm_back(d_act2, normed2, rstd2, gain2)
    g_out_bias = jnp.sum(d_middle, 0)
    d_middle_b = d_middle.astype(jnp.bfloat16)
    g_out = contract_first(context, d_middle_b)
    d_context = contract_last(d_middle_b, w_out).astype(jnp.bfloat16)

    def backward_clip(inputs):
        query_clip, keys_clip, values_clip, context_clip, dcontext_clip, lse, length = inputs
        raw = masked_scores(query_clip, keys_clip, length, positions, scale)
        probs_f = jnp.exp(raw - lse)
        probs = probs_f.astype(jnp.bfloat16)
        d_probs = jnp.einsum(
            "qhe,khe->hqk", dcontext_clip, values_clip, preferred_element_type=jnp.float32
        )
        delta = jnp.sum(dcontext_clip.astype(jnp.float32) * context_clip.astype(jnp.float32), -1).T[
            :, :, None
        ]
        d_scores = (probs_f * (d_probs - delta) * scale).astype(jnp.bfloat16)
        d_query_clip = jnp.einsum(
            "hqk,khe->qhe", d_scores, keys_clip, preferred_element_type=jnp.float32
        )
        d_keys_clip = jnp.einsum(
            "hqk,qhe->khe", d_scores, query_clip, preferred_element_type=jnp.float32
        )
        d_values_clip = jnp.einsum(
            "hqk,qhe->khe", probs, dcontext_clip, preferred_element_type=jnp.float32
        )
        return (d_query_clip, d_keys_clip, d_values_clip)

    d_query, d_keys, d_values = lax.map(
        backward_clip,
        (
            per_clip(query),
            per_clip(keys),
            per_clip(values),
            context_all,
            per_clip(d_context),
            lse_all,
            lengths,
        ),
    )
    d_query = d_query.reshape(rows, local)
    d_keys = d_keys.reshape(rows, local)
    d_values = d_values.reshape(rows, local)
    g_bias_q = jnp.sum(d_query, 0)
    g_bias_v = jnp.sum(d_values, 0)
    stacked = jnp.concatenate(
        [d_query.astype(jnp.bfloat16), d_keys.astype(jnp.bfloat16), d_values.astype(jnp.bfloat16)],
        1,
    )
    g_qkv = contract_first(act1, stacked).reshape(width, 3, local)
    d_act1 = lax.psum(contract_last(stacked, joined).astype(jnp.bfloat16), "tensor").astype(
        jnp.float32
    )
    g_gain1 = jnp.sum(d_act1 * normed1, 0)
    g_shift1 = jnp.sum(d_act1, 0)
    d_tokens = jnp.where(valid, d_middle + layer_norm_back(d_act1, normed1, rstd1, gain1), 0.0)
    (
        g_qkv,
        g_bias_q,
        g_bias_v,
        g_out,
        g_out_bias,
        g_up,
        g_up_bias,
        g_down,
        g_down_bias,
        g_gain1,
        g_shift1,
        g_gain2,
        g_shift2,
    ) = (
        lax.psum(g_qkv.astype(jnp.bfloat16), "dp").astype(jnp.float32),
        lax.psum(g_bias_q.astype(jnp.bfloat16), "dp").astype(jnp.float32),
        lax.psum(g_bias_v.astype(jnp.bfloat16), "dp").astype(jnp.float32),
        lax.psum(g_out.astype(jnp.bfloat16), "dp").astype(jnp.float32),
        lax.psum(g_out_bias.astype(jnp.bfloat16), "dp").astype(jnp.float32),
        lax.psum(g_up.astype(jnp.bfloat16), "dp").astype(jnp.float32),
        lax.psum(g_up_bias.astype(jnp.bfloat16), "dp").astype(jnp.float32),
        lax.psum(g_down.astype(jnp.bfloat16), "dp").astype(jnp.float32),
        lax.psum(g_down_bias.astype(jnp.bfloat16), "dp").astype(jnp.float32),
        lax.psum(g_gain1.astype(jnp.bfloat16), "dp").astype(jnp.float32),
        lax.psum(g_shift1.astype(jnp.bfloat16), "dp").astype(jnp.float32),
        lax.psum(g_gain2.astype(jnp.bfloat16), "dp").astype(jnp.float32),
        lax.psum(g_shift2.astype(jnp.bfloat16), "dp").astype(jnp.float32),
    )
    return (
        mixed,
        d_tokens,
        g_qkv,
        g_bias_q,
        g_bias_v,
        g_out,
        g_out_bias,
        g_up,
        g_up_bias,
        g_down,
        g_down_bias,
        g_gain1,
        g_shift1,
        g_gain2,
        g_shift2,
    )


MESH = pl.DeviceIdType.MESH
DMA = pltpu.SemaphoreType.DMA
ANY = pl.BlockSpec(memory_space=pl.ANY)
VMEM = pl.BlockSpec(memory_space=pltpu.VMEM)
SMEM = pl.BlockSpec(memory_space=pltpu.SMEM)
BLOCKS = (96, 80, 112)
BQ = 256
BK = 256


def cost(us):
    return pl.CostEstimate(flops=int(us * 1e9), bytes_accessed=int(us * 3e6), transcendentals=0)


def coords():
    dp = lax.axis_index("dp")
    t = lax.axis_index("tensor")
    return dp // 2, dp % 2, t // 2, t % 2


def device(z, y, x, c):
    return (z * 2 + y, x * 2 + c)


def greet(peers):
    barrier = pltpu.get_barrier_semaphore()
    for peer in peers:
        pl.semaphore_signal(barrier, inc=1, device_id=peer, device_id_type=MESH)
    pl.semaphore_wait(barrier, len(peers))


def greet_grid():
    z, y, x, c = coords()
    barrier = pltpu.get_barrier_semaphore()

    def signal(peer):
        pl.semaphore_signal(barrier, inc=1, device_id=peer, device_id_type=MESH)

    @pl.when(z > 0)
    def _():
        signal(device(z - 1, y, x, c))

    @pl.when(z < 3)
    def _():
        signal(device(z + 1, y, x, c))

    signal(device(z, 1 - y, x, c))
    signal(device(z, y, 1 - x, c))
    signal(device(z, y, x, 1 - c))

    pl.semaphore_wait(barrier, 3 + jnp.minimum(z, 1) + jnp.minimum(3 - z, 1))


GATHER_SEMS = [DMA, DMA((4,)), DMA((4,)), DMA((4,)), DMA((8,)), DMA((16,)), DMA((32,))]


def gather_steps(x_refs, o_refs, sems, work=None, ahead=None):
    z, y, x, c = coords()
    n = len(GATHER_SEMS)
    arrays = [(a, o) + tuple(sems[n * i : n * i + n]) for i, (a, o) in enumerate(zip(x_refs, o_refs))]

    def block(z, y, x, c):
        return (z * 2 + y) * 4 + x * 2 + c

    ux, uy = x + (1 - c) * (1 - 2 * x), y + c * (1 - 2 * y)
    vx, vy = x + c * (1 - 2 * x), y + (1 - c) * (1 - 2 * y)
    own = block(z, y, x, c)
    core = device(z, y, x, 1 - c)

    def rows(array, b):
        size = array[0].shape[0]
        return array[1].at[pl.ds(pl.multiple_of(b * size, size), size)]

    def copy(array, b, kind, i, peer):
        return pltpu.make_async_remote_copy(
            src_ref=rows(array, b),
            dst_ref=rows(array, b),
            send_sem=array[kind].at[i],
            recv_sem=array[8].at[b],
            device_id=peer,
            device_id_type=MESH,
        )

    def send(b, kind, i, peer, first=False):
        for array in arrays:
            if first:
                pltpu.make_async_remote_copy(
                    src_ref=array[0],
                    dst_ref=rows(array, b),
                    send_sem=array[kind].at[i],
                    recv_sem=array[8].at[b],
                    device_id=peer,
                    device_id_type=MESH,
                ).start()
            else:
                copy(array, b, kind, i, peer).start()

    def arrived(b):
        for array in arrays:
            copy(array, b, 7, 0, core).wait_recv()

    right, left = device(z + 1, y, x, c), device(z - 1, y, x, c)
    u, v = device(z, uy, ux, c), device(z, vy, vx, c)
    locals_ = [pltpu.make_async_copy(a[0], rows(a, own), a[2]) for a in arrays]

    @pl.when(z < 3)
    def _():
        send(own, 3, z, right, True)

    @pl.when(z > 0)
    def _():
        send(own, 4, z, left, True)

    send(own, 5, z, u, True)
    send(own, 6, z, v, True)
    send(own, 7, z, core, True)
    for local in locals_:
        local.start()

    def near(step):
        def from_low(low):
            return jnp.where((low == 1) & (step < 2), 1 - step, step)

        return jnp.where(z < 2, from_low(z), 3 - from_low(3 - z))

    def got_line(at):
        b = block(at, y, x, c)
        arrived(b)

        @pl.when((at < z) & (z < 3))
        def _():
            send(b, 3, at, right)

        @pl.when((at > z) & (z > 0))
        def _():
            send(b, 4, at, left)

        send(b, 5, at, u)
        send(b, 6, at, v)
        send(b, 7, at, core)

    def got_u(at):
        b = block(at, uy, ux, c)
        arrived(b)
        send(b, 6, 4 + at, v)
        send(b, 7, 4 + at, core)

    def got_v(at):
        b = block(at, vy, vx, c)
        arrived(b)
        send(b, 7, 8 + at, core)

    def got_uv(at):
        b = block(at, 1 - y, 1 - x, c)
        arrived(b)
        send(b, 7, 12 + at, core)

    def meanwhile(step):
        if ahead is not None:
            ahead(step)

    def around(event, distance):
        for side in (-1, 1) if distance else (0,):
            at = z + side * distance
            pl.when((at >= 0) & (at < 4))(functools.partial(event, at))

    for distance in range(1, 4):
        around(got_line, distance)
        meanwhile(2 * distance - 2)
        around(got_u, distance - 1)
        meanwhile(2 * distance - 1)
    around(got_u, 3)
    meanwhile(6)
    for local in locals_:
        local.wait()

    @pl.loop(0, 4)
    def _(step):
        at = near(step)
        got_v(at)
        meanwhile(7 + 3 * step)
        got_uv(at)
        meanwhile(8 + 3 * step)

        @pl.loop(0, 4)
        def _(i):
            arrived(at * 8 + i * 2 + 1 - c)

        meanwhile(9 + 3 * step)

        if work is not None:
            work(at)

    def sent(kind, i):
        for array in arrays:
            copy(array, own, kind, i, core).wait_send()

    @pl.loop(0, 16)
    def _(i):
        sent(7, i)

    @pl.loop(0, 8)
    def _(i):
        sent(6, i)

    @pl.loop(0, 4)
    def _(i):
        sent(5, i)

        @pl.when((i <= z) & (z < 3))
        def _():
            sent(3, i)

        @pl.when((i >= z) & (z > 0))
        def _():
            sent(4, i)


def table_kernel(x_ref, o_ref, send_sem, recv_sem):
    me = lax.axis_index("dp")
    t = lax.axis_index("tensor")
    peers = [(lax.rem(me + s, 8), t) for s in range(1, 8)]
    greet(peers)
    o_ref[me] = x_ref[...]
    copies = [
        pltpu.make_async_remote_copy(
            src_ref=x_ref,
            dst_ref=o_ref.at[me],
            send_sem=send_sem.at[s],
            recv_sem=recv_sem.at[s],
            device_id=peer,
            device_id_type=MESH,
        )
        for s, peer in enumerate(peers)
    ]
    for copy in copies:
        copy.start()
    for copy in copies:
        copy.wait()


def gather_table(value, cid):
    tile = jnp.broadcast_to(value.reshape(1, 1), (8, 128))
    out = pl.pallas_call(
        table_kernel,
        out_shape=jax.ShapeDtypeStruct((8, 8, 128), value.dtype),
        in_specs=[VMEM],
        out_specs=VMEM,
        scratch_shapes=[DMA((7,)), DMA((7,))],
        compiler_params=pltpu.CompilerParams(collective_id=cid, has_side_effects=True),
        name="table",
    )(tile)
    return out[:, 0, 0]


def pieces_kernel(size, table_ref, clip_ref, x_ref, u_ref, xo_ref, uo_ref, offset_ref, length_ref, held, sems):
    t = lax.axis_index("tensor")
    dp = lax.axis_index("dp")
    cap = x_ref.shape[0]
    loads = [
        pltpu.make_async_copy(src, held.at[i, pl.ds(size, cap)], sems.at[i])
        for i, src in enumerate((x_ref, u_ref))
    ]
    for load in loads:
        load.start()
    lengths = []
    for s in range(8):
        clip = table_ref[s]
        lengths.append(jnp.where(clip >= 0, clip_ref[jnp.maximum(clip, 0)], 0))
    offset = length = 0
    for s in range(8):
        before = 0
        for o in range(8):
            if o != s:
                ahead = lengths[o] >= lengths[s] if o < s else lengths[o] > lengths[s]
                before += jnp.where(ahead, (lengths[o] + 15) // 16 * 16, 0)
        offset_ref[s] = before
        length_ref[s] = lengths[s]
        offset = jnp.where(dp == s, before, offset)
        length = jnp.where(dp == s, lengths[s], length)
    offset_ref[8] = offset
    length_ref[8] = length
    for i in (0, 1):
        held[i, 0:size, :] = jnp.zeros((size, held.shape[2]), held.dtype)
        held[i, size + cap :, :] = jnp.zeros((size, held.shape[2]), held.dtype)
    for i, out in enumerate((xo_ref, uo_ref)):
        loads[i].wait()

        @pl.loop(0, 8)
        def _(b):
            first = (b * 4 + t) * size - offset + size
            first = pl.multiple_of(jnp.clip(first, 0, cap + size), 16)
            row = lax.broadcasted_iota(jnp.int32, (size, 1), 0) + first - size
            value = held[i, pl.ds(first, size), :].astype(jnp.float32)
            value = jnp.where((row >= 0) & (row < length), value, 0.0)
            out[b] = value.astype(jnp.bfloat16)


def take_pieces(x, u, table, clip_len, size):
    cap, width = x.shape
    shape = jax.ShapeDtypeStruct((8, size, width), jnp.bfloat16)
    ints = jax.ShapeDtypeStruct((9,), jnp.int32)
    return pl.pallas_call(
        functools.partial(pieces_kernel, size),
        out_shape=(shape, shape, ints, ints),
        in_specs=[SMEM, SMEM, ANY, ANY],
        out_specs=(VMEM, VMEM, SMEM, SMEM),
        scratch_shapes=[pltpu.VMEM((2, cap + 2 * size, width), jnp.bfloat16), DMA((2,))],
        compiler_params=pltpu.CompilerParams(vmem_limit_bytes=60 << 20),
        name="pieces",
    )(table, clip_len, x, u)


def pack_kernel(
    p_ref,
    wt_ref,
    bias_ref,
    vec_ref,
    own,
    act_ref,
    k_ref,
    vt_ref,
    qt_ref,
    x_all,
    acc,
    y_out,
    y_in,
    r_out,
    r_in,
    l_out,
    l_in,
    ys,
    yr,
    rs,
    rr,
    ls,
    lr,
    *gather_sems,
):
    z, y, x, c = coords()
    size = own.shape[0]
    local = k_ref.shape[1]
    greet_grid()

    def piece(zp, yp):
        return p_ref[zp * 2 + yp].astype(jnp.float32)

    def project(at):
        @pl.loop(0, 8)
        def _(i):
            r = pl.ds(pl.multiple_of(at * 8 * size + i * size, size), size)
            _, _, pre = layer_norm(x_all[r, :].astype(jnp.float32), vec_ref[0:1, :], vec_ref[1:2, :])
            act_ref[r, :] = pre.astype(jnp.bfloat16)

        r = pl.ds(pl.multiple_of(at * 8 * size, 8 * size), 8 * size)
        k_ref[r, :] = dot_nt(act_ref[r, :], wt_ref[local : 2 * local, :]).astype(jnp.bfloat16)
        vt = dot_nt(wt_ref[2 * local :, :], act_ref[r, :]) + bias_ref[2 * local :, :]
        vt_ref[:, r] = vt.astype(jnp.bfloat16)

        @pl.when(at == z)
        def _():
            qt = dot_nt(wt_ref[:local, :], act_ref[r, :]) + bias_ref[:local, :]
            qt_ref[...] = qt.astype(jnp.bfloat16) * jnp.bfloat16(HD**-0.5)

    def y_copy(i):
        return pltpu.make_async_remote_copy(
            src_ref=y_out.at[i],
            dst_ref=y_in.at[i],
            send_sem=ys.at[i],
            recv_sem=yr.at[i],
            device_id=device(z, 1 - y, x, c),
            device_id_type=MESH,
        )

    def r_copy(i):
        return pltpu.make_async_remote_copy(
            src_ref=r_out.at[i],
            dst_ref=r_in.at[i],
            send_sem=rs.at[i],
            recv_sem=rr.at[i],
            device_id=device(z + 1, y, x, c),
            device_id_type=MESH,
        )

    def l_copy(i):
        return pltpu.make_async_remote_copy(
            src_ref=l_out.at[i],
            dst_ref=l_in.at[i],
            send_sem=ls.at[i],
            recv_sem=lr.at[i],
            device_id=device(z - 1, y, x, c),
            device_id_type=MESH,
        )

    def add(ref, copy, i):
        copy(i).wait_recv()
        acc[...] += ref[i].astype(jnp.float32)

    def flow(zp, yp, first):
        i = zp * 2 + yp

        @pl.when(z < zp)
        def _():
            first()

            @pl.when(z > 0)
            def _():
                add(r_in, r_copy, i)

            r_out[i] = acc[...].astype(jnp.bfloat16)
            r_copy(i).start()

        @pl.when(z > zp)
        def _():
            first()

            @pl.when(z < 3)
            def _():
                add(l_in, l_copy, i)

            l_out[i] = acc[...].astype(jnp.bfloat16)
            l_copy(i).start()

    def land(yp):
        @pl.when(z > 0)
        def _():
            add(r_in, r_copy, z * 2 + yp)

        @pl.when(z < 3)
        def _():
            add(l_in, l_copy, z * 2 + yp)

    low = z < 2
    order = [
        jnp.where(low, 3, 0),
        jnp.where(low, 2, 1),
        jnp.where(low, 1 - z, 5 - z),
    ]

    @pl.when(c == 0)
    def _():
        for zp in order + [z]:
            y_out[zp] = piece(zp, 1 - y).astype(jnp.bfloat16)
            y_copy(zp).start()
        for zp in order:

            def first(zp=zp):
                acc[...] = piece(zp, y)
                add(y_in, y_copy, zp)

            flow(zp, y, first)
        acc[...] = piece(z, y)
        add(y_in, y_copy, z)
        land(y)
        own[...] = acc[...].astype(jnp.bfloat16)
        for zp in range(4):
            y_copy(zp).wait_send()

    @pl.when(c == 1)
    def _():
        for zp in order:
            for yp in (0, 1):

                def first(zp=zp, yp=yp):
                    acc[...] = piece(zp, yp)

                flow(zp, yp, first)
        acc[...] = piece(z, 1 - y)
        land(1 - y)
        y_out[0] = acc[...].astype(jnp.bfloat16)
        y_copy(0).start()
        acc[...] = piece(z, y)
        land(y)
        add(y_in, y_copy, 0)
        own[...] = acc[...].astype(jnp.bfloat16)
        y_copy(0).wait_send()

    for zp in range(4):
        for yp in (0, 1):
            used = (c == 1) | (y == yp)

            @pl.when(used & (z < zp))
            def _(i=zp * 2 + yp):
                r_copy(i).wait_send()

            @pl.when(used & (z > zp))
            def _(i=zp * 2 + yp):
                l_copy(i).wait_send()

    gather_steps([own], [x_all], gather_sems, project)


def pack_gather(parts, wt, bias, rows8, cid):
    _, size, width = parts.shape
    bf16 = jnp.bfloat16
    rows = 32 * size
    local = wt.shape[0] // 3
    slots = pltpu.VMEM((8, size, width), bf16)
    quarter = pltpu.VMEM((4, size, width), bf16)
    return pl.pallas_call(
        pack_kernel,
        out_shape=(
            jax.ShapeDtypeStruct((size, width), bf16),
            jax.ShapeDtypeStruct((rows, width), bf16),
            jax.ShapeDtypeStruct((rows, local), bf16),
            jax.ShapeDtypeStruct((local, rows), bf16),
            jax.ShapeDtypeStruct((local, 8 * size), bf16),
        ),
        in_specs=[VMEM] * 4,
        out_specs=[VMEM] * 5,
        scratch_shapes=[
            pltpu.VMEM((rows, width), bf16),
            pltpu.VMEM((size, width), jnp.float32),
            quarter,
            quarter,
            slots,
            slots,
            slots,
            slots,
            DMA((4,)),
            DMA((4,)),
            DMA((8,)),
            DMA((8,)),
            DMA((8,)),
            DMA((8,)),
        ]
        + GATHER_SEMS,
        compiler_params=pltpu.CompilerParams(
            collective_id=cid, has_side_effects=True, vmem_limit_bytes=60 << 20
        ),
        cost_estimate=cost(90),
        name="pack_gather",
    )(parts, wt, bias[:, None], rows8)


def share_start(p_ref, landed, sends, send_sem, recv_sem):
    z, y, x, c = coords()

    def to_core(i):
        return pltpu.make_async_remote_copy(
            src_ref=p_ref.at[i * 2 + 1 - c],
            dst_ref=landed.at[i],
            send_sem=send_sem.at[i],
            recv_sem=recv_sem.at[i],
            device_id=device(z, y, x, 1 - c),
            device_id_type=MESH,
        )

    to_chip = pltpu.make_async_remote_copy(
        src_ref=sends,
        dst_ref=landed.at[2],
        send_sem=send_sem.at[2],
        recv_sem=recv_sem.at[2],
        device_id=device(z, y, 1 - x, c),
        device_id_type=MESH,
    )
    for i in (1 - x, x):
        to_core(i).start()
    return p_ref, landed, sends, to_core, to_chip


def share_pass(share):
    p_ref, landed, sends, to_core, to_chip = share
    _, _, x, c = coords()
    to_core(1 - x).wait_recv()
    total = p_ref[(1 - x) * 2 + c].astype(jnp.float32) + landed[1 - x].astype(jnp.float32)
    sends[...] = total.astype(jnp.bfloat16)
    to_chip.start()


def share_sum(share):
    p_ref, landed, sends, to_core, to_chip = share
    _, _, x, c = coords()
    to_core(x).wait_recv()
    total = p_ref[x * 2 + c].astype(jnp.float32) + landed[x].astype(jnp.float32)
    to_chip.wait_recv()
    total += landed[2].astype(jnp.float32)
    for i in (0, 1):
        to_core(i).wait_send()
    to_chip.wait_send()
    return total


def share_scratch(size, width):
    bf16 = jnp.bfloat16
    return [pltpu.VMEM((3, size, width), bf16), pltpu.VMEM((size, width), bf16), DMA((3,)), DMA((3,))]


def load_all(sources, targets, sems):
    copies = [
        pltpu.make_async_copy(a, b, sems.at[i]) for i, (a, b) in enumerate(zip(sources, targets))
    ]
    for copy in copies:
        copy.start()
    return copies


def products(units, early):
    total = sum(count for _, count in units)
    each = (total - early + 9) // 10

    def run(job):
        before = 0
        for unit, count in units:
            pl.when((job >= before) & (job < before + count))(functools.partial(unit, job - before))
            before += count

    def now():
        pl.loop(0, early)(run)

    def ahead(step):
        @pl.when(step < 10)
        def _():
            pl.loop(0, each)(lambda i: run(early + step * each + i))

    return now, ahead


def outer_unit(a, b, out, tall, wide):
    across = b.shape[1] // wide

    def unit(job):
        n = pl.ds(pl.multiple_of(lax.rem(job, across) * wide, 128), wide)
        if tall == out.shape[0]:
            out[:, n] = dot_tn(a[:, :tall], b[:, n]).astype(out.dtype)
        else:
            m = pl.ds(pl.multiple_of(job // across * tall, 128), tall)
            out[m, n] = dot_tn(a[:, m], b[:, n]).astype(out.dtype)

    return unit, out.shape[0] // tall * across


def first_kernel(
    p_ref, x_ref, rows_ref, wt_ref, wbias_ref, act_ref,
    mid_ref, o_ref, qkt_ref, v_ref,
    own, act, load_sem, landed, sends, ss, sr, *sems,
):
    (load,) = load_all((act_ref,), (act,), load_sem)
    greet_grid()
    share = share_start(p_ref, landed, sends, ss, sr)
    share_pass(share)
    local = v_ref.shape[1]
    chunk = act.shape[0] // 4
    load.wait()

    def project(job):
        r = pl.ds(pl.multiple_of(job // 3 * chunk, 128), chunk)
        kind = lax.rem(job, 3)

        @pl.when(kind == 0)
        def _():
            qt = dot_nt(wt_ref[:local, :], act[r, :]) + wbias_ref[:local, :]
            qkt_ref[:local, r] = qt.astype(jnp.bfloat16) * jnp.bfloat16(HD**-0.5)

        @pl.when(kind == 1)
        def _():
            kt = dot_nt(wt_ref[local : 2 * local, :], act[r, :])
            qkt_ref[local:, r] = kt.astype(jnp.bfloat16)

        @pl.when(kind == 2)
        def _():
            v = dot_nt(act[r, :], wt_ref[2 * local :, :]) + wbias_ref[2 * local :, :].T
            v_ref[r, :] = v.astype(jnp.bfloat16)

    project(0)
    project(1)
    middle = x_ref[...].astype(jnp.float32) + share_sum(share) + rows_ref[4:5, :]
    mid_ref[...] = middle
    _, _, pre = layer_norm(middle, rows_ref[2:3, :], rows_ref[3:4, :])
    own[...] = pre.astype(jnp.bfloat16)

    def ahead(step):
        pl.when(step < 10)(functools.partial(project, step + 2))

    gather_steps([own], [o_ref], sems, ahead=ahead)


def first_exchange(part, source, rows8, wt, bias, act1, cid):
    size, width = source.shape
    rows = 32 * size
    local = wt.shape[0] // 3
    bf16 = jnp.bfloat16
    return pl.pallas_call(
        first_kernel,
        out_shape=(
            jax.ShapeDtypeStruct((size, width), jnp.float32),
            jax.ShapeDtypeStruct((rows, width), bf16),
            jax.ShapeDtypeStruct((2 * local, rows), bf16),
            jax.ShapeDtypeStruct((rows, local), bf16),
        ),
        in_specs=[VMEM] * 5 + [ANY],
        out_specs=[VMEM, ANY, VMEM, VMEM],
        scratch_shapes=[pltpu.VMEM((size, width), bf16), pltpu.VMEM((rows, width), bf16), DMA((1,))]
        + share_scratch(size, width)
        + GATHER_SEMS,
        compiler_params=pltpu.CompilerParams(
            collective_id=cid, has_side_effects=True, vmem_limit_bytes=60 << 20
        ),
        cost_estimate=cost(60),
        name="first_exchange",
    )(
        part.reshape(4, size, width), source, rows8, wt, bias[:, None], act1,
    )


def second_kernel(
    p_ref, b_ref, mid_ref, up_ref, rows_ref, wout_ref, act_ref, hid_ref, dpre_ref, upall_ref,
    dmid_ref, mixed_ref, vec_ref, o_ref, gup_ref, gdown_ref, dctx_ref,
    own, landed, sends, ss, sr, landed2, sends2, ss2, sr2, some, act, hid, dpre, upall, load_sem, *sems,
):
    loads = load_all((act_ref, dpre_ref, hid_ref, upall_ref), (act, dpre, hid, upall), load_sem)
    greet_grid()
    share = share_start(p_ref, landed, sends, ss, sr)
    branch_share = share_start(b_ref, landed2, sends2, ss2, sr2)
    share_pass(share)
    share_pass(branch_share)
    now, work = products(
        [outer_unit(act, dpre, gup_ref, 256, 1280), outer_unit(hid, upall, gdown_ref, 256, 1280)], 2
    )
    for load in loads:
        load.wait()
    now()
    grad = share_sum(share)
    middle = mid_ref[...]
    normed, rstd, _ = layer_norm(middle, 1.0, 0.0)
    d_middle = up_ref[...].astype(jnp.float32) + layer_norm_back(grad, normed, rstd, rows_ref[2:3, :])
    own[...] = d_middle.astype(jnp.bfloat16)
    dmid_ref[...] = d_middle
    vec_ref[...] = jnp.concatenate(
        [
            jnp.sum(grad * normed, 0, keepdims=True),
            jnp.sum(grad, 0, keepdims=True),
            jnp.sum(up_ref[...].astype(jnp.float32), 0, keepdims=True),
            jnp.sum(d_middle, 0, keepdims=True),
            jnp.zeros((4, grad.shape[1]), jnp.float32),
        ],
        0,
    )
    def ahead(step):
        @pl.when(step == 0)
        def _():
            branch = share_sum(branch_share)
            mixed_ref[...] = (mid_ref[...] + branch + rows_ref[5:6, :]).astype(jnp.bfloat16)

        work(step)

    size = own.shape[0]

    def context_grad(at):
        r = pl.ds(pl.multiple_of(at * 8 * size, 8 * size), 8 * size)
        pltpu.sync_copy(o_ref.at[r], some)
        dctx_ref[:, r] = dot_nt(wout_ref[...], some[...]).astype(jnp.bfloat16)

    gather_steps([own], [o_ref], sems, context_grad, ahead)


def second_exchange(part, branch, middle, upstream, rows8, w_out, act2, hidden, d_pre, up_all, cid):
    size, width = middle.shape
    f32, bf16 = jnp.float32, jnp.bfloat16
    rows, inner = hidden.shape
    return pl.pallas_call(
        second_kernel,
        out_shape=(
            jax.ShapeDtypeStruct((size, width), f32),
            jax.ShapeDtypeStruct((size, width), bf16),
            jax.ShapeDtypeStruct((8, width), f32),
            jax.ShapeDtypeStruct((rows, width), bf16),
            jax.ShapeDtypeStruct((width, inner), bf16),
            jax.ShapeDtypeStruct((inner, width), bf16),
            jax.ShapeDtypeStruct((w_out.shape[0], rows), bf16),
        ),
        in_specs=[VMEM] * 6 + [ANY] * 4,
        out_specs=[VMEM, VMEM, VMEM, ANY, VMEM, VMEM, VMEM],
        scratch_shapes=[pltpu.VMEM((size, width), bf16)]
        + share_scratch(size, width) * 2
        + [pltpu.VMEM((8 * size, width), bf16)]
        + [pltpu.VMEM((rows, n), bf16) for n in (width, inner, inner, width)]
        + [DMA((4,))]
        + GATHER_SEMS,
        compiler_params=pltpu.CompilerParams(
            collective_id=cid, has_side_effects=True, vmem_limit_bytes=60 << 20
        ),
        cost_estimate=cost(80),
        name="second_exchange",
    )(
        part.reshape(4, size, width), branch.reshape(4, size, width), middle, upstream,
        rows8, w_out, act2, hidden, d_pre, up_all,
    )


def third_kernel(
    p_ref, x_ref, dmid_ref, rows_ref, vec_ref, act_ref, dt_ref, ctx_ref, dmall_ref,
    o_ref, vo_ref, gqkv_ref, gout_ref,
    own, vec, landed, sends, ss, sr, act, dt, ctx, dmall, load_sem, *sems,
):
    loads = load_all((act_ref, dt_ref, ctx_ref, dmall_ref), (act, dt, ctx, dmall), load_sem)
    greet_grid()
    share = share_start(p_ref, landed, sends, ss, sr)
    share_pass(share)
    part = dt.shape[0] // 3

    def project(job):
        k = pl.ds(pl.multiple_of(job // 2 * part, 64), part)
        m = pl.ds(pl.multiple_of(lax.rem(job, 2) * 640, 128), 640)
        gqkv_ref[k, m] = dot_nn(dt[k, :], act[:, m]).astype(jnp.bfloat16)

    now, work = products([(project, 6), outer_unit(ctx, dmall, gout_ref, part, 640)], 2)
    for load in loads:
        load.wait()
    now()
    grad = share_sum(share)
    normed, rstd, _ = layer_norm(x_ref[...].astype(jnp.float32), 1.0, 0.0)
    own[...] = (dmid_ref[...] + layer_norm_back(grad, normed, rstd, rows_ref[0:1, :])).astype(jnp.bfloat16)
    vec[...] = jnp.concatenate(
        [
            vec_ref[0:4, :],
            jnp.sum(grad * normed, 0, keepdims=True),
            jnp.sum(grad, 0, keepdims=True),
            jnp.zeros((2, grad.shape[1]), jnp.float32),
        ],
        0,
    )
    gather_steps([own, vec], [o_ref, vo_ref], sems, ahead=work)


def third_exchange(part, source, d_middle, rows8, vec, act1, d_qkv, context, d_middle_all, cid):
    size, width = d_middle.shape
    f32, bf16 = jnp.float32, jnp.bfloat16
    rows = act1.shape[0]
    total = d_qkv.shape[0]
    return pl.pallas_call(
        third_kernel,
        out_shape=(
            jax.ShapeDtypeStruct((rows, width), bf16),
            jax.ShapeDtypeStruct((256, width), f32),
            jax.ShapeDtypeStruct((total, width), bf16),
            jax.ShapeDtypeStruct((total // 3, width), bf16),
        ),
        in_specs=[VMEM] * 5 + [ANY] * 4,
        out_specs=[ANY, ANY, VMEM, VMEM],
        scratch_shapes=[pltpu.VMEM((size, width), bf16), pltpu.VMEM((8, width), f32)]
        + share_scratch(size, width)
        + [pltpu.VMEM(a.shape, bf16) for a in (act1, d_qkv, context, d_middle_all)]
        + [DMA((4,))]
        + GATHER_SEMS * 2,
        compiler_params=pltpu.CompilerParams(
            collective_id=cid, has_side_effects=True, vmem_limit_bytes=60 << 20
        ),
        cost_estimate=cost(60),
        name="third_exchange",
    )(
        part.reshape(4, size, width), source, d_middle, rows8, vec,
        act1, d_qkv, context, d_middle_all,
    )


def dot_nt(a, b):
    return lax.dot_general(a, b, (((1,), (1,)), ((), ())), preferred_element_type=jnp.float32)


def dot_nn(a, b):
    return lax.dot_general(a, b, (((1,), (0,)), ((), ())), preferred_element_type=jnp.float32)


def dot_tn(a, b):
    return lax.dot_general(a, b, (((0,), (0,)), ((), ())), preferred_element_type=jnp.float32)


def spans(offset_ref, length_ref, first, count):
    row = lax.broadcasted_iota(jnp.int32, (1, count), 1) + first
    start = jnp.zeros((1, count), jnp.int32)
    end = jnp.zeros((1, count), jnp.int32)
    low, high = 1 << 20, 0
    for i in range(8):
        a = offset_ref[i]
        b = a + length_ref[i]
        inside = (row >= a) & (row < b)
        start = jnp.where(inside, a, start)
        end = jnp.where(inside, b, end)
        used = (a < first + count) & (b > first) & (b > a)
        low = jnp.where(used, jnp.minimum(low, a // BK), low)
        high = jnp.where(used, jnp.maximum(high, (b + BK - 1) // BK), high)
    return start, end, low, high


def attend_kernel(heads, offset_ref, length_ref, qt_ref, k_ref, vt_ref, sent_ref, m_s, l_s, acc_s, win):
    mine = sent_ref.shape[0]
    rows = win.shape[0]
    local = heads * HD
    span = range(heads)
    dp = lax.axis_index("dp")
    skip = lax.rem(dp, 2) * (mine % 128)
    first = dp * mine - skip
    window = pl.ds(pl.multiple_of(lax.rem(dp, 2) * mine - skip, 128), rows)
    start, end, low, high = spans(offset_ref, length_ref, first, rows)
    m_s[...] = jnp.full_like(m_s, NEG)
    l_s[...] = jnp.zeros_like(l_s)
    acc_s[...] = jnp.zeros_like(acc_s)
    q = [qt_ref[h * HD : (h + 1) * HD, window] for h in span]

    def body(kb, carry):
        k0 = pl.multiple_of(kb * BK, BK)
        key = lax.broadcasted_iota(jnp.int32, (BK, rows), 0) + k0
        mask = (key >= start) & (key < end)
        s = [
            jnp.where(
                mask,
                dot_nn(k_ref[pl.ds(k0, BK), h * HD : (h + 1) * HD], q[h]),
                NEG,
            )
            for h in span
        ]
        p, a = [], []
        for h in span:
            old = m_s[h]
            new = jnp.maximum(old, jnp.max(s[h], 0, keepdims=True))
            e = jnp.exp(s[h] - new)
            scale = jnp.exp(old - new)
            l_s[h] = scale * l_s[h] + jnp.sum(e, 0, keepdims=True)
            m_s[h] = new
            p.append(e.astype(jnp.bfloat16))
            a.append(scale)
        for h in span:
            vt = vt_ref[h * HD : (h + 1) * HD, pl.ds(k0, BK)]
            acc_s[h] = a[h] * acc_s[h] + dot_nn(vt, p[h])
        return carry

    lax.fori_loop(low, high, body, 0)
    parts = [[], [], []]
    for h in span:
        total = l_s[h]
        total = jnp.where(total == 0.0, 1.0, total)
        rest = m_s[h] + jnp.log(total)
        for part in parts:
            part.append(rest.astype(jnp.bfloat16).astype(jnp.float32))
            rest = rest - part[-1]
        out = acc_s[h] * (1.0 / total)
        win[:, h * HD : (h + 1) * HD] = out.T
    blank = [jnp.zeros((win.shape[1] - local - 3 * heads, rows), jnp.float32)]
    win[:, local:] = jnp.concatenate(parts[0] + parts[1] + parts[2] + blank, 0).T
    sent_ref[...] = win[pl.ds(pl.multiple_of(skip, 16), mine), :].astype(jnp.bfloat16)


def whole(a):
    return pl.BlockSpec(a.shape, lambda i, *_: (0,) * len(a.shape), pipeline_mode=pl.Buffered(1))


def attend(qt, k, vt, offsets, lengths, heads):
    mine = k.shape[0] // 8
    rows = (mine + mine % 128 + 127) // 128 * 128
    local = heads * HD
    wide = (local + 3 * heads + 127) // 128 * 128
    row = pltpu.VMEM((heads, 1, rows), jnp.float32)
    return pl.pallas_call(
        functools.partial(attend_kernel, heads),
        out_shape=jax.ShapeDtypeStruct((mine, wide), jnp.bfloat16),
        in_specs=[SMEM, SMEM, VMEM, VMEM, VMEM],
        out_specs=VMEM,
        scratch_shapes=[
            row,
            row,
            pltpu.VMEM((heads, HD, rows), jnp.float32),
            pltpu.VMEM((rows, wide), jnp.float32),
        ],
        compiler_params=pltpu.CompilerParams(vmem_limit_bytes=60 << 20),
        cost_estimate=cost(10),
        name="attend",
    )(offsets, lengths, qt, k, vt)


def attend_back_kernel(
    heads, offset_ref, length_ref, k_ref, v_ref, qkt_ref, dot_ref, sent_ref, up_ref, down_ref,
    d_ref, sum_ref, up_out, down_out, dk_s, dv_s, dq_s
):
    i = pl.program_id(0)
    local = heads * HD
    span = range(heads)
    sl = [slice(h * HD, (h + 1) * HD) for h in span]
    at_q = pl.ds(pl.multiple_of(i * BQ, BQ), BQ)

    @pl.when(i == 0)
    def _():
        dk_s[...] = jnp.zeros_like(dk_s)
        dv_s[...] = jnp.zeros_like(dv_s)
        sum_ref[...] = jnp.zeros_like(sum_ref)

    start, end, low, high = spans(offset_ref, length_ref, i * BQ, BQ)
    dq_s[...] = jnp.zeros_like(dq_s)
    sent = sent_ref[at_q, :].astype(jnp.float32).T
    lse, delta = [], []
    for h in span:
        a = local + h
        lse.append(
            sent[a : a + 1] + sent[a + heads : a + heads + 1] + sent[a + 2 * heads : a + 2 * heads + 1]
        )
        delta.append(jnp.sum(dot_ref[sl[h], at_q].astype(jnp.float32) * sent[sl[h]], 0, keepdims=True))

    def blocks(first, count):
        keys = []
        for n in range(count):
            at_k = pl.ds(pl.multiple_of((first + n) * BK, BK), BK)
            key = lax.broadcasted_iota(jnp.int32, (BK, BQ), 0) + (first + n) * BK
            keys.append((at_k, (key >= start) & (key < end)))
        jobs = [(at_k, mask, h) for at_k, mask in keys for h in span]

        def products(at_k, mask, h):
            s = dot_nn(k_ref[at_k, sl[h]], qkt_ref[sl[h], at_q])
            dp = dot_nn(v_ref[at_k, sl[h]], dot_ref[sl[h], at_q])
            return s, dp

        def scores(at_k, mask, h, s, dp):
            p = jnp.exp(jnp.where(mask, s, NEG) - lse[h])
            ds = (p * (dp - delta[h])).astype(jnp.bfloat16)
            return p.astype(jnp.bfloat16), ds

        def gradients(at_k, mask, h, p, ds):
            dv_s[h, :, at_k] += dot_nt(dot_ref[sl[h], at_q], p)
            dk_s[h, :, at_k] += dot_nt(qkt_ref[sl[h], at_q], ds)
            dq_s[h] += dot_nn(qkt_ref[local + h * HD : local + (h + 1) * HD, at_k], ds)

        now = products(*jobs[0])
        held = None
        for n, job in enumerate(jobs):
            later = products(*jobs[n + 1]) if n + 1 < len(jobs) else None
            done = scores(*job, *now)
            if held is not None:
                gradients(*jobs[n - 1], *held)
            held, now = done, later
        gradients(*jobs[-1], *held)

    def pair(n, carry):
        blocks(low + 2 * n, 2)
        return carry

    pairs = jnp.maximum(high - low, 0) // 2
    lax.fori_loop(0, pairs, pair, 0)

    @pl.when(low + 2 * pairs < high)
    def _():
        blocks(low + 2 * pairs, 1)

    for src, dst in ((up_ref, up_out), (down_ref, down_out)):
        dst[...] = src[...].astype(jnp.float32)
    for h in span:
        dq = dq_s[h] * HD**-0.5
        d_ref[sl[h], at_q] = dq.astype(jnp.bfloat16)
        sum_ref[sl[h], :] += dq[:, :128] + dq[:, 128:]

    @pl.when(i == pl.num_programs(0) - 1)
    def _():
        for h in span:
            d_ref[local + h * HD : local + (h + 1) * HD, :] = dk_s[h].astype(jnp.bfloat16)
            d_ref[2 * local + h * HD : 2 * local + (h + 1) * HD, :] = dv_s[h].astype(jnp.bfloat16)
            total = dv_s[h, :, 0:128]
            for n in range(1, dv_s.shape[2] // 128):
                total += dv_s[h, :, n * 128 : (n + 1) * 128]
            sum_ref[local + h * HD : local + (h + 1) * HD, :] = total


def attend_back(k, v, qkt, dot, sent, offsets, lengths, up, down, heads):
    rows = k.shape[0]
    local = heads * HD
    tall = pltpu.VMEM((heads, HD, rows), jnp.float32)

    def const(shape):
        return pl.BlockSpec(shape, lambda i, *_: (0, 0), pipeline_mode=pl.Buffered(1))

    strips = [
        pl.BlockSpec((a.shape[0] // 10, a.shape[1]), lambda i, *_: (jnp.minimum(i, 9), 0))
        for a in (up, down)
    ]
    return pl.pallas_call(
        functools.partial(attend_back_kernel, heads),
        out_shape=(
            jax.ShapeDtypeStruct((3 * local, rows), jnp.bfloat16),
            jax.ShapeDtypeStruct((2 * local, 128), jnp.float32),
            jax.ShapeDtypeStruct(up.shape, jnp.float32),
            jax.ShapeDtypeStruct(down.shape, jnp.float32),
        ),
        grid_spec=pltpu.PrefetchScalarGridSpec(
            num_scalar_prefetch=2,
            grid=(rows // BQ,),
            in_specs=[whole(a) for a in (k, v, qkt, dot, sent)] + strips,
            out_specs=[const((3 * local, rows)), const((2 * local, 128))] + strips,
            scratch_shapes=[tall, tall, pltpu.VMEM((heads, HD, BQ), jnp.float32)],
        ),
        compiler_params=pltpu.CompilerParams(vmem_limit_bytes=60 << 20),
        cost_estimate=cost(60),
        name="attend_back",
    )(offsets, lengths, k, v, qkt, dot, sent, up, down)


def finish_kernel(
    offset_ref, length_ref, m_ref, d_ref, qkv_ref, out_ref, mo_ref, do_ref, qkv_out, out_out, m, d, sems
):
    i = pl.program_id(0)
    size = mo_ref.shape[0]
    rows = m_ref.shape[0]
    offset = offset_ref[8]
    length = length_ref[8]

    def first(n):
        return pl.multiple_of(jnp.minimum(offset + n * size, rows - size), 16)

    def loads(n):
        return [
            pltpu.make_async_copy(
                src.at[pl.ds(first(n), size)], dst.at[n, pl.ds(0, size)], sems.at[k, n]
            )
            for k, (src, dst) in enumerate(((m_ref, m), (d_ref, d)))
        ]

    @pl.when(i == 0)
    def _():
        for n in range(m.shape[0]):
            for load in loads(n):
                load.start()

    qkv_out[...] = qkv_ref[...].astype(jnp.float32)
    out_out[...] = out_ref[...].astype(jnp.float32)
    shift = pl.multiple_of(jnp.minimum(offset + i * size - first(i), size), 16)
    row = lax.broadcasted_iota(jnp.int32, (size, 1), 0) + i * size
    for load, src, dst in zip(loads(i), (m, d), (mo_ref, do_ref)):
        load.wait()
        value = jnp.where(row < length, src[i, pl.ds(shift, size), :].astype(jnp.float32), 0.0)
        dst[...] = value.astype(dst.dtype)


def finish(offsets, lengths, mixed, d_tokens, g_qkv, g_out, cap):
    width = mixed.shape[1]
    steps = cap // 128
    held = pltpu.VMEM((steps, 256, width), jnp.bfloat16)
    f32 = jnp.float32

    def strip(count):
        return pl.BlockSpec((count, width), lambda i: (i, 0))

    short = pl.BlockSpec((g_out.shape[0] // 10, width), lambda i: (jnp.minimum(i, 9), 0))
    tall = strip(g_qkv.shape[0] // steps)
    return pl.pallas_call(
        finish_kernel,
        grid=(steps,),
        out_shape=(
            jax.ShapeDtypeStruct((cap, width), jnp.bfloat16),
            jax.ShapeDtypeStruct((cap, width), f32),
            jax.ShapeDtypeStruct(g_qkv.shape, f32),
            jax.ShapeDtypeStruct(g_out.shape, f32),
        ),
        in_specs=[SMEM, SMEM, ANY, ANY, tall, short],
        out_specs=[strip(128), strip(128), tall, short],
        scratch_shapes=[held, held, DMA((2, steps))],
        compiler_params=pltpu.CompilerParams(vmem_limit_bytes=60 << 20),
        name="finish",
    )(offsets, lengths, mixed, d_tokens, g_qkv, g_out)


def packed_step(size, cids, table, args):
    (
        tokens, clip_len, _, w_qkv, bias_q, bias_v, w_out, bias_out, w_up, bias_up, w_down, bias_down,
        gain1, shift1, gain2, shift2, grad_out,
    ) = args
    f32, bf16 = jnp.float32, jnp.bfloat16
    cap, width = tokens.shape
    local = w_qkv.shape[2]
    heads = local // HD
    rows = 32 * size
    mine = 4 * size
    dp = lax.axis_index("dp")
    pack_id, first_id, second_id, third_id = cids

    def own(value):
        return lax.dynamic_slice_in_dim(value, dp * mine, mine, 0)

    x_parts, up_parts, offsets, lengths = take_pieces(tokens, grad_out, table, clip_len, size)
    wt = w_qkv.transpose(1, 2, 0).reshape(3 * local, width)
    bias = jnp.concatenate([bias_q, jnp.zeros_like(bias_q), bias_v])
    spare = jnp.zeros_like(gain1)
    rows8 = jnp.stack([gain1, shift1, gain2, shift2, bias_out, bias_down, spare, spare])
    source, act1, k, vt, qt = pack_gather(x_parts, wt, bias, rows8, pack_id)
    up_own = lax.psum_scatter(up_parts, "dp", scatter_dimension=0, tiled=True)
    up_own, source = lax.optimization_barrier((up_own, source))
    up_all = lax.all_gather(up_own.reshape(size, width), ("dp", "tensor"), tiled=True)

    sent_own = attend(qt, k, vt, offsets, lengths, heads)
    part = jnp.dot(sent_own[:, :local], w_out, preferred_element_type=f32).astype(bf16)
    sent = lax.all_gather(sent_own, "dp", tiled=True)
    middle, act2, qkt, v = first_exchange(
        part, source, rows8, wt, bias, act1, first_id
    )

    pre = jnp.dot(act2, w_up, preferred_element_type=f32) + bias_up
    hidden_f, slope = gelu_pair(pre)
    hidden = hidden_f.astype(bf16)
    d_pre = contract_last(up_all, w_down) * slope
    g_up_bias = jnp.sum(d_pre, 0)
    d_pre_b = d_pre.astype(bf16)
    d_part = contract_last(own(d_pre_b), w_up).astype(bf16)
    branch = jnp.dot(own(hidden), w_down, preferred_element_type=f32).astype(bf16)
    d_middle, mixed, vec, d_middle_b, g_up, g_down, d_context = second_exchange(
        d_part, branch, middle, up_own.reshape(size, width), rows8, w_out,
        act2, hidden, d_pre_b, up_all, second_id,
    )
    mixed_all = lax.all_gather(mixed, ("dp", "tensor"), tiled=True)
    d_qkv, column, g_up, g_down = attend_back(
        k, v, qkt, d_context, sent, offsets, lengths, g_up, g_down, heads
    )
    column = jnp.sum(column, 1)
    d_own = lax.dynamic_slice_in_dim(d_qkv, dp * mine, mine, 1)
    d_act1 = jnp.einsum("kr,kd->rd", d_own, wt, preferred_element_type=f32).astype(bf16)
    d_tokens_all, vectors_all, g_qkv, g_out = third_exchange(
        d_act1, source, d_middle, rows8, vec, act1, d_qkv, sent, d_middle_b, third_id
    )
    sums = jnp.sum(vectors_all.reshape(32, 8, width), 0)
    mixed, d_tokens, g_qkv, g_out = finish(
        offsets, lengths, mixed_all, d_tokens_all, g_qkv, g_out, cap
    )
    g_qkv = g_qkv.reshape(3, local, width).transpose(2, 0, 1)

    return (
        mixed,
        d_tokens,
        g_qkv,
        column[:local],
        column[local:],
        g_out,
        sums[3],
        g_up,
        g_up_bias,
        g_down,
        sums[2],
        sums[4],
        sums[5],
        sums[0],
        sums[1],
    )


def packed(*args):
    clip_len, slot_clip = args[1], args[2]

    def padded(value):
        return (value + 15) // 16 * 16

    need = jnp.sum(padded(clip_len))
    table = gather_table(slot_clip[0], 0)
    branches = [
        functools.partial(packed_step, size, [1 + 4 * n + i for i in range(4)])
        for n, size in enumerate(BLOCKS)
    ]
    rank = sum((need > 32 * size).astype(jnp.int32) for size in sorted(BLOCKS))
    pick = jnp.array([BLOCKS.index(size) for size in sorted(BLOCKS)] + [len(BLOCKS)], jnp.int32)[rank]

    def fallback(table, args):
        return plain(*args)

    return lax.switch(pick, branches + [fallback], table, args)


def solution(mesh):
    placed = (
        P("dp", None),
        P(),
        P("dp"),
        P(None, None, "tensor"),
        P("tensor"),
        P("tensor"),
        P("tensor", None),
        P(),
        P(None, "tensor"),
        P("tensor"),
        P("tensor", None),
        P(),
        P(),
        P(),
        P(),
        P(),
        P("dp", None),
    )
    fits = mesh.shape["dp"] == 8 and mesh.shape["tensor"] == 4
    return jax.shard_map(
        packed if fits else plain,
        mesh=mesh,
        in_specs=placed,
        out_specs=(
            P("dp", None),
            P("dp", None),
            P(None, None, "tensor"),
            P("tensor"),
            P("tensor"),
            P("tensor", None),
            P(),
            P(None, "tensor"),
            P("tensor"),
            P("tensor", None),
            P(),
            P(),
            P(),
            P(),
            P(),
        ),
        check_vma=False,
    )
```

```python
import functools

import jax
import jax.numpy as jnp
from jax import lax
from jax.experimental import pallas as pl
from jax.experimental.pallas import tpu as pltpu
from jax.sharding import PartitionSpec as P

HD = 64


EPS = 1e-05
NEG = -1e30
HALF_ROOT = 0.7071067811865476
INV_ROOT_TAU = 0.3989422804014327


def layer_norm(value, gain, shift):
    center = value - jnp.mean(value, -1, keepdims=True)
    rstd = lax.rsqrt(jnp.mean(center * center, -1, keepdims=True) + EPS)
    normed = center * rstd
    return (normed, rstd, normed * gain + shift)


def layer_norm_back(grad, normed, rstd, gain):
    scaled = grad * gain
    return rstd * (
        scaled
        - jnp.mean(scaled, -1, keepdims=True)
        - normed * jnp.mean(scaled * normed, -1, keepdims=True)
    )


def gelu_pair(value):
    cdf = 0.5 * (1.0 + jax.scipy.special.erf(value * HALF_ROOT))
    return (value * cdf, cdf + value * jnp.exp(-0.5 * value * value) * INV_ROOT_TAU)


def contract_first(left, right):
    return lax.dot_general(
        left, right, (((0,), (0,)), ((), ())), preferred_element_type=jnp.float32
    )


def contract_last(left, right):
    return lax.dot_general(
        left, right, (((1,), (1,)), ((), ())), preferred_element_type=jnp.float32
    )


def masked_scores(query_clip, keys_clip, length, positions, scale):
    raw = (
        jnp.einsum("qhe,khe->hqk", query_clip, keys_clip, preferred_element_type=jnp.float32)
        * scale
    )
    return jnp.where((positions < length)[None, None, :], raw, NEG)


def plain(
    tokens,
    clip_len,
    slot_clip,
    w_qkv,
    bias_q,
    bias_v,
    w_out,
    bias_out,
    w_up,
    bias_up,
    w_down,
    bias_down,
    gain1,
    shift1,
    gain2,
    shift2,
    grad_out,
):
    rows, width = tokens.shape
    clips = slot_clip.shape[0]
    cap = rows // clips
    local = w_qkv.shape[2]
    heads = local // HD
    scale = HD ** (-0.5)
    positions = jnp.arange(cap, dtype=jnp.int32)
    match = slot_clip[:, None] == jnp.arange(clip_len.shape[0], dtype=jnp.int32)[None, :]
    lengths = jnp.sum(jnp.where(match, clip_len[None, :], 0), 1)
    valid = (positions[None, :] < lengths[:, None]).reshape(rows, 1)
    source = tokens.astype(jnp.float32)
    normed1, rstd1, pre1 = layer_norm(source, gain1, shift1)
    act1 = pre1.astype(jnp.bfloat16)
    joined = w_qkv.reshape(width, 3 * local)
    proj = jnp.dot(act1, joined, preferred_element_type=jnp.float32)
    query = (proj[:, :local] + bias_q).astype(jnp.bfloat16)
    keys = proj[:, local : 2 * local].astype(jnp.bfloat16)
    values = (proj[:, 2 * local :] + bias_v).astype(jnp.bfloat16)

    def per_clip(value):
        return value.reshape(clips, cap, heads, HD)

    def forward_clip(inputs):
        query_clip, keys_clip, values_clip, length = inputs
        raw = masked_scores(query_clip, keys_clip, length, positions, scale)
        top = jnp.max(raw, -1, keepdims=True)
        lse = top + jnp.log(jnp.sum(jnp.exp(raw - top), -1, keepdims=True))
        probs = jnp.exp(raw - lse).astype(jnp.bfloat16)
        context_clip = jnp.einsum(
            "hqk,khe->qhe", probs, values_clip, preferred_element_type=jnp.float32
        )
        return (context_clip.astype(jnp.bfloat16), lse)

    context_all, lse_all = lax.map(
        forward_clip, (per_clip(query), per_clip(keys), per_clip(values), lengths)
    )
    context = context_all.reshape(rows, local)
    attended = lax.psum(
        jnp.dot(context, w_out, preferred_element_type=jnp.float32).astype(jnp.bfloat16), "tensor"
    ).astype(jnp.float32)
    middle = source + attended + bias_out
    normed2, rstd2, pre2 = layer_norm(middle, gain2, shift2)
    act2 = pre2.astype(jnp.bfloat16)
    pre = jnp.dot(act2, w_up, preferred_element_type=jnp.float32) + bias_up
    hidden_f, slope = gelu_pair(pre)
    hidden = hidden_f.astype(jnp.bfloat16)
    branch = lax.psum(
        jnp.dot(hidden, w_down, preferred_element_type=jnp.float32).astype(jnp.bfloat16), "tensor"
    ).astype(jnp.float32)
    mixed = jnp.where(valid, middle + branch + bias_down, 0.0).astype(jnp.bfloat16)
    upstream = jnp.where(valid, grad_out.astype(jnp.float32), 0.0)
    upstream_b = upstream.astype(jnp.bfloat16)
    g_down_bias = jnp.sum(upstream, 0)
    g_down = contract_first(hidden, upstream_b)
    d_pre = contract_last(upstream_b, w_down) * slope
    g_up_bias = jnp.sum(d_pre, 0)
    d_pre_b = d_pre.astype(jnp.bfloat16)
    g_up = contract_first(act2, d_pre_b)
    d_act2 = lax.psum(contract_last(d_pre_b, w_up).astype(jnp.bfloat16), "tensor").astype(
        jnp.float32
    )
    g_gain2 = jnp.sum(d_act2 * normed2, 0)
    g_shift2 = jnp.sum(d_act2, 0)
    d_middle = upstream + layer_norm_back(d_act2, normed2, rstd2, gain2)
    g_out_bias = jnp.sum(d_middle, 0)
    d_middle_b = d_middle.astype(jnp.bfloat16)
    g_out = contract_first(context, d_middle_b)
    d_context = contract_last(d_middle_b, w_out).astype(jnp.bfloat16)

    def backward_clip(inputs):
        query_clip, keys_clip, values_clip, context_clip, dcontext_clip, lse, length = inputs
        raw = masked_scores(query_clip, keys_clip, length, positions, scale)
        probs_f = jnp.exp(raw - lse)
        probs = probs_f.astype(jnp.bfloat16)
        d_probs = jnp.einsum(
            "qhe,khe->hqk", dcontext_clip, values_clip, preferred_element_type=jnp.float32
        )
        delta = jnp.sum(dcontext_clip.astype(jnp.float32) * context_clip.astype(jnp.float32), -1).T[
            :, :, None
        ]
        d_scores = (probs_f * (d_probs - delta) * scale).astype(jnp.bfloat16)
        d_query_clip = jnp.einsum(
            "hqk,khe->qhe", d_scores, keys_clip, preferred_element_type=jnp.float32
        )
        d_keys_clip = jnp.einsum(
            "hqk,qhe->khe", d_scores, query_clip, preferred_element_type=jnp.float32
        )
        d_values_clip = jnp.einsum(
            "hqk,qhe->khe", probs, dcontext_clip, preferred_element_type=jnp.float32
        )
        return (d_query_clip, d_keys_clip, d_values_clip)

    d_query, d_keys, d_values = lax.map(
        backward_clip,
        (
            per_clip(query),
            per_clip(keys),
            per_clip(values),
            context_all,
            per_clip(d_context),
            lse_all,
            lengths,
        ),
    )
    d_query = d_query.reshape(rows, local)
    d_keys = d_keys.reshape(rows, local)
    d_values = d_values.reshape(rows, local)
    g_bias_q = jnp.sum(d_query, 0)
    g_bias_v = jnp.sum(d_values, 0)
    stacked = jnp.concatenate(
        [d_query.astype(jnp.bfloat16), d_keys.astype(jnp.bfloat16), d_values.astype(jnp.bfloat16)],
        1,
    )
    g_qkv = contract_first(act1, stacked).reshape(width, 3, local)
    d_act1 = lax.psum(contract_last(stacked, joined).astype(jnp.bfloat16), "tensor").astype(
        jnp.float32
    )
    g_gain1 = jnp.sum(d_act1 * normed1, 0)
    g_shift1 = jnp.sum(d_act1, 0)
    d_tokens = jnp.where(valid, d_middle + layer_norm_back(d_act1, normed1, rstd1, gain1), 0.0)
    (
        g_qkv,
        g_bias_q,
        g_bias_v,
        g_out,
        g_out_bias,
        g_up,
        g_up_bias,
        g_down,
        g_down_bias,
        g_gain1,
        g_shift1,
        g_gain2,
        g_shift2,
    ) = (
        lax.psum(g_qkv.astype(jnp.bfloat16), "dp").astype(jnp.float32),
        lax.psum(g_bias_q.astype(jnp.bfloat16), "dp").astype(jnp.float32),
        lax.psum(g_bias_v.astype(jnp.bfloat16), "dp").astype(jnp.float32),
        lax.psum(g_out.astype(jnp.bfloat16), "dp").astype(jnp.float32),
        lax.psum(g_out_bias.astype(jnp.bfloat16), "dp").astype(jnp.float32),
        lax.psum(g_up.astype(jnp.bfloat16), "dp").astype(jnp.float32),
        lax.psum(g_up_bias.astype(jnp.bfloat16), "dp").astype(jnp.float32),
        lax.psum(g_down.astype(jnp.bfloat16), "dp").astype(jnp.float32),
        lax.psum(g_down_bias.astype(jnp.bfloat16), "dp").astype(jnp.float32),
        lax.psum(g_gain1.astype(jnp.bfloat16), "dp").astype(jnp.float32),
        lax.psum(g_shift1.astype(jnp.bfloat16), "dp").astype(jnp.float32),
        lax.psum(g_gain2.astype(jnp.bfloat16), "dp").astype(jnp.float32),
        lax.psum(g_shift2.astype(jnp.bfloat16), "dp").astype(jnp.float32),
    )
    return (
        mixed,
        d_tokens,
        g_qkv,
        g_bias_q,
        g_bias_v,
        g_out,
        g_out_bias,
        g_up,
        g_up_bias,
        g_down,
        g_down_bias,
        g_gain1,
        g_shift1,
        g_gain2,
        g_shift2,
    )


MESH = pl.DeviceIdType.MESH
DMA = pltpu.SemaphoreType.DMA
ANY = pl.BlockSpec(memory_space=pl.ANY)
VMEM = pl.BlockSpec(memory_space=pltpu.VMEM)
SMEM = pl.BlockSpec(memory_space=pltpu.SMEM)
BLOCKS = (96, 80, 112, 128)
BQ = 256
BK = 256


def cost(us):
    return pl.CostEstimate(flops=int(us * 1e9), bytes_accessed=int(us * 3e6), transcendentals=0)


def coords():
    dp = lax.axis_index("dp")
    t = lax.axis_index("tensor")
    return dp // 2, dp % 2, t // 2, t % 2


def device(z, y, x, c):
    return (z * 2 + y, x * 2 + c)


def greet(peers):
    barrier = pltpu.get_barrier_semaphore()
    for peer in peers:
        pl.semaphore_signal(barrier, inc=1, device_id=peer, device_id_type=MESH)
    pl.semaphore_wait(barrier, len(peers))


def greet_grid():
    z, y, x, c = coords()
    barrier = pltpu.get_barrier_semaphore()

    def signal(peer):
        pl.semaphore_signal(barrier, inc=1, device_id=peer, device_id_type=MESH)

    @pl.when(z > 0)
    def _():
        signal(device(z - 1, y, x, c))

    @pl.when(z < 3)
    def _():
        signal(device(z + 1, y, x, c))

    signal(device(z, 1 - y, x, c))
    signal(device(z, y, 1 - x, c))
    signal(device(z, y, x, 1 - c))

    pl.semaphore_wait(barrier, 3 + jnp.minimum(z, 1) + jnp.minimum(3 - z, 1))


GATHER_SEMS = [DMA, DMA((4,)), DMA((4,)), DMA((4,)), DMA((8,)), DMA((16,)), DMA((32,))]


def gather_steps(x_refs, o_refs, sems, work=None, ahead=None):
    z, y, x, c = coords()
    n = len(GATHER_SEMS)
    arrays = [(a, o) + tuple(sems[n * i : n * i + n]) for i, (a, o) in enumerate(zip(x_refs, o_refs))]

    def block(z, y, x, c):
        return (z * 2 + y) * 4 + x * 2 + c

    ux, uy = x + (1 - c) * (1 - 2 * x), y + c * (1 - 2 * y)
    vx, vy = x + c * (1 - 2 * x), y + (1 - c) * (1 - 2 * y)
    own = block(z, y, x, c)
    core = device(z, y, x, 1 - c)

    def rows(array, b):
        size = array[0].shape[0]
        return array[1].at[pl.ds(pl.multiple_of(b * size, size), size)]

    def copy(array, b, kind, i, peer):
        return pltpu.make_async_remote_copy(
            src_ref=rows(array, b),
            dst_ref=rows(array, b),
            send_sem=array[kind].at[i],
            recv_sem=array[8].at[b],
            device_id=peer,
            device_id_type=MESH,
        )

    def send(b, kind, i, peer, first=False):
        for array in arrays:
            if first:
                pltpu.make_async_remote_copy(
                    src_ref=array[0],
                    dst_ref=rows(array, b),
                    send_sem=array[kind].at[i],
                    recv_sem=array[8].at[b],
                    device_id=peer,
                    device_id_type=MESH,
                ).start()
            else:
                copy(array, b, kind, i, peer).start()

    def arrived(b):
        for array in arrays:
            copy(array, b, 7, 0, core).wait_recv()

    right, left = device(z + 1, y, x, c), device(z - 1, y, x, c)
    u, v = device(z, uy, ux, c), device(z, vy, vx, c)
    locals_ = [pltpu.make_async_copy(a[0], rows(a, own), a[2]) for a in arrays]

    @pl.when(z < 3)
    def _():
        send(own, 3, z, right, True)

    @pl.when(z > 0)
    def _():
        send(own, 4, z, left, True)

    send(own, 5, z, u, True)
    send(own, 6, z, v, True)
    send(own, 7, z, core, True)
    for local in locals_:
        local.start()

    def near(step):
        def from_low(low):
            return jnp.where((low == 1) & (step < 2), 1 - step, step)

        return jnp.where(z < 2, from_low(z), 3 - from_low(3 - z))

    def got_line(at):
        b = block(at, y, x, c)
        arrived(b)

        @pl.when((at < z) & (z < 3))
        def _():
            send(b, 3, at, right)

        @pl.when((at > z) & (z > 0))
        def _():
            send(b, 4, at, left)

        send(b, 5, at, u)
        send(b, 6, at, v)
        send(b, 7, at, core)

    def got_u(at):
        b = block(at, uy, ux, c)
        arrived(b)
        send(b, 6, 4 + at, v)
        send(b, 7, 4 + at, core)

    def got_v(at):
        b = block(at, vy, vx, c)
        arrived(b)
        send(b, 7, 8 + at, core)

    def got_uv(at):
        b = block(at, 1 - y, 1 - x, c)
        arrived(b)
        send(b, 7, 12 + at, core)

    def around(event, distance):
        for side in (-1, 1):
            at = z + side * distance
            here = (at >= 0) & (at < 4)
            if side == 1:
                here = here & (distance > 0)
            pl.when(here)(functools.partial(event, at))

    @pl.loop(0, 19)
    def _(step):
        line = (step < 6) & (lax.rem(step, 2) == 0)
        at = near(jnp.maximum(step - 7, 0) // 3)
        kind = lax.rem(step + 2, 3)

        @pl.when(line)
        def _():
            around(got_line, step // 2 + 1)

        @pl.when((step < 7) & jnp.logical_not(line))
        def _():
            around(got_u, step // 2)

        @pl.when((step >= 7) & (kind == 0))
        def _():
            got_v(at)

        @pl.when((step >= 7) & (kind == 1))
        def _():
            got_uv(at)

        @pl.when((step >= 7) & (kind == 2))
        def _():
            @pl.loop(0, 4)
            def _(i):
                arrived(at * 8 + i * 2 + 1 - c)

        @pl.when(step == 6)
        def _():
            for local in locals_:
                local.wait()

        if ahead is not None:
            ahead(step)
        if work is not None:
            pl.when((step >= 7) & (kind == 2))(functools.partial(work, at))

    def sent(kind, i):
        for array in arrays:
            copy(array, own, kind, i, core).wait_send()

    @pl.loop(0, 16)
    def _(i):
        sent(7, i)

    @pl.loop(0, 8)
    def _(i):
        sent(6, i)

    @pl.loop(0, 4)
    def _(i):
        sent(5, i)

        @pl.when((i <= z) & (z < 3))
        def _():
            sent(3, i)

        @pl.when((i >= z) & (z > 0))
        def _():
            sent(4, i)


def table_kernel(x_ref, o_ref, send_sem, recv_sem):
    me = lax.axis_index("dp")
    t = lax.axis_index("tensor")
    peers = [(lax.rem(me + s, 8), t) for s in range(1, 8)]
    greet(peers)
    o_ref[me] = x_ref[...]
    copies = [
        pltpu.make_async_remote_copy(
            src_ref=x_ref,
            dst_ref=o_ref.at[me],
            send_sem=send_sem.at[s],
            recv_sem=recv_sem.at[s],
            device_id=peer,
            device_id_type=MESH,
        )
        for s, peer in enumerate(peers)
    ]
    for copy in copies:
        copy.start()
    for copy in copies:
        copy.wait()


def gather_table(value, cid):
    tile = jnp.broadcast_to(value.reshape(1, 1), (8, 128))
    out = pl.pallas_call(
        table_kernel,
        out_shape=jax.ShapeDtypeStruct((8, 8, 128), value.dtype),
        in_specs=[VMEM],
        out_specs=VMEM,
        scratch_shapes=[DMA((7,)), DMA((7,))],
        compiler_params=pltpu.CompilerParams(collective_id=cid, has_side_effects=True),
        name="table",
    )(tile)
    return out[:, 0, 0]


def pieces_kernel(size, table_ref, clip_ref, x_ref, u_ref, xo_ref, uo_ref, offset_ref, length_ref, held, sems):
    t = lax.axis_index("tensor")
    dp = lax.axis_index("dp")
    cap = x_ref.shape[0]
    loads = [
        pltpu.make_async_copy(src, held.at[i, pl.ds(size, cap)], sems.at[i])
        for i, src in enumerate((x_ref, u_ref))
    ]
    for load in loads:
        load.start()
    lengths = []
    for s in range(8):
        clip = table_ref[s]
        lengths.append(jnp.where(clip >= 0, clip_ref[jnp.maximum(clip, 0)], 0))
    offset = length = 0
    for s in range(8):
        before = 0
        for o in range(8):
            if o != s:
                ahead = lengths[o] >= lengths[s] if o < s else lengths[o] > lengths[s]
                before += jnp.where(ahead, (lengths[o] + 15) // 16 * 16, 0)
        offset_ref[s] = before
        length_ref[s] = lengths[s]
        offset = jnp.where(dp == s, before, offset)
        length = jnp.where(dp == s, lengths[s], length)
    offset_ref[8] = offset
    length_ref[8] = length
    for i in (0, 1):
        held[i, 0:size, :] = jnp.zeros((size, held.shape[2]), held.dtype)
        held[i, size + cap :, :] = jnp.zeros((size, held.shape[2]), held.dtype)
    for i, out in enumerate((xo_ref, uo_ref)):
        loads[i].wait()

        @pl.loop(0, 8)
        def _(b):
            first = (b * 4 + t) * size - offset + size
            first = pl.multiple_of(jnp.clip(first, 0, cap + size), 16)
            row = lax.broadcasted_iota(jnp.int32, (size, 1), 0) + first - size
            value = held[i, pl.ds(first, size), :].astype(jnp.float32)
            value = jnp.where((row >= 0) & (row < length), value, 0.0)
            out[b] = value.astype(jnp.bfloat16)


def take_pieces(x, u, table, clip_len, size):
    cap, width = x.shape
    shape = jax.ShapeDtypeStruct((8, size, width), jnp.bfloat16)
    ints = jax.ShapeDtypeStruct((9,), jnp.int32)
    return pl.pallas_call(
        functools.partial(pieces_kernel, size),
        out_shape=(shape, shape, ints, ints),
        in_specs=[SMEM, SMEM, ANY, ANY],
        out_specs=(VMEM, VMEM, SMEM, SMEM),
        scratch_shapes=[pltpu.VMEM((2, cap + 2 * size, width), jnp.bfloat16), DMA((2,))],
        compiler_params=pltpu.CompilerParams(vmem_limit_bytes=60 << 20),
        name="pieces",
    )(table, clip_len, x, u)


def pack_kernel(
    p_ref,
    wt_ref,
    bias_ref,
    vec_ref,
    own,
    act_ref,
    k_ref,
    vt_ref,
    qt_ref,
    x_all,
    acc,
    y_out,
    y_in,
    r_out,
    r_in,
    l_out,
    l_in,
    ys,
    yr,
    rs,
    rr,
    ls,
    lr,
    *gather_sems,
):
    z, y, x, c = coords()
    size = own.shape[0]
    local = k_ref.shape[1]
    greet_grid()

    def piece(zp, yp):
        return p_ref[zp * 2 + yp].astype(jnp.float32)

    def project(at):
        @pl.loop(0, 8)
        def _(i):
            r = pl.ds(pl.multiple_of(at * 8 * size + i * size, size), size)
            _, _, pre = layer_norm(x_all[r, :].astype(jnp.float32), vec_ref[0:1, :], vec_ref[1:2, :])
            act_ref[r, :] = pre.astype(jnp.bfloat16)

        r = pl.ds(pl.multiple_of(at * 8 * size, 8 * size), 8 * size)
        k_ref[r, :] = dot_nt(act_ref[r, :], wt_ref[local : 2 * local, :]).astype(jnp.bfloat16)
        vt = dot_nt(wt_ref[2 * local :, :], act_ref[r, :]) + bias_ref[2 * local :, :]
        vt_ref[:, r] = vt.astype(jnp.bfloat16)

        @pl.when(at == z)
        def _():
            qt = dot_nt(wt_ref[:local, :], act_ref[r, :]) + bias_ref[:local, :]
            qt_ref[...] = qt.astype(jnp.bfloat16) * jnp.bfloat16(HD**-0.5)

    def y_copy(i):
        return pltpu.make_async_remote_copy(
            src_ref=y_out.at[i],
            dst_ref=y_in.at[i],
            send_sem=ys.at[i],
            recv_sem=yr.at[i],
            device_id=device(z, 1 - y, x, c),
            device_id_type=MESH,
        )

    def r_copy(i):
        return pltpu.make_async_remote_copy(
            src_ref=r_out.at[i],
            dst_ref=r_in.at[i],
            send_sem=rs.at[i],
            recv_sem=rr.at[i],
            device_id=device(z + 1, y, x, c),
            device_id_type=MESH,
        )

    def l_copy(i):
        return pltpu.make_async_remote_copy(
            src_ref=l_out.at[i],
            dst_ref=l_in.at[i],
            send_sem=ls.at[i],
            recv_sem=lr.at[i],
            device_id=device(z - 1, y, x, c),
            device_id_type=MESH,
        )

    def add(ref, copy, i):
        copy(i).wait_recv()
        acc[...] += ref[i].astype(jnp.float32)

    def flow(zp, yp, first):
        i = zp * 2 + yp

        @pl.when(z < zp)
        def _():
            first()

            @pl.when(z > 0)
            def _():
                add(r_in, r_copy, i)

            r_out[i] = acc[...].astype(jnp.bfloat16)
            r_copy(i).start()

        @pl.when(z > zp)
        def _():
            first()

            @pl.when(z < 3)
            def _():
                add(l_in, l_copy, i)

            l_out[i] = acc[...].astype(jnp.bfloat16)
            l_copy(i).start()

    def land(yp):
        @pl.when(z > 0)
        def _():
            add(r_in, r_copy, z * 2 + yp)

        @pl.when(z < 3)
        def _():
            add(l_in, l_copy, z * 2 + yp)

    low = z < 2
    order = [
        jnp.where(low, 3, 0),
        jnp.where(low, 2, 1),
        jnp.where(low, 1 - z, 5 - z),
    ]

    @pl.when(c == 0)
    def _():
        for zp in order + [z]:
            y_out[zp] = piece(zp, 1 - y).astype(jnp.bfloat16)
            y_copy(zp).start()
        for zp in order:

            def first(zp=zp):
                acc[...] = piece(zp, y)
                add(y_in, y_copy, zp)

            flow(zp, y, first)
        acc[...] = piece(z, y)
        add(y_in, y_copy, z)
        land(y)
        own[...] = acc[...].astype(jnp.bfloat16)
        for zp in range(4):
            y_copy(zp).wait_send()

    @pl.when(c == 1)
    def _():
        for zp in order:
            for yp in (0, 1):

                def first(zp=zp, yp=yp):
                    acc[...] = piece(zp, yp)

                flow(zp, yp, first)
        acc[...] = piece(z, 1 - y)
        land(1 - y)
        y_out[0] = acc[...].astype(jnp.bfloat16)
        y_copy(0).start()
        acc[...] = piece(z, y)
        land(y)
        add(y_in, y_copy, 0)
        own[...] = acc[...].astype(jnp.bfloat16)
        y_copy(0).wait_send()

    for zp in range(4):
        for yp in (0, 1):
            used = (c == 1) | (y == yp)

            @pl.when(used & (z < zp))
            def _(i=zp * 2 + yp):
                r_copy(i).wait_send()

            @pl.when(used & (z > zp))
            def _(i=zp * 2 + yp):
                l_copy(i).wait_send()

    gather_steps([own], [x_all], gather_sems, project)


def pack_gather(parts, wt, bias, rows8, cid):
    _, size, width = parts.shape
    bf16 = jnp.bfloat16
    rows = 32 * size
    local = wt.shape[0] // 3
    slots = pltpu.VMEM((8, size, width), bf16)
    quarter = pltpu.VMEM((4, size, width), bf16)
    return pl.pallas_call(
        pack_kernel,
        out_shape=(
            jax.ShapeDtypeStruct((size, width), bf16),
            jax.ShapeDtypeStruct((rows, width), bf16),
            jax.ShapeDtypeStruct((rows, local), bf16),
            jax.ShapeDtypeStruct((local, rows), bf16),
            jax.ShapeDtypeStruct((local, 8 * size), bf16),
        ),
        in_specs=[VMEM] * 4,
        out_specs=[VMEM] * 5,
        scratch_shapes=[
            pltpu.VMEM((rows, width), bf16),
            pltpu.VMEM((size, width), jnp.float32),
            quarter,
            quarter,
            slots,
            slots,
            slots,
            slots,
            DMA((4,)),
            DMA((4,)),
            DMA((8,)),
            DMA((8,)),
            DMA((8,)),
            DMA((8,)),
        ]
        + GATHER_SEMS,
        compiler_params=pltpu.CompilerParams(
            collective_id=cid, has_side_effects=True, vmem_limit_bytes=60 << 20
        ),
        cost_estimate=cost(90),
        name="pack_gather",
    )(parts, wt, bias[:, None], rows8)


def share_start(p_ref, landed, sends, send_sem, recv_sem):
    z, y, x, c = coords()

    def to_core(i):
        return pltpu.make_async_remote_copy(
            src_ref=p_ref.at[i * 2 + 1 - c],
            dst_ref=landed.at[i],
            send_sem=send_sem.at[i],
            recv_sem=recv_sem.at[i],
            device_id=device(z, y, x, 1 - c),
            device_id_type=MESH,
        )

    to_chip = pltpu.make_async_remote_copy(
        src_ref=sends,
        dst_ref=landed.at[2],
        send_sem=send_sem.at[2],
        recv_sem=recv_sem.at[2],
        device_id=device(z, y, 1 - x, c),
        device_id_type=MESH,
    )
    for i in (1 - x, x):
        to_core(i).start()
    return p_ref, landed, sends, to_core, to_chip


def share_pass(share):
    p_ref, landed, sends, to_core, to_chip = share
    _, _, x, c = coords()
    to_core(1 - x).wait_recv()
    total = p_ref[(1 - x) * 2 + c].astype(jnp.float32) + landed[1 - x].astype(jnp.float32)
    sends[...] = total.astype(jnp.bfloat16)
    to_chip.start()


def share_sum(share):
    p_ref, landed, sends, to_core, to_chip = share
    _, _, x, c = coords()
    to_core(x).wait_recv()
    total = p_ref[x * 2 + c].astype(jnp.float32) + landed[x].astype(jnp.float32)
    to_chip.wait_recv()
    total += landed[2].astype(jnp.float32)
    for i in (0, 1):
        to_core(i).wait_send()
    to_chip.wait_send()
    return total


def share_scratch(size, width):
    bf16 = jnp.bfloat16
    return [pltpu.VMEM((3, size, width), bf16), pltpu.VMEM((size, width), bf16), DMA((3,)), DMA((3,))]


def load_all(sources, targets, sems):
    copies = [
        pltpu.make_async_copy(a, b, sems.at[i]) for i, (a, b) in enumerate(zip(sources, targets))
    ]
    for copy in copies:
        copy.start()
    return copies


def products(units, early):
    total = sum(count for _, count in units)
    each = (total - early + 9) // 10

    def run(job):
        before = 0
        for unit, count in units:
            pl.when((job >= before) & (job < before + count))(functools.partial(unit, job - before))
            before += count

    def now():
        pl.loop(0, early)(run)

    def ahead(step):
        @pl.when(step < 10)
        def _():
            pl.loop(0, each)(lambda i: run(early + step * each + i))

    return now, ahead


def outer_unit(a, b, out, tall, wide):
    across = b.shape[1] // wide

    def unit(job):
        n = pl.ds(pl.multiple_of(lax.rem(job, across) * wide, 128), wide)
        if tall == out.shape[0]:
            out[:, n] = dot_tn(a[:, :tall], b[:, n]).astype(out.dtype)
        else:
            m = pl.ds(pl.multiple_of(job // across * tall, 128), tall)
            out[m, n] = dot_tn(a[:, m], b[:, n]).astype(out.dtype)

    return unit, out.shape[0] // tall * across


def first_kernel(
    p_ref, x_ref, rows_ref, wt_ref, wbias_ref, act_ref,
    mid_ref, o_ref, qkt_ref, v_ref,
    own, act, load_sem, landed, sends, ss, sr, *sems,
):
    (load,) = load_all((act_ref,), (act,), load_sem)
    greet_grid()
    share = share_start(p_ref, landed, sends, ss, sr)
    share_pass(share)
    local = v_ref.shape[1]
    chunk = act.shape[0] // 4
    load.wait()

    def project(job):
        r = pl.ds(pl.multiple_of(job // 3 * chunk, 128), chunk)
        kind = lax.rem(job, 3)

        @pl.when(kind == 0)
        def _():
            qt = dot_nt(wt_ref[:local, :], act[r, :]) + wbias_ref[:local, :]
            qkt_ref[:local, r] = qt.astype(jnp.bfloat16) * jnp.bfloat16(HD**-0.5)

        @pl.when(kind == 1)
        def _():
            kt = dot_nt(wt_ref[local : 2 * local, :], act[r, :])
            qkt_ref[local:, r] = kt.astype(jnp.bfloat16)

        @pl.when(kind == 2)
        def _():
            v = dot_nt(act[r, :], wt_ref[2 * local :, :]) + wbias_ref[2 * local :, :].T
            v_ref[r, :] = v.astype(jnp.bfloat16)

    pl.loop(0, 2)(project)
    middle = x_ref[...].astype(jnp.float32) + share_sum(share) + rows_ref[4:5, :]
    mid_ref[...] = middle
    _, _, pre = layer_norm(middle, rows_ref[2:3, :], rows_ref[3:4, :])
    own[...] = pre.astype(jnp.bfloat16)

    def ahead(step):
        pl.when(step < 10)(functools.partial(project, step + 2))

    gather_steps([own], [o_ref], sems, ahead=ahead)


def first_exchange(part, source, rows8, wt, bias, act1, cid):
    size, width = source.shape
    rows = 32 * size
    local = wt.shape[0] // 3
    bf16 = jnp.bfloat16
    return pl.pallas_call(
        first_kernel,
        out_shape=(
            jax.ShapeDtypeStruct((size, width), jnp.float32),
            jax.ShapeDtypeStruct((rows, width), bf16),
            jax.ShapeDtypeStruct((2 * local, rows), bf16),
            jax.ShapeDtypeStruct((rows, local), bf16),
        ),
        in_specs=[VMEM] * 5 + [ANY],
        out_specs=[VMEM, ANY, VMEM, VMEM],
        scratch_shapes=[pltpu.VMEM((size, width), bf16), pltpu.VMEM((rows, width), bf16), DMA((1,))]
        + share_scratch(size, width)
        + GATHER_SEMS,
        compiler_params=pltpu.CompilerParams(
            collective_id=cid, has_side_effects=True, vmem_limit_bytes=60 << 20
        ),
        cost_estimate=cost(60),
        name="first_exchange",
    )(
        part.reshape(4, size, width), source, rows8, wt, bias[:, None], act1,
    )


def second_kernel(
    mid_ref, up_ref, rows_ref, wout_ref, act_ref, hid_ref, dpre_ref, upall_ref, wup_ref, wdown_ref,
    dmid_ref, mixed_ref, vec_ref, o_ref, gup_ref, gdown_ref, dctx_ref,
    own, part, branch, landed, sends, ss, sr, landed2, sends2, ss2, sr2, some, act, hid, dpre, upall,
    load_sem, *sems,
):
    loads = load_all(
        (dpre_ref, wup_ref, hid_ref, wdown_ref, act_ref, upall_ref),
        (dpre, gup_ref, hid, gdown_ref, act, upall),
        load_sem,
    )
    greet_grid()
    size = own.shape[0]
    mine = pl.ds(pl.multiple_of(lax.axis_index("dp") * 4 * size, 64), 4 * size)
    loads[0].wait()
    loads[1].wait()
    part[...] = dot_nt(dpre[mine, :], gup_ref[...]).astype(jnp.bfloat16).reshape(part.shape)
    share = share_start(part, landed, sends, ss, sr)
    loads[2].wait()
    loads[3].wait()
    branch[...] = dot_nn(hid[mine, :], gdown_ref[...]).astype(jnp.bfloat16).reshape(branch.shape)
    branch_share = share_start(branch, landed2, sends2, ss2, sr2)
    share_pass(share)
    share_pass(branch_share)
    now, work = products(
        [outer_unit(act, dpre, gup_ref, 256, 1280), outer_unit(hid, upall, gdown_ref, 256, 1280)], 2
    )
    for load in loads[4:]:
        load.wait()
    now()
    grad = share_sum(share)
    middle = mid_ref[...]
    normed, rstd, _ = layer_norm(middle, 1.0, 0.0)
    d_middle = up_ref[...].astype(jnp.float32) + layer_norm_back(grad, normed, rstd, rows_ref[2:3, :])
    own[...] = d_middle.astype(jnp.bfloat16)
    dmid_ref[...] = d_middle
    vec_ref[...] = jnp.concatenate(
        [
            jnp.sum(grad * normed, 0, keepdims=True),
            jnp.sum(grad, 0, keepdims=True),
            jnp.sum(up_ref[...].astype(jnp.float32), 0, keepdims=True),
            jnp.sum(d_middle, 0, keepdims=True),
            jnp.zeros((4, grad.shape[1]), jnp.float32),
        ],
        0,
    )
    def ahead(step):
        @pl.when(step == 0)
        def _():
            total = share_sum(branch_share)
            mixed_ref[...] = (mid_ref[...] + total + rows_ref[5:6, :]).astype(jnp.bfloat16)

        work(step)

    count = some.shape[0]

    def context_grad(at):
        @pl.loop(0, 8 * size // count)
        def _(i):
            r = pl.ds(pl.multiple_of(at * 8 * size + i * count, 128), count)
            pltpu.sync_copy(o_ref.at[r], some)
            dctx_ref[:, r] = dot_nt(wout_ref[...], some[...]).astype(jnp.bfloat16)

    gather_steps([own], [o_ref], sems, context_grad, ahead)


def second_exchange(middle, upstream, rows8, w_out, act2, hidden, d_pre, up_all, w_up, w_down, cid):
    size, width = middle.shape
    f32, bf16 = jnp.float32, jnp.bfloat16
    rows, inner = hidden.shape
    block = pltpu.VMEM((4, size, width), bf16)
    return pl.pallas_call(
        second_kernel,
        out_shape=(
            jax.ShapeDtypeStruct((size, width), f32),
            jax.ShapeDtypeStruct((size, width), bf16),
            jax.ShapeDtypeStruct((8, width), f32),
            jax.ShapeDtypeStruct((rows, width), bf16),
            jax.ShapeDtypeStruct((width, inner), bf16),
            jax.ShapeDtypeStruct((inner, width), bf16),
            jax.ShapeDtypeStruct((w_out.shape[0], rows), bf16),
        ),
        in_specs=[VMEM] * 4 + [ANY] * 6,
        out_specs=[VMEM, VMEM, VMEM, ANY, VMEM, VMEM, VMEM],
        scratch_shapes=[pltpu.VMEM((size, width), bf16), block, block]
        + share_scratch(size, width) * 2
        + [pltpu.VMEM((8 * size if size % 32 else 4 * size, width), bf16)]
        + [pltpu.VMEM((rows, n), bf16) for n in (width, inner, inner, width)]
        + [DMA((6,))]
        + GATHER_SEMS,
        compiler_params=pltpu.CompilerParams(
            collective_id=cid, has_side_effects=True, vmem_limit_bytes=62 << 20
        ),
        cost_estimate=cost(80),
        name="second_exchange",
    )(middle, upstream, rows8, w_out, act2, hidden, d_pre, up_all, w_up, w_down)


def third_kernel(
    p_ref, x_ref, dmid_ref, rows_ref, vec_ref, act_ref, dt_ref, ctx_ref, dmall_ref,
    o_ref, vo_ref, gqkv_ref, gout_ref,
    own, vec, landed, sends, ss, sr, act, dt, ctx, dmall, load_sem, *sems,
):
    loads = load_all((act_ref, dt_ref, ctx_ref, dmall_ref), (act, dt, ctx, dmall), load_sem)
    greet_grid()
    share = share_start(p_ref, landed, sends, ss, sr)
    share_pass(share)
    part = dt.shape[0] // 3

    def project(job):
        k = pl.ds(pl.multiple_of(job // 2 * part, 64), part)
        m = pl.ds(pl.multiple_of(lax.rem(job, 2) * 640, 128), 640)
        gqkv_ref[k, m] = dot_nn(dt[k, :], act[:, m]).astype(jnp.bfloat16)

    now, work = products([(project, 6), outer_unit(ctx, dmall, gout_ref, part, 640)], 2)
    for load in loads:
        load.wait()
    now()
    grad = share_sum(share)
    normed, rstd, _ = layer_norm(x_ref[...].astype(jnp.float32), 1.0, 0.0)
    own[...] = (dmid_ref[...] + layer_norm_back(grad, normed, rstd, rows_ref[0:1, :])).astype(jnp.bfloat16)
    vec[...] = jnp.concatenate(
        [
            vec_ref[0:4, :],
            jnp.sum(grad * normed, 0, keepdims=True),
            jnp.sum(grad, 0, keepdims=True),
            jnp.zeros((2, grad.shape[1]), jnp.float32),
        ],
        0,
    )
    gather_steps([own, vec], [o_ref, vo_ref], sems, ahead=work)


def third_exchange(part, source, d_middle, rows8, vec, act1, d_qkv, context, d_middle_all, cid):
    size, width = d_middle.shape
    f32, bf16 = jnp.float32, jnp.bfloat16
    rows = act1.shape[0]
    total = d_qkv.shape[0]
    return pl.pallas_call(
        third_kernel,
        out_shape=(
            jax.ShapeDtypeStruct((rows, width), bf16),
            jax.ShapeDtypeStruct((256, width), f32),
            jax.ShapeDtypeStruct((total, width), bf16),
            jax.ShapeDtypeStruct((total // 3, width), bf16),
        ),
        in_specs=[VMEM] * 5 + [ANY] * 4,
        out_specs=[ANY, ANY, VMEM, VMEM],
        scratch_shapes=[pltpu.VMEM((size, width), bf16), pltpu.VMEM((8, width), f32)]
        + share_scratch(size, width)
        + [pltpu.VMEM(a.shape, bf16) for a in (act1, d_qkv, context, d_middle_all)]
        + [DMA((4,))]
        + GATHER_SEMS * 2,
        compiler_params=pltpu.CompilerParams(
            collective_id=cid, has_side_effects=True, vmem_limit_bytes=60 << 20
        ),
        cost_estimate=cost(60),
        name="third_exchange",
    )(
        part.reshape(4, size, width), source, d_middle, rows8, vec,
        act1, d_qkv, context, d_middle_all,
    )


def dot_nt(a, b):
    return lax.dot_general(a, b, (((1,), (1,)), ((), ())), preferred_element_type=jnp.float32)


def dot_nn(a, b):
    return lax.dot_general(a, b, (((1,), (0,)), ((), ())), preferred_element_type=jnp.float32)


def dot_tn(a, b):
    return lax.dot_general(a, b, (((0,), (0,)), ((), ())), preferred_element_type=jnp.float32)


def spans(offset_ref, length_ref, first, count):
    row = lax.broadcasted_iota(jnp.int32, (1, count), 1) + first
    start = jnp.zeros((1, count), jnp.int32)
    end = jnp.zeros((1, count), jnp.int32)
    low, high = 1 << 20, 0
    for i in range(8):
        a = offset_ref[i]
        b = a + length_ref[i]
        inside = (row >= a) & (row < b)
        start = jnp.where(inside, a, start)
        end = jnp.where(inside, b, end)
        used = (a < first + count) & (b > first) & (b > a)
        low = jnp.where(used, jnp.minimum(low, a // BK), low)
        high = jnp.where(used, jnp.maximum(high, (b + BK - 1) // BK), high)
    return start, end, low, high


def attend_kernel(heads, offset_ref, length_ref, qt_ref, k_ref, vt_ref, sent_ref, m_s, l_s, acc_s, win):
    mine = sent_ref.shape[0]
    rows = win.shape[0]
    local = heads * HD
    span = range(heads)
    dp = lax.axis_index("dp")
    skip = lax.rem(dp, 2) * (mine % 128)
    first = dp * mine - skip
    window = pl.ds(pl.multiple_of(lax.rem(dp, 2) * mine - skip, 128), rows)
    start, end, low, high = spans(offset_ref, length_ref, first, rows)
    m_s[...] = jnp.full_like(m_s, NEG)
    l_s[...] = jnp.zeros_like(l_s)
    acc_s[...] = jnp.zeros_like(acc_s)
    q = [qt_ref[h * HD : (h + 1) * HD, window] for h in span]

    def body(kb, carry):
        k0 = pl.multiple_of(kb * BK, BK)
        key = lax.broadcasted_iota(jnp.int32, (BK, rows), 0) + k0
        mask = (key >= start) & (key < end)
        s = [
            jnp.where(
                mask,
                dot_nn(k_ref[pl.ds(k0, BK), h * HD : (h + 1) * HD], q[h]),
                NEG,
            )
            for h in span
        ]
        p, a = [], []
        for h in span:
            old = m_s[h]
            new = jnp.maximum(old, jnp.max(s[h], 0, keepdims=True))
            e = jnp.exp(s[h] - new)
            scale = jnp.exp(old - new)
            l_s[h] = scale * l_s[h] + jnp.sum(e, 0, keepdims=True)
            m_s[h] = new
            p.append(e.astype(jnp.bfloat16))
            a.append(scale)
        for h in span:
            vt = vt_ref[h * HD : (h + 1) * HD, pl.ds(k0, BK)]
            acc_s[h] = a[h] * acc_s[h] + dot_nn(vt, p[h])
        return carry

    lax.fori_loop(low, high, body, 0)
    parts = [[], [], []]
    for h in span:
        total = l_s[h]
        total = jnp.where(total == 0.0, 1.0, total)
        rest = m_s[h] + jnp.log(total)
        for part in parts:
            part.append(rest.astype(jnp.bfloat16).astype(jnp.float32))
            rest = rest - part[-1]
        out = acc_s[h] * (1.0 / total)
        win[:, h * HD : (h + 1) * HD] = out.T
    blank = [jnp.zeros((win.shape[1] - local - 3 * heads, rows), jnp.float32)]
    win[:, local:] = jnp.concatenate(parts[0] + parts[1] + parts[2] + blank, 0).T
    sent_ref[...] = win[pl.ds(pl.multiple_of(skip, 16), mine), :].astype(jnp.bfloat16)


def whole(a):
    return pl.BlockSpec(a.shape, lambda i, *_: (0,) * len(a.shape), pipeline_mode=pl.Buffered(1))


def attend(qt, k, vt, offsets, lengths, heads):
    mine = k.shape[0] // 8
    rows = (mine + mine % 128 + 127) // 128 * 128
    local = heads * HD
    wide = (local + 3 * heads + 127) // 128 * 128
    row = pltpu.VMEM((heads, 1, rows), jnp.float32)
    return pl.pallas_call(
        functools.partial(attend_kernel, heads),
        out_shape=jax.ShapeDtypeStruct((mine, wide), jnp.bfloat16),
        in_specs=[SMEM, SMEM, VMEM, VMEM, VMEM],
        out_specs=VMEM,
        scratch_shapes=[
            row,
            row,
            pltpu.VMEM((heads, HD, rows), jnp.float32),
            pltpu.VMEM((rows, wide), jnp.float32),
        ],
        compiler_params=pltpu.CompilerParams(vmem_limit_bytes=60 << 20),
        cost_estimate=cost(10),
        name="attend",
    )(offsets, lengths, qt, k, vt)


def attend_back_kernel(
    heads, offset_ref, length_ref, k_ref, v_ref, qkt_ref, dot_ref, sent_ref, up_ref, down_ref,
    d_ref, sum_ref, up_out, down_out, dk_s, dv_s, dq_s
):
    i = pl.program_id(0)
    local = heads * HD
    span = range(heads)
    sl = [slice(h * HD, (h + 1) * HD) for h in span]
    at_q = pl.ds(pl.multiple_of(i * BQ, BQ), BQ)

    @pl.when(i == 0)
    def _():
        dk_s[...] = jnp.zeros_like(dk_s)
        dv_s[...] = jnp.zeros_like(dv_s)
        sum_ref[...] = jnp.zeros_like(sum_ref)

    start, end, low, high = spans(offset_ref, length_ref, i * BQ, BQ)
    dq_s[...] = jnp.zeros_like(dq_s)
    sent = sent_ref[at_q, :].astype(jnp.float32).T
    lse, delta = [], []
    for h in span:
        a = local + h
        lse.append(
            sent[a : a + 1] + sent[a + heads : a + heads + 1] + sent[a + 2 * heads : a + 2 * heads + 1]
        )
        delta.append(jnp.sum(dot_ref[sl[h], at_q].astype(jnp.float32) * sent[sl[h]], 0, keepdims=True))

    def blocks(first, count):
        keys = []
        for n in range(count):
            at_k = pl.ds(pl.multiple_of((first + n) * BK, BK), BK)
            key = lax.broadcasted_iota(jnp.int32, (BK, BQ), 0) + (first + n) * BK
            keys.append((at_k, (key >= start) & (key < end)))
        jobs = [(at_k, mask, h) for at_k, mask in keys for h in span]

        def products(at_k, mask, h):
            s = dot_nn(k_ref[at_k, sl[h]], qkt_ref[sl[h], at_q])
            dp = dot_nn(v_ref[at_k, sl[h]], dot_ref[sl[h], at_q])
            return s, dp

        def scores(at_k, mask, h, s, dp):
            p = jnp.exp(jnp.where(mask, s, NEG) - lse[h])
            ds = (p * (dp - delta[h])).astype(jnp.bfloat16)
            return p.astype(jnp.bfloat16), ds

        def gradients(at_k, mask, h, p, ds):
            dv_s[h, :, at_k] += dot_nt(dot_ref[sl[h], at_q], p)
            dk_s[h, :, at_k] += dot_nt(qkt_ref[sl[h], at_q], ds)
            dq_s[h] += dot_nn(qkt_ref[local + h * HD : local + (h + 1) * HD, at_k], ds)

        now = products(*jobs[0])
        held = None
        for n, job in enumerate(jobs):
            later = products(*jobs[n + 1]) if n + 1 < len(jobs) else None
            done = scores(*job, *now)
            if held is not None:
                gradients(*jobs[n - 1], *held)
            held, now = done, later
        gradients(*jobs[-1], *held)

    def pair(n, carry):
        blocks(low + 2 * n, 2)
        return carry

    pairs = jnp.maximum(high - low, 0) // 2
    lax.fori_loop(0, pairs, pair, 0)

    @pl.when(low + 2 * pairs < high)
    def _():
        blocks(low + 2 * pairs, 1)

    for src, dst in ((up_ref, up_out), (down_ref, down_out)):
        dst[...] = src[...].astype(jnp.float32)
    for h in span:
        dq = dq_s[h] * HD**-0.5
        d_ref[sl[h], at_q] = dq.astype(jnp.bfloat16)
        sum_ref[sl[h], :] += dq[:, :128] + dq[:, 128:]

    @pl.when(i == pl.num_programs(0) - 1)
    def _():
        for h in span:
            d_ref[local + h * HD : local + (h + 1) * HD, :] = dk_s[h].astype(jnp.bfloat16)
            d_ref[2 * local + h * HD : 2 * local + (h + 1) * HD, :] = dv_s[h].astype(jnp.bfloat16)
            total = dv_s[h, :, 0:128]
            for n in range(1, dv_s.shape[2] // 128):
                total += dv_s[h, :, n * 128 : (n + 1) * 128]
            sum_ref[local + h * HD : local + (h + 1) * HD, :] = total


def attend_back(k, v, qkt, dot, sent, offsets, lengths, up, down, heads):
    rows = k.shape[0]
    local = heads * HD
    tall = pltpu.VMEM((heads, HD, rows), jnp.float32)

    def const(shape):
        return pl.BlockSpec(shape, lambda i, *_: (0, 0), pipeline_mode=pl.Buffered(1))

    strips = [
        pl.BlockSpec((a.shape[0] // 10, a.shape[1]), lambda i, *_: (jnp.minimum(i, 9), 0))
        for a in (up, down)
    ]
    return pl.pallas_call(
        functools.partial(attend_back_kernel, heads),
        out_shape=(
            jax.ShapeDtypeStruct((3 * local, rows), jnp.bfloat16),
            jax.ShapeDtypeStruct((2 * local, 128), jnp.float32),
            jax.ShapeDtypeStruct(up.shape, jnp.float32),
            jax.ShapeDtypeStruct(down.shape, jnp.float32),
        ),
        grid_spec=pltpu.PrefetchScalarGridSpec(
            num_scalar_prefetch=2,
            grid=(rows // BQ,),
            in_specs=[whole(a) for a in (k, v, qkt, dot, sent)] + strips,
            out_specs=[const((3 * local, rows)), const((2 * local, 128))] + strips,
            scratch_shapes=[tall, tall, pltpu.VMEM((heads, HD, BQ), jnp.float32)],
        ),
        compiler_params=pltpu.CompilerParams(vmem_limit_bytes=60 << 20),
        cost_estimate=cost(60),
        name="attend_back",
    )(offsets, lengths, k, v, qkt, dot, sent, up, down)


def finish_kernel(
    offset_ref, length_ref, m_ref, d_ref, qkv_ref, out_ref, mo_ref, do_ref, qkv_out, out_out, m, d, sems
):
    i = pl.program_id(0)
    size = mo_ref.shape[0]
    rows = m_ref.shape[0]
    offset = offset_ref[8]
    length = length_ref[8]

    def first(n):
        return pl.multiple_of(jnp.minimum(offset + n * size, rows - size), 16)

    def loads(n):
        return [
            pltpu.make_async_copy(
                src.at[pl.ds(first(n), size)], dst.at[n, pl.ds(0, size)], sems.at[k, n]
            )
            for k, (src, dst) in enumerate(((m_ref, m), (d_ref, d)))
        ]

    @pl.when(i == 0)
    def _():
        for n in range(m.shape[0]):
            for load in loads(n):
                load.start()

    qkv_out[...] = qkv_ref[...].astype(jnp.float32)
    out_out[...] = out_ref[...].astype(jnp.float32)
    shift = pl.multiple_of(jnp.minimum(offset + i * size - first(i), size), 16)
    row = lax.broadcasted_iota(jnp.int32, (size, 1), 0) + i * size
    for load, src, dst in zip(loads(i), (m, d), (mo_ref, do_ref)):
        load.wait()
        value = jnp.where(row < length, src[i, pl.ds(shift, size), :].astype(jnp.float32), 0.0)
        dst[...] = value.astype(dst.dtype)


def finish(offsets, lengths, mixed, d_tokens, g_qkv, g_out, cap):
    width = mixed.shape[1]
    steps = cap // 128
    held = pltpu.VMEM((steps, 256, width), jnp.bfloat16)
    f32 = jnp.float32

    def strip(count):
        return pl.BlockSpec((count, width), lambda i: (i, 0))

    short = pl.BlockSpec((g_out.shape[0] // 10, width), lambda i: (jnp.minimum(i, 9), 0))
    tall = strip(g_qkv.shape[0] // steps)
    return pl.pallas_call(
        finish_kernel,
        grid=(steps,),
        out_shape=(
            jax.ShapeDtypeStruct((cap, width), jnp.bfloat16),
            jax.ShapeDtypeStruct((cap, width), f32),
            jax.ShapeDtypeStruct(g_qkv.shape, f32),
            jax.ShapeDtypeStruct(g_out.shape, f32),
        ),
        in_specs=[SMEM, SMEM, ANY, ANY, tall, short],
        out_specs=[strip(128), strip(128), tall, short],
        scratch_shapes=[held, held, DMA((2, steps))],
        compiler_params=pltpu.CompilerParams(vmem_limit_bytes=60 << 20),
        name="finish",
    )(offsets, lengths, mixed, d_tokens, g_qkv, g_out)


def packed_step(size, cids, table, args):
    (
        tokens, clip_len, _, w_qkv, bias_q, bias_v, w_out, bias_out, w_up, bias_up, w_down, bias_down,
        gain1, shift1, gain2, shift2, grad_out,
    ) = args
    f32, bf16 = jnp.float32, jnp.bfloat16
    cap, width = tokens.shape
    local = w_qkv.shape[2]
    heads = local // HD
    rows = 32 * size
    mine = 4 * size
    dp = lax.axis_index("dp")
    pack_id, first_id, second_id, third_id = cids

    x_parts, up_parts, offsets, lengths = take_pieces(tokens, grad_out, table, clip_len, size)
    wt = w_qkv.transpose(1, 2, 0).reshape(3 * local, width)
    bias = jnp.concatenate([bias_q, jnp.zeros_like(bias_q), bias_v])
    spare = jnp.zeros_like(gain1)
    rows8 = jnp.stack([gain1, shift1, gain2, shift2, bias_out, bias_down, spare, spare])
    source, act1, k, vt, qt = pack_gather(x_parts, wt, bias, rows8, pack_id)
    up_own = lax.psum_scatter(up_parts, "dp", scatter_dimension=0, tiled=True)
    up_own, source = lax.optimization_barrier((up_own, source))
    up_all = lax.all_gather(up_own.reshape(size, width), ("dp", "tensor"), tiled=True)

    sent_own = attend(qt, k, vt, offsets, lengths, heads)
    part = jnp.dot(sent_own[:, :local], w_out, preferred_element_type=f32).astype(bf16)
    sent = lax.all_gather(sent_own, "dp", tiled=True)
    middle, act2, qkt, v = first_exchange(
        part, source, rows8, wt, bias, act1, first_id
    )

    pre = jnp.dot(act2, w_up, preferred_element_type=f32) + bias_up
    hidden_f, slope = gelu_pair(pre)
    hidden = hidden_f.astype(bf16)
    d_pre = contract_last(up_all, w_down) * slope
    g_up_bias = jnp.sum(d_pre, 0)
    d_pre_b = d_pre.astype(bf16)
    d_middle, mixed, vec, d_middle_b, g_up, g_down, d_context = second_exchange(
        middle, up_own.reshape(size, width), rows8, w_out, act2, hidden, d_pre_b, up_all,
        w_up, w_down, second_id,
    )
    mixed_all = lax.all_gather(mixed, ("dp", "tensor"), tiled=True)
    d_qkv, column, g_up, g_down = attend_back(
        k, v, qkt, d_context, sent, offsets, lengths, g_up, g_down, heads
    )
    column = jnp.sum(column, 1)
    d_own = lax.dynamic_slice_in_dim(d_qkv, dp * mine, mine, 1)
    d_act1 = jnp.einsum("kr,kd->rd", d_own, wt, preferred_element_type=f32).astype(bf16)
    d_tokens_all, vectors_all, g_qkv, g_out = third_exchange(
        d_act1, source, d_middle, rows8, vec, act1, d_qkv, sent, d_middle_b, third_id
    )
    sums = jnp.sum(vectors_all.reshape(32, 8, width), 0)
    mixed, d_tokens, g_qkv, g_out = finish(
        offsets, lengths, mixed_all, d_tokens_all, g_qkv, g_out, cap
    )
    g_qkv = g_qkv.reshape(3, local, width).transpose(2, 0, 1)

    return (
        mixed,
        d_tokens,
        g_qkv,
        column[:local],
        column[local:],
        g_out,
        sums[3],
        g_up,
        g_up_bias,
        g_down,
        sums[2],
        sums[4],
        sums[5],
        sums[0],
        sums[1],
    )


def packed(*args):
    clip_len, slot_clip = args[1], args[2]

    def padded(value):
        return (value + 15) // 16 * 16

    need = jnp.sum(padded(clip_len))
    table = gather_table(slot_clip[0], 0)
    branches = [
        functools.partial(packed_step, size, [1 + 4 * n + i for i in range(4)])
        for n, size in enumerate(BLOCKS)
    ]
    rank = sum((need > 32 * size).astype(jnp.int32) for size in sorted(BLOCKS))
    pick = jnp.array([BLOCKS.index(size) for size in sorted(BLOCKS)] + [len(BLOCKS)], jnp.int32)[rank]

    def fallback(table, args):
        return plain(*args)

    return lax.switch(pick, branches + [fallback], table, args)


def solution(mesh):
    placed = (
        P("dp", None),
        P(),
        P("dp"),
        P(None, None, "tensor"),
        P("tensor"),
        P("tensor"),
        P("tensor", None),
        P(),
        P(None, "tensor"),
        P("tensor"),
        P("tensor", None),
        P(),
        P(),
        P(),
        P(),
        P(),
        P("dp", None),
    )
    fits = mesh.shape["dp"] == 8 and mesh.shape["tensor"] == 4
    return jax.shard_map(
        packed if fits else plain,
        mesh=mesh,
        in_specs=placed,
        out_specs=(
            P("dp", None),
            P("dp", None),
            P(None, None, "tensor"),
            P("tensor"),
            P("tensor"),
            P("tensor", None),
            P(),
            P(None, "tensor"),
            P("tensor"),
            P("tensor", None),
            P(),
            P(),
            P(),
            P(),
            P(),
        ),
        check_vma=False,
    )
```

```python
import functools

import jax
import jax.numpy as jnp
from jax import lax
from jax.experimental import pallas as pl
from jax.experimental.pallas import tpu as pltpu
from jax.sharding import PartitionSpec as P

HD = 64


EPS = 1e-05
NEG = -1e30
HALF_ROOT = 0.7071067811865476
INV_ROOT_TAU = 0.3989422804014327


def layer_norm(value, gain, shift):
    center = value - jnp.mean(value, -1, keepdims=True)
    rstd = lax.rsqrt(jnp.mean(center * center, -1, keepdims=True) + EPS)
    normed = center * rstd
    return (normed, rstd, normed * gain + shift)


def layer_norm_back(grad, normed, rstd, gain):
    scaled = grad * gain
    return rstd * (
        scaled
        - jnp.mean(scaled, -1, keepdims=True)
        - normed * jnp.mean(scaled * normed, -1, keepdims=True)
    )


def gelu_pair(value):
    cdf = 0.5 * (1.0 + jax.scipy.special.erf(value * HALF_ROOT))
    return (value * cdf, cdf + value * jnp.exp(-0.5 * value * value) * INV_ROOT_TAU)


def contract_first(left, right):
    return lax.dot_general(
        left, right, (((0,), (0,)), ((), ())), preferred_element_type=jnp.float32
    )


def contract_last(left, right):
    return lax.dot_general(
        left, right, (((1,), (1,)), ((), ())), preferred_element_type=jnp.float32
    )


def masked_scores(query_clip, keys_clip, length, positions, scale):
    raw = (
        jnp.einsum("qhe,khe->hqk", query_clip, keys_clip, preferred_element_type=jnp.float32)
        * scale
    )
    return jnp.where((positions < length)[None, None, :], raw, NEG)


def plain(
    tokens,
    clip_len,
    slot_clip,
    w_qkv,
    bias_q,
    bias_v,
    w_out,
    bias_out,
    w_up,
    bias_up,
    w_down,
    bias_down,
    gain1,
    shift1,
    gain2,
    shift2,
    grad_out,
):
    rows, width = tokens.shape
    clips = slot_clip.shape[0]
    cap = rows // clips
    local = w_qkv.shape[2]
    heads = local // HD
    scale = HD ** (-0.5)
    positions = jnp.arange(cap, dtype=jnp.int32)
    match = slot_clip[:, None] == jnp.arange(clip_len.shape[0], dtype=jnp.int32)[None, :]
    lengths = jnp.sum(jnp.where(match, clip_len[None, :], 0), 1)
    valid = (positions[None, :] < lengths[:, None]).reshape(rows, 1)
    source = tokens.astype(jnp.float32)
    normed1, rstd1, pre1 = layer_norm(source, gain1, shift1)
    act1 = pre1.astype(jnp.bfloat16)
    joined = w_qkv.reshape(width, 3 * local)
    proj = jnp.dot(act1, joined, preferred_element_type=jnp.float32)
    query = (proj[:, :local] + bias_q).astype(jnp.bfloat16)
    keys = proj[:, local : 2 * local].astype(jnp.bfloat16)
    values = (proj[:, 2 * local :] + bias_v).astype(jnp.bfloat16)

    def per_clip(value):
        return value.reshape(clips, cap, heads, HD)

    def forward_clip(inputs):
        query_clip, keys_clip, values_clip, length = inputs
        raw = masked_scores(query_clip, keys_clip, length, positions, scale)
        top = jnp.max(raw, -1, keepdims=True)
        lse = top + jnp.log(jnp.sum(jnp.exp(raw - top), -1, keepdims=True))
        probs = jnp.exp(raw - lse).astype(jnp.bfloat16)
        context_clip = jnp.einsum(
            "hqk,khe->qhe", probs, values_clip, preferred_element_type=jnp.float32
        )
        return (context_clip.astype(jnp.bfloat16), lse)

    context_all, lse_all = lax.map(
        forward_clip, (per_clip(query), per_clip(keys), per_clip(values), lengths)
    )
    context = context_all.reshape(rows, local)
    attended = lax.psum(
        jnp.dot(context, w_out, preferred_element_type=jnp.float32).astype(jnp.bfloat16), "tensor"
    ).astype(jnp.float32)
    middle = source + attended + bias_out
    normed2, rstd2, pre2 = layer_norm(middle, gain2, shift2)
    act2 = pre2.astype(jnp.bfloat16)
    pre = jnp.dot(act2, w_up, preferred_element_type=jnp.float32) + bias_up
    hidden_f, slope = gelu_pair(pre)
    hidden = hidden_f.astype(jnp.bfloat16)
    branch = lax.psum(
        jnp.dot(hidden, w_down, preferred_element_type=jnp.float32).astype(jnp.bfloat16), "tensor"
    ).astype(jnp.float32)
    mixed = jnp.where(valid, middle + branch + bias_down, 0.0).astype(jnp.bfloat16)
    upstream = jnp.where(valid, grad_out.astype(jnp.float32), 0.0)
    upstream_b = upstream.astype(jnp.bfloat16)
    g_down_bias = jnp.sum(upstream, 0)
    g_down = contract_first(hidden, upstream_b)
    d_pre = contract_last(upstream_b, w_down) * slope
    g_up_bias = jnp.sum(d_pre, 0)
    d_pre_b = d_pre.astype(jnp.bfloat16)
    g_up = contract_first(act2, d_pre_b)
    d_act2 = lax.psum(contract_last(d_pre_b, w_up).astype(jnp.bfloat16), "tensor").astype(
        jnp.float32
    )
    g_gain2 = jnp.sum(d_act2 * normed2, 0)
    g_shift2 = jnp.sum(d_act2, 0)
    d_middle = upstream + layer_norm_back(d_act2, normed2, rstd2, gain2)
    g_out_bias = jnp.sum(d_middle, 0)
    d_middle_b = d_middle.astype(jnp.bfloat16)
    g_out = contract_first(context, d_middle_b)
    d_context = contract_last(d_middle_b, w_out).astype(jnp.bfloat16)

    def backward_clip(inputs):
        query_clip, keys_clip, values_clip, context_clip, dcontext_clip, lse, length = inputs
        raw = masked_scores(query_clip, keys_clip, length, positions, scale)
        probs_f = jnp.exp(raw - lse)
        probs = probs_f.astype(jnp.bfloat16)
        d_probs = jnp.einsum(
            "qhe,khe->hqk", dcontext_clip, values_clip, preferred_element_type=jnp.float32
        )
        delta = jnp.sum(dcontext_clip.astype(jnp.float32) * context_clip.astype(jnp.float32), -1).T[
            :, :, None
        ]
        d_scores = (probs_f * (d_probs - delta) * scale).astype(jnp.bfloat16)
        d_query_clip = jnp.einsum(
            "hqk,khe->qhe", d_scores, keys_clip, preferred_element_type=jnp.float32
        )
        d_keys_clip = jnp.einsum(
            "hqk,qhe->khe", d_scores, query_clip, preferred_element_type=jnp.float32
        )
        d_values_clip = jnp.einsum(
            "hqk,qhe->khe", probs, dcontext_clip, preferred_element_type=jnp.float32
        )
        return (d_query_clip, d_keys_clip, d_values_clip)

    d_query, d_keys, d_values = lax.map(
        backward_clip,
        (
            per_clip(query),
            per_clip(keys),
            per_clip(values),
            context_all,
            per_clip(d_context),
            lse_all,
            lengths,
        ),
    )
    d_query = d_query.reshape(rows, local)
    d_keys = d_keys.reshape(rows, local)
    d_values = d_values.reshape(rows, local)
    g_bias_q = jnp.sum(d_query, 0)
    g_bias_v = jnp.sum(d_values, 0)
    stacked = jnp.concatenate(
        [d_query.astype(jnp.bfloat16), d_keys.astype(jnp.bfloat16), d_values.astype(jnp.bfloat16)],
        1,
    )
    g_qkv = contract_first(act1, stacked).reshape(width, 3, local)
    d_act1 = lax.psum(contract_last(stacked, joined).astype(jnp.bfloat16), "tensor").astype(
        jnp.float32
    )
    g_gain1 = jnp.sum(d_act1 * normed1, 0)
    g_shift1 = jnp.sum(d_act1, 0)
    d_tokens = jnp.where(valid, d_middle + layer_norm_back(d_act1, normed1, rstd1, gain1), 0.0)
    (
        g_qkv,
        g_bias_q,
        g_bias_v,
        g_out,
        g_out_bias,
        g_up,
        g_up_bias,
        g_down,
        g_down_bias,
        g_gain1,
        g_shift1,
        g_gain2,
        g_shift2,
    ) = (
        lax.psum(g_qkv.astype(jnp.bfloat16), "dp").astype(jnp.float32),
        lax.psum(g_bias_q.astype(jnp.bfloat16), "dp").astype(jnp.float32),
        lax.psum(g_bias_v.astype(jnp.bfloat16), "dp").astype(jnp.float32),
        lax.psum(g_out.astype(jnp.bfloat16), "dp").astype(jnp.float32),
        lax.psum(g_out_bias.astype(jnp.bfloat16), "dp").astype(jnp.float32),
        lax.psum(g_up.astype(jnp.bfloat16), "dp").astype(jnp.float32),
        lax.psum(g_up_bias.astype(jnp.bfloat16), "dp").astype(jnp.float32),
        lax.psum(g_down.astype(jnp.bfloat16), "dp").astype(jnp.float32),
        lax.psum(g_down_bias.astype(jnp.bfloat16), "dp").astype(jnp.float32),
        lax.psum(g_gain1.astype(jnp.bfloat16), "dp").astype(jnp.float32),
        lax.psum(g_shift1.astype(jnp.bfloat16), "dp").astype(jnp.float32),
        lax.psum(g_gain2.astype(jnp.bfloat16), "dp").astype(jnp.float32),
        lax.psum(g_shift2.astype(jnp.bfloat16), "dp").astype(jnp.float32),
    )
    return (
        mixed,
        d_tokens,
        g_qkv,
        g_bias_q,
        g_bias_v,
        g_out,
        g_out_bias,
        g_up,
        g_up_bias,
        g_down,
        g_down_bias,
        g_gain1,
        g_shift1,
        g_gain2,
        g_shift2,
    )


MESH = pl.DeviceIdType.MESH
DMA = pltpu.SemaphoreType.DMA
ANY = pl.BlockSpec(memory_space=pl.ANY)
VMEM = pl.BlockSpec(memory_space=pltpu.VMEM)
SMEM = pl.BlockSpec(memory_space=pltpu.SMEM)
BLOCKS = (96, 80, 112)
BQ = 256
BK = 256


def cost(us):
    return pl.CostEstimate(flops=int(us * 1e9), bytes_accessed=int(us * 3e6), transcendentals=0)


def coords():
    dp = lax.axis_index("dp")
    t = lax.axis_index("tensor")
    return dp // 2, dp % 2, t // 2, t % 2


def device(z, y, x, c):
    return (z * 2 + y, x * 2 + c)


def greet(peers):
    barrier = pltpu.get_barrier_semaphore()
    for peer in peers:
        pl.semaphore_signal(barrier, inc=1, device_id=peer, device_id_type=MESH)
    pl.semaphore_wait(barrier, len(peers))


def greet_grid():
    z, y, x, c = coords()
    barrier = pltpu.get_barrier_semaphore()

    def signal(peer):
        pl.semaphore_signal(barrier, inc=1, device_id=peer, device_id_type=MESH)

    @pl.when(z > 0)
    def _():
        signal(device(z - 1, y, x, c))

    @pl.when(z < 3)
    def _():
        signal(device(z + 1, y, x, c))

    signal(device(z, 1 - y, x, c))
    signal(device(z, y, 1 - x, c))
    signal(device(z, y, x, 1 - c))

    pl.semaphore_wait(barrier, 3 + jnp.minimum(z, 1) + jnp.minimum(3 - z, 1))


GATHER_SEMS = [DMA, DMA((4,)), DMA((4,)), DMA((4,)), DMA((8,)), DMA((16,)), DMA((32,))]


def gather_steps(x_refs, o_refs, sems, work=None, ahead=None):
    z, y, x, c = coords()
    n = len(GATHER_SEMS)
    arrays = [(a, o) + tuple(sems[n * i : n * i + n]) for i, (a, o) in enumerate(zip(x_refs, o_refs))]

    def block(z, y, x, c):
        return (z * 2 + y) * 4 + x * 2 + c

    ux, uy = x + (1 - c) * (1 - 2 * x), y + c * (1 - 2 * y)
    vx, vy = x + c * (1 - 2 * x), y + (1 - c) * (1 - 2 * y)
    own = block(z, y, x, c)
    core = device(z, y, x, 1 - c)

    def rows(array, b):
        size = array[0].shape[0]
        return array[1].at[pl.ds(pl.multiple_of(b * size, size), size)]

    def copy(array, b, kind, i, peer):
        return pltpu.make_async_remote_copy(
            src_ref=rows(array, b),
            dst_ref=rows(array, b),
            send_sem=array[kind].at[i],
            recv_sem=array[8].at[b],
            device_id=peer,
            device_id_type=MESH,
        )

    def send(b, kind, i, peer, first=False):
        for array in arrays:
            if first:
                pltpu.make_async_remote_copy(
                    src_ref=array[0],
                    dst_ref=rows(array, b),
                    send_sem=array[kind].at[i],
                    recv_sem=array[8].at[b],
                    device_id=peer,
                    device_id_type=MESH,
                ).start()
            else:
                copy(array, b, kind, i, peer).start()

    def arrived(b):
        for array in arrays:
            copy(array, b, 7, 0, core).wait_recv()

    right, left = device(z + 1, y, x, c), device(z - 1, y, x, c)
    u, v = device(z, uy, ux, c), device(z, vy, vx, c)
    locals_ = [pltpu.make_async_copy(a[0], rows(a, own), a[2]) for a in arrays]

    @pl.when(z < 3)
    def _():
        send(own, 3, z, right, True)

    @pl.when(z > 0)
    def _():
        send(own, 4, z, left, True)

    send(own, 5, z, u, True)
    send(own, 6, z, v, True)
    send(own, 7, z, core, True)
    for local in locals_:
        local.start()

    def near(step):
        def from_low(low):
            return jnp.where((low == 1) & (step < 2), 1 - step, step)

        return jnp.where(z < 2, from_low(z), 3 - from_low(3 - z))

    def got_line(at):
        b = block(at, y, x, c)
        arrived(b)

        @pl.when((at < z) & (z < 3))
        def _():
            send(b, 3, at, right)

        @pl.when((at > z) & (z > 0))
        def _():
            send(b, 4, at, left)

        send(b, 5, at, u)
        send(b, 6, at, v)
        send(b, 7, at, core)

    def got_u(at):
        b = block(at, uy, ux, c)
        arrived(b)
        send(b, 6, 4 + at, v)
        send(b, 7, 4 + at, core)

    def got_v(at):
        b = block(at, vy, vx, c)
        arrived(b)
        send(b, 7, 8 + at, core)

    def got_uv(at):
        b = block(at, 1 - y, 1 - x, c)
        arrived(b)
        send(b, 7, 12 + at, core)

    def around(event, distance):
        for side in (-1, 1):
            at = z + side * distance
            here = (at >= 0) & (at < 4)
            if side == 1:
                here = here & (distance > 0)
            pl.when(here)(functools.partial(event, at))

    @pl.loop(0, 19)
    def _(step):
        line = (step < 6) & (lax.rem(step, 2) == 0)
        at = near(jnp.maximum(step - 7, 0) // 3)
        kind = lax.rem(step + 2, 3)

        @pl.when(line)
        def _():
            around(got_line, step // 2 + 1)

        @pl.when((step < 7) & jnp.logical_not(line))
        def _():
            around(got_u, step // 2)

        @pl.when((step >= 7) & (kind == 0))
        def _():
            got_v(at)

        @pl.when((step >= 7) & (kind == 1))
        def _():
            got_uv(at)

        @pl.when((step >= 7) & (kind == 2))
        def _():
            @pl.loop(0, 4)
            def _(i):
                arrived(at * 8 + i * 2 + 1 - c)

        @pl.when(step == 6)
        def _():
            for local in locals_:
                local.wait()

        if ahead is not None:
            ahead(step)
        if work is not None:
            pl.when((step >= 7) & (kind == 2))(functools.partial(work, at))

    def sent(kind, i):
        for array in arrays:
            copy(array, own, kind, i, core).wait_send()

    @pl.loop(0, 16)
    def _(i):
        sent(7, i)

    @pl.loop(0, 8)
    def _(i):
        sent(6, i)

    @pl.loop(0, 4)
    def _(i):
        sent(5, i)

        @pl.when((i <= z) & (z < 3))
        def _():
            sent(3, i)

        @pl.when((i >= z) & (z > 0))
        def _():
            sent(4, i)


def table_kernel(x_ref, o_ref, send_sem, recv_sem):
    me = lax.axis_index("dp")
    t = lax.axis_index("tensor")
    peers = [(lax.rem(me + s, 8), t) for s in range(1, 8)]
    greet(peers)
    o_ref[me] = x_ref[...]
    copies = [
        pltpu.make_async_remote_copy(
            src_ref=x_ref,
            dst_ref=o_ref.at[me],
            send_sem=send_sem.at[s],
            recv_sem=recv_sem.at[s],
            device_id=peer,
            device_id_type=MESH,
        )
        for s, peer in enumerate(peers)
    ]
    for copy in copies:
        copy.start()
    for copy in copies:
        copy.wait()


def gather_table(value, cid):
    tile = jnp.broadcast_to(value.reshape(1, 1), (8, 128))
    out = pl.pallas_call(
        table_kernel,
        out_shape=jax.ShapeDtypeStruct((8, 8, 128), value.dtype),
        in_specs=[VMEM],
        out_specs=VMEM,
        scratch_shapes=[DMA((7,)), DMA((7,))],
        compiler_params=pltpu.CompilerParams(collective_id=cid, has_side_effects=True),
        name="table",
    )(tile)
    return out[:, 0, 0]


def pieces_kernel(size, table_ref, clip_ref, x_ref, u_ref, xo_ref, uo_ref, offset_ref, length_ref, held, sems):
    t = lax.axis_index("tensor")
    dp = lax.axis_index("dp")
    cap = x_ref.shape[0]
    loads = [
        pltpu.make_async_copy(src, held.at[i, pl.ds(size, cap)], sems.at[i])
        for i, src in enumerate((x_ref, u_ref))
    ]
    for load in loads:
        load.start()
    lengths = []
    for s in range(8):
        clip = table_ref[s]
        lengths.append(jnp.where(clip >= 0, clip_ref[jnp.maximum(clip, 0)], 0))
    offset = length = 0
    for s in range(8):
        before = 0
        for o in range(8):
            if o != s:
                ahead = lengths[o] >= lengths[s] if o < s else lengths[o] > lengths[s]
                before += jnp.where(ahead, (lengths[o] + 15) // 16 * 16, 0)
        offset_ref[s] = before
        length_ref[s] = lengths[s]
        offset = jnp.where(dp == s, before, offset)
        length = jnp.where(dp == s, lengths[s], length)
    offset_ref[8] = offset
    length_ref[8] = length
    for i in (0, 1):
        held[i, 0:size, :] = jnp.zeros((size, held.shape[2]), held.dtype)
        held[i, size + cap :, :] = jnp.zeros((size, held.shape[2]), held.dtype)
    for i, out in enumerate((xo_ref, uo_ref)):
        loads[i].wait()

        @pl.loop(0, 8)
        def _(b):
            first = (b * 4 + t) * size - offset + size
            first = pl.multiple_of(jnp.clip(first, 0, cap + size), 16)
            row = lax.broadcasted_iota(jnp.int32, (size, 1), 0) + first - size
            value = held[i, pl.ds(first, size), :].astype(jnp.float32)
            value = jnp.where((row >= 0) & (row < length), value, 0.0)
            out[b] = value.astype(jnp.bfloat16)


def take_pieces(x, u, table, clip_len, size):
    cap, width = x.shape
    shape = jax.ShapeDtypeStruct((8, size, width), jnp.bfloat16)
    ints = jax.ShapeDtypeStruct((9,), jnp.int32)
    return pl.pallas_call(
        functools.partial(pieces_kernel, size),
        out_shape=(shape, shape, ints, ints),
        in_specs=[SMEM, SMEM, ANY, ANY],
        out_specs=(VMEM, VMEM, SMEM, SMEM),
        scratch_shapes=[pltpu.VMEM((2, cap + 2 * size, width), jnp.bfloat16), DMA((2,))],
        compiler_params=pltpu.CompilerParams(vmem_limit_bytes=60 << 20),
        name="pieces",
    )(table, clip_len, x, u)


def pack_kernel(
    p_ref,
    wt_ref,
    bias_ref,
    vec_ref,
    own,
    act_ref,
    k_ref,
    vt_ref,
    qt_ref,
    x_all,
    acc,
    y_out,
    y_in,
    r_out,
    r_in,
    l_out,
    l_in,
    ys,
    yr,
    rs,
    rr,
    ls,
    lr,
    *gather_sems,
):
    z, y, x, c = coords()
    size = own.shape[0]
    local = k_ref.shape[1]
    greet_grid()

    def piece(zp, yp):
        return p_ref[zp * 2 + yp].astype(jnp.float32)

    def project(at):
        @pl.loop(0, 8)
        def _(i):
            r = pl.ds(pl.multiple_of(at * 8 * size + i * size, size), size)
            _, _, pre = layer_norm(x_all[r, :].astype(jnp.float32), vec_ref[0:1, :], vec_ref[1:2, :])
            act_ref[r, :] = pre.astype(jnp.bfloat16)

        r = pl.ds(pl.multiple_of(at * 8 * size, 8 * size), 8 * size)
        k_ref[r, :] = dot_nt(act_ref[r, :], wt_ref[local : 2 * local, :]).astype(jnp.bfloat16)
        vt = dot_nt(wt_ref[2 * local :, :], act_ref[r, :]) + bias_ref[2 * local :, :]
        vt_ref[:, r] = vt.astype(jnp.bfloat16)

        @pl.when(at == z)
        def _():
            qt = dot_nt(wt_ref[:local, :], act_ref[r, :]) + bias_ref[:local, :]
            qt_ref[...] = qt.astype(jnp.bfloat16) * jnp.bfloat16(HD**-0.5)

    def y_copy(i):
        return pltpu.make_async_remote_copy(
            src_ref=y_out.at[i],
            dst_ref=y_in.at[i],
            send_sem=ys.at[i],
            recv_sem=yr.at[i],
            device_id=device(z, 1 - y, x, c),
            device_id_type=MESH,
        )

    def r_copy(i):
        return pltpu.make_async_remote_copy(
            src_ref=r_out.at[i],
            dst_ref=r_in.at[i],
            send_sem=rs.at[i],
            recv_sem=rr.at[i],
            device_id=device(z + 1, y, x, c),
            device_id_type=MESH,
        )

    def l_copy(i):
        return pltpu.make_async_remote_copy(
            src_ref=l_out.at[i],
            dst_ref=l_in.at[i],
            send_sem=ls.at[i],
            recv_sem=lr.at[i],
            device_id=device(z - 1, y, x, c),
            device_id_type=MESH,
        )

    def add(ref, copy, i):
        copy(i).wait_recv()
        acc[...] += ref[i].astype(jnp.float32)

    def flow(zp, yp, first):
        i = zp * 2 + yp

        @pl.when(z < zp)
        def _():
            first()

            @pl.when(z > 0)
            def _():
                add(r_in, r_copy, i)

            r_out[i] = acc[...].astype(jnp.bfloat16)
            r_copy(i).start()

        @pl.when(z > zp)
        def _():
            first()

            @pl.when(z < 3)
            def _():
                add(l_in, l_copy, i)

            l_out[i] = acc[...].astype(jnp.bfloat16)
            l_copy(i).start()

    def land(yp):
        @pl.when(z > 0)
        def _():
            add(r_in, r_copy, z * 2 + yp)

        @pl.when(z < 3)
        def _():
            add(l_in, l_copy, z * 2 + yp)

    low = z < 2
    order = [
        jnp.where(low, 3, 0),
        jnp.where(low, 2, 1),
        jnp.where(low, 1 - z, 5 - z),
    ]

    @pl.when(c == 0)
    def _():
        for zp in order + [z]:
            y_out[zp] = piece(zp, 1 - y).astype(jnp.bfloat16)
            y_copy(zp).start()
        for zp in order:

            def first(zp=zp):
                acc[...] = piece(zp, y)
                add(y_in, y_copy, zp)

            flow(zp, y, first)
        acc[...] = piece(z, y)
        add(y_in, y_copy, z)
        land(y)
        own[...] = acc[...].astype(jnp.bfloat16)
        for zp in range(4):
            y_copy(zp).wait_send()

    @pl.when(c == 1)
    def _():
        for zp in order:
            for yp in (0, 1):

                def first(zp=zp, yp=yp):
                    acc[...] = piece(zp, yp)

                flow(zp, yp, first)
        acc[...] = piece(z, 1 - y)
        land(1 - y)
        y_out[0] = acc[...].astype(jnp.bfloat16)
        y_copy(0).start()
        acc[...] = piece(z, y)
        land(y)
        add(y_in, y_copy, 0)
        own[...] = acc[...].astype(jnp.bfloat16)
        y_copy(0).wait_send()

    for zp in range(4):
        for yp in (0, 1):
            used = (c == 1) | (y == yp)

            @pl.when(used & (z < zp))
            def _(i=zp * 2 + yp):
                r_copy(i).wait_send()

            @pl.when(used & (z > zp))
            def _(i=zp * 2 + yp):
                l_copy(i).wait_send()

    gather_steps([own], [x_all], gather_sems, project)


def pack_gather(parts, wt, bias, rows8, cid):
    _, size, width = parts.shape
    bf16 = jnp.bfloat16
    rows = 32 * size
    local = wt.shape[0] // 3
    slots = pltpu.VMEM((8, size, width), bf16)
    quarter = pltpu.VMEM((4, size, width), bf16)
    return pl.pallas_call(
        pack_kernel,
        out_shape=(
            jax.ShapeDtypeStruct((size, width), bf16),
            jax.ShapeDtypeStruct((rows, width), bf16),
            jax.ShapeDtypeStruct((rows, local), bf16),
            jax.ShapeDtypeStruct((local, rows), bf16),
            jax.ShapeDtypeStruct((local, 8 * size), bf16),
        ),
        in_specs=[VMEM] * 4,
        out_specs=[VMEM] * 5,
        scratch_shapes=[
            pltpu.VMEM((rows, width), bf16),
            pltpu.VMEM((size, width), jnp.float32),
            quarter,
            quarter,
            slots,
            slots,
            slots,
            slots,
            DMA((4,)),
            DMA((4,)),
            DMA((8,)),
            DMA((8,)),
            DMA((8,)),
            DMA((8,)),
        ]
        + GATHER_SEMS,
        compiler_params=pltpu.CompilerParams(
            collective_id=cid, has_side_effects=True, vmem_limit_bytes=60 << 20
        ),
        cost_estimate=cost(90),
        name="pack_gather",
    )(parts, wt, bias[:, None], rows8)


def share_start(p_ref, landed, sends, send_sem, recv_sem):
    z, y, x, c = coords()

    def to_core(i):
        return pltpu.make_async_remote_copy(
            src_ref=p_ref.at[i * 2 + 1 - c],
            dst_ref=landed.at[i],
            send_sem=send_sem.at[i],
            recv_sem=recv_sem.at[i],
            device_id=device(z, y, x, 1 - c),
            device_id_type=MESH,
        )

    to_chip = pltpu.make_async_remote_copy(
        src_ref=sends,
        dst_ref=landed.at[2],
        send_sem=send_sem.at[2],
        recv_sem=recv_sem.at[2],
        device_id=device(z, y, 1 - x, c),
        device_id_type=MESH,
    )
    for i in (1 - x, x):
        to_core(i).start()
    return p_ref, landed, sends, to_core, to_chip


def share_pass(share):
    p_ref, landed, sends, to_core, to_chip = share
    _, _, x, c = coords()
    to_core(1 - x).wait_recv()
    total = p_ref[(1 - x) * 2 + c].astype(jnp.float32) + landed[1 - x].astype(jnp.float32)
    sends[...] = total.astype(jnp.bfloat16)
    to_chip.start()


def share_sum(share):
    p_ref, landed, sends, to_core, to_chip = share
    _, _, x, c = coords()
    to_core(x).wait_recv()
    total = p_ref[x * 2 + c].astype(jnp.float32) + landed[x].astype(jnp.float32)
    to_chip.wait_recv()
    total += landed[2].astype(jnp.float32)
    for i in (0, 1):
        to_core(i).wait_send()
    to_chip.wait_send()
    return total


def share_scratch(size, width):
    bf16 = jnp.bfloat16
    return [pltpu.VMEM((3, size, width), bf16), pltpu.VMEM((size, width), bf16), DMA((3,)), DMA((3,))]


def load_all(sources, targets, sems):
    copies = [
        pltpu.make_async_copy(a, b, sems.at[i]) for i, (a, b) in enumerate(zip(sources, targets))
    ]
    for copy in copies:
        copy.start()
    return copies


def products(units, early):
    total = sum(count for _, count in units)
    each = (total - early + 9) // 10

    def run(job):
        before = 0
        for unit, count in units:
            pl.when((job >= before) & (job < before + count))(functools.partial(unit, job - before))
            before += count

    def now():
        pl.loop(0, early)(run)

    def ahead(step):
        @pl.when(step < 10)
        def _():
            pl.loop(0, each)(lambda i: run(early + step * each + i))

    return now, ahead


def outer_unit(a, b, out, tall, wide):
    across = b.shape[1] // wide

    def unit(job):
        n = pl.ds(pl.multiple_of(lax.rem(job, across) * wide, 128), wide)
        if tall == out.shape[0]:
            out[:, n] = dot_tn(a[:, :tall], b[:, n]).astype(out.dtype)
        else:
            m = pl.ds(pl.multiple_of(job // across * tall, 128), tall)
            out[m, n] = dot_tn(a[:, m], b[:, n]).astype(out.dtype)

    return unit, out.shape[0] // tall * across


def first_kernel(
    p_ref, x_ref, rows_ref, wt_ref, wbias_ref, act_ref,
    mid_ref, o_ref, qkt_ref, v_ref,
    own, act, load_sem, landed, sends, ss, sr, *sems,
):
    (load,) = load_all((act_ref,), (act,), load_sem)
    greet_grid()
    share = share_start(p_ref, landed, sends, ss, sr)
    share_pass(share)
    local = v_ref.shape[1]
    chunk = act.shape[0] // 4
    load.wait()

    def project(job):
        r = pl.ds(pl.multiple_of(job // 3 * chunk, 128), chunk)
        kind = lax.rem(job, 3)

        @pl.when(kind == 0)
        def _():
            qt = dot_nt(wt_ref[:local, :], act[r, :]) + wbias_ref[:local, :]
            qkt_ref[:local, r] = qt.astype(jnp.bfloat16) * jnp.bfloat16(HD**-0.5)

        @pl.when(kind == 1)
        def _():
            kt = dot_nt(wt_ref[local : 2 * local, :], act[r, :])
            qkt_ref[local:, r] = kt.astype(jnp.bfloat16)

        @pl.when(kind == 2)
        def _():
            v = dot_nt(act[r, :], wt_ref[2 * local :, :]) + wbias_ref[2 * local :, :].T
            v_ref[r, :] = v.astype(jnp.bfloat16)

    pl.loop(0, 2)(project)
    middle = x_ref[...].astype(jnp.float32) + share_sum(share) + rows_ref[4:5, :]
    mid_ref[...] = middle
    _, _, pre = layer_norm(middle, rows_ref[2:3, :], rows_ref[3:4, :])
    own[...] = pre.astype(jnp.bfloat16)

    def ahead(step):
        pl.when(step < 10)(functools.partial(project, step + 2))

    gather_steps([own], [o_ref], sems, ahead=ahead)


def first_exchange(part, source, rows8, wt, bias, act1, cid):
    size, width = source.shape
    rows = 32 * size
    local = wt.shape[0] // 3
    bf16 = jnp.bfloat16
    return pl.pallas_call(
        first_kernel,
        out_shape=(
            jax.ShapeDtypeStruct((size, width), jnp.float32),
            jax.ShapeDtypeStruct((rows, width), bf16),
            jax.ShapeDtypeStruct((2 * local, rows), bf16),
            jax.ShapeDtypeStruct((rows, local), bf16),
        ),
        in_specs=[VMEM] * 5 + [ANY],
        out_specs=[VMEM, ANY, VMEM, VMEM],
        scratch_shapes=[pltpu.VMEM((size, width), bf16), pltpu.VMEM((rows, width), bf16), DMA((1,))]
        + share_scratch(size, width)
        + GATHER_SEMS,
        compiler_params=pltpu.CompilerParams(
            collective_id=cid, has_side_effects=True, vmem_limit_bytes=60 << 20
        ),
        cost_estimate=cost(60),
        name="first_exchange",
    )(
        part.reshape(4, size, width), source, rows8, wt, bias[:, None], act1,
    )


def second_kernel(
    mid_ref, up_ref, rows_ref, wout_ref, act_ref, hid_ref, dpre_ref, upall_ref, wup_ref, wdown_ref,
    dmid_ref, mixed_ref, vec_ref, o_ref, gup_ref, gdown_ref, dctx_ref,
    own, part, branch, landed, sends, ss, sr, landed2, sends2, ss2, sr2, some, act, hid, dpre, upall,
    load_sem, *sems,
):
    loads = load_all(
        (dpre_ref, wup_ref, hid_ref, wdown_ref, act_ref, upall_ref),
        (dpre, gup_ref, hid, gdown_ref, act, upall),
        load_sem,
    )
    greet_grid()
    size = own.shape[0]
    mine = pl.ds(pl.multiple_of(lax.axis_index("dp") * 4 * size, 64), 4 * size)
    loads[0].wait()
    loads[1].wait()
    part[...] = dot_nt(dpre[mine, :], gup_ref[...]).astype(jnp.bfloat16).reshape(part.shape)
    share = share_start(part, landed, sends, ss, sr)
    loads[2].wait()
    loads[3].wait()
    branch[...] = dot_nn(hid[mine, :], gdown_ref[...]).astype(jnp.bfloat16).reshape(branch.shape)
    branch_share = share_start(branch, landed2, sends2, ss2, sr2)
    share_pass(share)
    share_pass(branch_share)
    now, work = products(
        [outer_unit(act, dpre, gup_ref, 256, 1280), outer_unit(hid, upall, gdown_ref, 256, 1280)], 2
    )
    for load in loads[4:]:
        load.wait()
    now()
    grad = share_sum(share)
    middle = mid_ref[...]
    normed, rstd, _ = layer_norm(middle, 1.0, 0.0)
    d_middle = up_ref[...].astype(jnp.float32) + layer_norm_back(grad, normed, rstd, rows_ref[2:3, :])
    own[...] = d_middle.astype(jnp.bfloat16)
    dmid_ref[...] = d_middle
    vec_ref[...] = jnp.concatenate(
        [
            jnp.sum(grad * normed, 0, keepdims=True),
            jnp.sum(grad, 0, keepdims=True),
            jnp.sum(up_ref[...].astype(jnp.float32), 0, keepdims=True),
            jnp.sum(d_middle, 0, keepdims=True),
            jnp.zeros((4, grad.shape[1]), jnp.float32),
        ],
        0,
    )
    def ahead(step):
        @pl.when(step == 0)
        def _():
            total = share_sum(branch_share)
            mixed_ref[...] = (mid_ref[...] + total + rows_ref[5:6, :]).astype(jnp.bfloat16)

        work(step)

    count = some.shape[0]

    def context_grad(at):
        @pl.loop(0, 8 * size // count)
        def _(i):
            r = pl.ds(pl.multiple_of(at * 8 * size + i * count, 128), count)
            pltpu.sync_copy(o_ref.at[r], some)
            dctx_ref[:, r] = dot_nt(wout_ref[...], some[...]).astype(jnp.bfloat16)

    gather_steps([own], [o_ref], sems, context_grad, ahead)


def second_exchange(middle, upstream, rows8, w_out, act2, hidden, d_pre, up_all, w_up, w_down, cid):
    size, width = middle.shape
    f32, bf16 = jnp.float32, jnp.bfloat16
    rows, inner = hidden.shape
    block = pltpu.VMEM((4, size, width), bf16)
    return pl.pallas_call(
        second_kernel,
        out_shape=(
            jax.ShapeDtypeStruct((size, width), f32),
            jax.ShapeDtypeStruct((size, width), bf16),
            jax.ShapeDtypeStruct((8, width), f32),
            jax.ShapeDtypeStruct((rows, width), bf16),
            jax.ShapeDtypeStruct((width, inner), bf16),
            jax.ShapeDtypeStruct((inner, width), bf16),
            jax.ShapeDtypeStruct((w_out.shape[0], rows), bf16),
        ),
        in_specs=[VMEM] * 4 + [ANY] * 6,
        out_specs=[VMEM, VMEM, VMEM, ANY, VMEM, VMEM, VMEM],
        scratch_shapes=[pltpu.VMEM((size, width), bf16), block, block]
        + share_scratch(size, width) * 2
        + [pltpu.VMEM((8 * size if size % 32 else 4 * size, width), bf16)]
        + [pltpu.VMEM((rows, n), bf16) for n in (width, inner, inner, width)]
        + [DMA((6,))]
        + GATHER_SEMS,
        compiler_params=pltpu.CompilerParams(
            collective_id=cid, has_side_effects=True, vmem_limit_bytes=62 << 20
        ),
        cost_estimate=cost(80),
        name="second_exchange",
    )(middle, upstream, rows8, w_out, act2, hidden, d_pre, up_all, w_up, w_down)


def third_kernel(
    p_ref, x_ref, dmid_ref, rows_ref, vec_ref, act_ref, dt_ref, ctx_ref, dmall_ref,
    o_ref, vo_ref, gqkv_ref, gout_ref,
    own, vec, landed, sends, ss, sr, act, dt, ctx, dmall, load_sem, *sems,
):
    loads = load_all((act_ref, dt_ref, ctx_ref, dmall_ref), (act, dt, ctx, dmall), load_sem)
    greet_grid()
    share = share_start(p_ref, landed, sends, ss, sr)
    share_pass(share)
    part = dt.shape[0] // 3

    def project(job):
        k = pl.ds(pl.multiple_of(job // 2 * part, 64), part)
        m = pl.ds(pl.multiple_of(lax.rem(job, 2) * 640, 128), 640)
        gqkv_ref[k, m] = dot_nn(dt[k, :], act[:, m]).astype(jnp.bfloat16)

    now, work = products([(project, 6), outer_unit(ctx, dmall, gout_ref, part, 640)], 2)
    for load in loads:
        load.wait()
    now()
    grad = share_sum(share)
    normed, rstd, _ = layer_norm(x_ref[...].astype(jnp.float32), 1.0, 0.0)
    own[...] = (dmid_ref[...] + layer_norm_back(grad, normed, rstd, rows_ref[0:1, :])).astype(jnp.bfloat16)
    vec[...] = jnp.concatenate(
        [
            vec_ref[0:4, :],
            jnp.sum(grad * normed, 0, keepdims=True),
            jnp.sum(grad, 0, keepdims=True),
            jnp.zeros((2, grad.shape[1]), jnp.float32),
        ],
        0,
    )
    gather_steps([own, vec], [o_ref, vo_ref], sems, ahead=work)


def third_exchange(part, source, d_middle, rows8, vec, act1, d_qkv, context, d_middle_all, cid):
    size, width = d_middle.shape
    f32, bf16 = jnp.float32, jnp.bfloat16
    rows = act1.shape[0]
    total = d_qkv.shape[0]
    return pl.pallas_call(
        third_kernel,
        out_shape=(
            jax.ShapeDtypeStruct((rows, width), bf16),
            jax.ShapeDtypeStruct((256, width), f32),
            jax.ShapeDtypeStruct((total, width), bf16),
            jax.ShapeDtypeStruct((total // 3, width), bf16),
        ),
        in_specs=[VMEM] * 5 + [ANY] * 4,
        out_specs=[ANY, ANY, VMEM, VMEM],
        scratch_shapes=[pltpu.VMEM((size, width), bf16), pltpu.VMEM((8, width), f32)]
        + share_scratch(size, width)
        + [pltpu.VMEM(a.shape, bf16) for a in (act1, d_qkv, context, d_middle_all)]
        + [DMA((4,))]
        + GATHER_SEMS * 2,
        compiler_params=pltpu.CompilerParams(
            collective_id=cid, has_side_effects=True, vmem_limit_bytes=60 << 20
        ),
        cost_estimate=cost(60),
        name="third_exchange",
    )(
        part.reshape(4, size, width), source, d_middle, rows8, vec,
        act1, d_qkv, context, d_middle_all,
    )


def dot_nt(a, b):
    return lax.dot_general(a, b, (((1,), (1,)), ((), ())), preferred_element_type=jnp.float32)


def dot_nn(a, b):
    return lax.dot_general(a, b, (((1,), (0,)), ((), ())), preferred_element_type=jnp.float32)


def dot_tn(a, b):
    return lax.dot_general(a, b, (((0,), (0,)), ((), ())), preferred_element_type=jnp.float32)


def spans(offset_ref, length_ref, first, count):
    row = lax.broadcasted_iota(jnp.int32, (1, count), 1) + first
    start = jnp.zeros((1, count), jnp.int32)
    end = jnp.zeros((1, count), jnp.int32)
    low, high = 1 << 20, 0
    for i in range(8):
        a = offset_ref[i]
        b = a + length_ref[i]
        inside = (row >= a) & (row < b)
        start = jnp.where(inside, a, start)
        end = jnp.where(inside, b, end)
        used = (a < first + count) & (b > first) & (b > a)
        low = jnp.where(used, jnp.minimum(low, a // BK), low)
        high = jnp.where(used, jnp.maximum(high, (b + BK - 1) // BK), high)
    return start, end, low, high


def attend_kernel(heads, offset_ref, length_ref, qt_ref, k_ref, vt_ref, sent_ref, m_s, l_s, acc_s, win):
    mine = sent_ref.shape[0]
    rows = win.shape[0]
    local = heads * HD
    span = range(heads)
    dp = lax.axis_index("dp")
    skip = lax.rem(dp, 2) * (mine % 128)
    first = dp * mine - skip
    window = pl.ds(pl.multiple_of(lax.rem(dp, 2) * mine - skip, 128), rows)
    start, end, low, high = spans(offset_ref, length_ref, first, rows)
    m_s[...] = jnp.full_like(m_s, NEG)
    l_s[...] = jnp.zeros_like(l_s)
    acc_s[...] = jnp.zeros_like(acc_s)
    q = [qt_ref[h * HD : (h + 1) * HD, window] for h in span]

    def body(kb, carry):
        k0 = pl.multiple_of(kb * BK, BK)
        key = lax.broadcasted_iota(jnp.int32, (BK, rows), 0) + k0
        mask = (key >= start) & (key < end)
        s = [
            jnp.where(
                mask,
                dot_nn(k_ref[pl.ds(k0, BK), h * HD : (h + 1) * HD], q[h]),
                NEG,
            )
            for h in span
        ]
        p, a = [], []
        for h in span:
            old = m_s[h]
            new = jnp.maximum(old, jnp.max(s[h], 0, keepdims=True))
            e = jnp.exp(s[h] - new)
            scale = jnp.exp(old - new)
            l_s[h] = scale * l_s[h] + jnp.sum(e, 0, keepdims=True)
            m_s[h] = new
            p.append(e.astype(jnp.bfloat16))
            a.append(scale)
        for h in span:
            vt = vt_ref[h * HD : (h + 1) * HD, pl.ds(k0, BK)]
            acc_s[h] = a[h] * acc_s[h] + dot_nn(vt, p[h])
        return carry

    lax.fori_loop(low, high, body, 0)
    parts = [[], [], []]
    for h in span:
        total = l_s[h]
        total = jnp.where(total == 0.0, 1.0, total)
        rest = m_s[h] + jnp.log(total)
        for part in parts:
            part.append(rest.astype(jnp.bfloat16).astype(jnp.float32))
            rest = rest - part[-1]
        out = acc_s[h] * (1.0 / total)
        win[:, h * HD : (h + 1) * HD] = out.T
    blank = [jnp.zeros((win.shape[1] - local - 3 * heads, rows), jnp.float32)]
    win[:, local:] = jnp.concatenate(parts[0] + parts[1] + parts[2] + blank, 0).T
    sent_ref[...] = win[pl.ds(pl.multiple_of(skip, 16), mine), :].astype(jnp.bfloat16)


def whole(a):
    return pl.BlockSpec(a.shape, lambda i, *_: (0,) * len(a.shape), pipeline_mode=pl.Buffered(1))


def attend(qt, k, vt, offsets, lengths, heads):
    mine = k.shape[0] // 8
    rows = (mine + mine % 128 + 127) // 128 * 128
    local = heads * HD
    wide = (local + 3 * heads + 127) // 128 * 128
    row = pltpu.VMEM((heads, 1, rows), jnp.float32)
    return pl.pallas_call(
        functools.partial(attend_kernel, heads),
        out_shape=jax.ShapeDtypeStruct((mine, wide), jnp.bfloat16),
        in_specs=[SMEM, SMEM, VMEM, VMEM, VMEM],
        out_specs=VMEM,
        scratch_shapes=[
            row,
            row,
            pltpu.VMEM((heads, HD, rows), jnp.float32),
            pltpu.VMEM((rows, wide), jnp.float32),
        ],
        compiler_params=pltpu.CompilerParams(vmem_limit_bytes=60 << 20),
        cost_estimate=cost(10),
        name="attend",
    )(offsets, lengths, qt, k, vt)


def attend_back_kernel(
    heads, offset_ref, length_ref, k_ref, v_ref, qkt_ref, dot_ref, sent_ref, up_ref, down_ref,
    d_ref, sum_ref, up_out, down_out, dk_s, dv_s, dq_s
):
    i = pl.program_id(0)
    local = heads * HD
    span = range(heads)
    sl = [slice(h * HD, (h + 1) * HD) for h in span]
    at_q = pl.ds(pl.multiple_of(i * BQ, BQ), BQ)

    @pl.when(i == 0)
    def _():
        dk_s[...] = jnp.zeros_like(dk_s)
        dv_s[...] = jnp.zeros_like(dv_s)
        sum_ref[...] = jnp.zeros_like(sum_ref)

    start, end, low, high = spans(offset_ref, length_ref, i * BQ, BQ)
    dq_s[...] = jnp.zeros_like(dq_s)
    sent = sent_ref[at_q, :].astype(jnp.float32).T
    lse, delta = [], []
    for h in span:
        a = local + h
        lse.append(
            sent[a : a + 1] + sent[a + heads : a + heads + 1] + sent[a + 2 * heads : a + 2 * heads + 1]
        )
        delta.append(jnp.sum(dot_ref[sl[h], at_q].astype(jnp.float32) * sent[sl[h]], 0, keepdims=True))

    def blocks(first, count):
        keys = []
        for n in range(count):
            at_k = pl.ds(pl.multiple_of((first + n) * BK, BK), BK)
            key = lax.broadcasted_iota(jnp.int32, (BK, BQ), 0) + (first + n) * BK
            keys.append((at_k, (key >= start) & (key < end)))
        jobs = [(at_k, mask, h) for at_k, mask in keys for h in span]

        def products(at_k, mask, h):
            s = dot_nn(k_ref[at_k, sl[h]], qkt_ref[sl[h], at_q])
            dp = dot_nn(v_ref[at_k, sl[h]], dot_ref[sl[h], at_q])
            return s, dp

        def scores(at_k, mask, h, s, dp):
            p = jnp.exp(jnp.where(mask, s, NEG) - lse[h])
            ds = (p * (dp - delta[h])).astype(jnp.bfloat16)
            return p.astype(jnp.bfloat16), ds

        def gradients(at_k, mask, h, p, ds):
            dv_s[h, :, at_k] += dot_nt(dot_ref[sl[h], at_q], p)
            dk_s[h, :, at_k] += dot_nt(qkt_ref[sl[h], at_q], ds)
            dq_s[h] += dot_nn(qkt_ref[local + h * HD : local + (h + 1) * HD, at_k], ds)

        now = products(*jobs[0])
        held = None
        for n, job in enumerate(jobs):
            later = products(*jobs[n + 1]) if n + 1 < len(jobs) else None
            done = scores(*job, *now)
            if held is not None:
                gradients(*jobs[n - 1], *held)
            held, now = done, later
        gradients(*jobs[-1], *held)

    def pair(n, carry):
        blocks(low + 2 * n, 2)
        return carry

    pairs = jnp.maximum(high - low, 0) // 2
    lax.fori_loop(0, pairs, pair, 0)

    @pl.when(low + 2 * pairs < high)
    def _():
        blocks(low + 2 * pairs, 1)

    for src, dst in ((up_ref, up_out), (down_ref, down_out)):
        dst[...] = src[...].astype(jnp.float32)
    for h in span:
        dq = dq_s[h] * HD**-0.5
        d_ref[sl[h], at_q] = dq.astype(jnp.bfloat16)
        sum_ref[sl[h], :] += dq[:, :128] + dq[:, 128:]

    @pl.when(i == pl.num_programs(0) - 1)
    def _():
        for h in span:
            d_ref[local + h * HD : local + (h + 1) * HD, :] = dk_s[h].astype(jnp.bfloat16)
            d_ref[2 * local + h * HD : 2 * local + (h + 1) * HD, :] = dv_s[h].astype(jnp.bfloat16)
            total = dv_s[h, :, 0:128]
            for n in range(1, dv_s.shape[2] // 128):
                total += dv_s[h, :, n * 128 : (n + 1) * 128]
            sum_ref[local + h * HD : local + (h + 1) * HD, :] = total


def attend_back(k, v, qkt, dot, sent, offsets, lengths, up, down, heads):
    rows = k.shape[0]
    local = heads * HD
    tall = pltpu.VMEM((heads, HD, rows), jnp.float32)

    def const(shape):
        return pl.BlockSpec(shape, lambda i, *_: (0, 0), pipeline_mode=pl.Buffered(1))

    strips = [
        pl.BlockSpec((a.shape[0] // 10, a.shape[1]), lambda i, *_: (jnp.minimum(i, 9), 0))
        for a in (up, down)
    ]
    return pl.pallas_call(
        functools.partial(attend_back_kernel, heads),
        out_shape=(
            jax.ShapeDtypeStruct((3 * local, rows), jnp.bfloat16),
            jax.ShapeDtypeStruct((2 * local, 128), jnp.float32),
            jax.ShapeDtypeStruct(up.shape, jnp.float32),
            jax.ShapeDtypeStruct(down.shape, jnp.float32),
        ),
        grid_spec=pltpu.PrefetchScalarGridSpec(
            num_scalar_prefetch=2,
            grid=(rows // BQ,),
            in_specs=[whole(a) for a in (k, v, qkt, dot, sent)] + strips,
            out_specs=[const((3 * local, rows)), const((2 * local, 128))] + strips,
            scratch_shapes=[tall, tall, pltpu.VMEM((heads, HD, BQ), jnp.float32)],
        ),
        compiler_params=pltpu.CompilerParams(vmem_limit_bytes=60 << 20),
        cost_estimate=cost(60),
        name="attend_back",
    )(offsets, lengths, k, v, qkt, dot, sent, up, down)


def finish_kernel(
    offset_ref, length_ref, m_ref, d_ref, qkv_ref, out_ref, mo_ref, do_ref, qkv_out, out_out, m, d, sems
):
    i = pl.program_id(0)
    size = mo_ref.shape[0]
    rows = m_ref.shape[0]
    offset = offset_ref[8]
    length = length_ref[8]

    def first(n):
        return pl.multiple_of(jnp.minimum(offset + n * size, rows - size), 16)

    def loads(n):
        return [
            pltpu.make_async_copy(
                src.at[pl.ds(first(n), size)], dst.at[n, pl.ds(0, size)], sems.at[k, n]
            )
            for k, (src, dst) in enumerate(((m_ref, m), (d_ref, d)))
        ]

    @pl.when(i == 0)
    def _():
        for n in range(m.shape[0]):
            for load in loads(n):
                load.start()

    qkv_out[...] = qkv_ref[...].astype(jnp.float32)
    out_out[...] = out_ref[...].astype(jnp.float32)
    shift = pl.multiple_of(jnp.minimum(offset + i * size - first(i), size), 16)
    row = lax.broadcasted_iota(jnp.int32, (size, 1), 0) + i * size
    for load, src, dst in zip(loads(i), (m, d), (mo_ref, do_ref)):
        load.wait()
        value = jnp.where(row < length, src[i, pl.ds(shift, size), :].astype(jnp.float32), 0.0)
        dst[...] = value.astype(dst.dtype)


def finish(offsets, lengths, mixed, d_tokens, g_qkv, g_out, cap):
    width = mixed.shape[1]
    steps = cap // 128
    held = pltpu.VMEM((steps, 256, width), jnp.bfloat16)
    f32 = jnp.float32

    def strip(count):
        return pl.BlockSpec((count, width), lambda i: (i, 0))

    short = pl.BlockSpec((g_out.shape[0] // 10, width), lambda i: (jnp.minimum(i, 9), 0))
    tall = strip(g_qkv.shape[0] // steps)
    return pl.pallas_call(
        finish_kernel,
        grid=(steps,),
        out_shape=(
            jax.ShapeDtypeStruct((cap, width), jnp.bfloat16),
            jax.ShapeDtypeStruct((cap, width), f32),
            jax.ShapeDtypeStruct(g_qkv.shape, f32),
            jax.ShapeDtypeStruct(g_out.shape, f32),
        ),
        in_specs=[SMEM, SMEM, ANY, ANY, tall, short],
        out_specs=[strip(128), strip(128), tall, short],
        scratch_shapes=[held, held, DMA((2, steps))],
        compiler_params=pltpu.CompilerParams(vmem_limit_bytes=60 << 20),
        name="finish",
    )(offsets, lengths, mixed, d_tokens, g_qkv, g_out)


def packed_step(size, cids, table, args):
    (
        tokens, clip_len, _, w_qkv, bias_q, bias_v, w_out, bias_out, w_up, bias_up, w_down, bias_down,
        gain1, shift1, gain2, shift2, grad_out,
    ) = args
    f32, bf16 = jnp.float32, jnp.bfloat16
    cap, width = tokens.shape
    local = w_qkv.shape[2]
    heads = local // HD
    rows = 32 * size
    mine = 4 * size
    dp = lax.axis_index("dp")
    pack_id, first_id, second_id, third_id = cids

    x_parts, up_parts, offsets, lengths = take_pieces(tokens, grad_out, table, clip_len, size)
    wt = w_qkv.transpose(1, 2, 0).reshape(3 * local, width)
    bias = jnp.concatenate([bias_q, jnp.zeros_like(bias_q), bias_v])
    spare = jnp.zeros_like(gain1)
    rows8 = jnp.stack([gain1, shift1, gain2, shift2, bias_out, bias_down, spare, spare])
    source, act1, k, vt, qt = pack_gather(x_parts, wt, bias, rows8, pack_id)
    up_own = lax.psum_scatter(up_parts, "dp", scatter_dimension=0, tiled=True)
    up_own, source = lax.optimization_barrier((up_own, source))
    up_all = lax.all_gather(up_own.reshape(size, width), ("dp", "tensor"), tiled=True)

    sent_own = attend(qt, k, vt, offsets, lengths, heads)
    part = jnp.dot(sent_own[:, :local], w_out, preferred_element_type=f32).astype(bf16)
    sent = lax.all_gather(sent_own, "dp", tiled=True)
    middle, act2, qkt, v = first_exchange(
        part, source, rows8, wt, bias, act1, first_id
    )

    pre = jnp.dot(act2, w_up, preferred_element_type=f32) + bias_up
    hidden_f, slope = gelu_pair(pre)
    hidden = hidden_f.astype(bf16)
    d_pre = contract_last(up_all, w_down) * slope
    g_up_bias = jnp.sum(d_pre, 0)
    d_pre_b = d_pre.astype(bf16)
    d_middle, mixed, vec, d_middle_b, g_up, g_down, d_context = second_exchange(
        middle, up_own.reshape(size, width), rows8, w_out, act2, hidden, d_pre_b, up_all,
        w_up, w_down, second_id,
    )
    mixed_all = lax.all_gather(mixed, ("dp", "tensor"), tiled=True)
    d_qkv, column, g_up, g_down = attend_back(
        k, v, qkt, d_context, sent, offsets, lengths, g_up, g_down, heads
    )
    column = jnp.sum(column, 1)
    d_own = lax.dynamic_slice_in_dim(d_qkv, dp * mine, mine, 1)
    d_act1 = jnp.einsum("kr,kd->rd", d_own, wt, preferred_element_type=f32).astype(bf16)
    d_tokens_all, vectors_all, g_qkv, g_out = third_exchange(
        d_act1, source, d_middle, rows8, vec, act1, d_qkv, sent, d_middle_b, third_id
    )
    sums = jnp.sum(vectors_all.reshape(32, 8, width), 0)
    mixed, d_tokens, g_qkv, g_out = finish(
        offsets, lengths, mixed_all, d_tokens_all, g_qkv, g_out, cap
    )
    g_qkv = g_qkv.reshape(3, local, width).transpose(2, 0, 1)

    return (
        mixed,
        d_tokens,
        g_qkv,
        column[:local],
        column[local:],
        g_out,
        sums[3],
        g_up,
        g_up_bias,
        g_down,
        sums[2],
        sums[4],
        sums[5],
        sums[0],
        sums[1],
    )


def packed(*args):
    clip_len, slot_clip = args[1], args[2]

    def padded(value):
        return (value + 15) // 16 * 16

    need = jnp.sum(padded(clip_len))
    table = gather_table(slot_clip[0], 0)
    branches = [
        functools.partial(packed_step, size, [1 + 4 * n + i for i in range(4)])
        for n, size in enumerate(BLOCKS)
    ]
    rank = sum((need > 32 * size).astype(jnp.int32) for size in sorted(BLOCKS))
    pick = jnp.array([BLOCKS.index(size) for size in sorted(BLOCKS)] + [len(BLOCKS)], jnp.int32)[rank]

    def fallback(table, args):
        return plain(*args)

    return lax.switch(pick, branches + [fallback], table, args)


def solution(mesh):
    placed = (
        P("dp", None),
        P(),
        P("dp"),
        P(None, None, "tensor"),
        P("tensor"),
        P("tensor"),
        P("tensor", None),
        P(),
        P(None, "tensor"),
        P("tensor"),
        P("tensor", None),
        P(),
        P(),
        P(),
        P(),
        P(),
        P("dp", None),
    )
    fits = mesh.shape["dp"] == 8 and mesh.shape["tensor"] == 4
    return jax.shard_map(
        packed if fits else plain,
        mesh=mesh,
        in_specs=placed,
        out_specs=(
            P("dp", None),
            P("dp", None),
            P(None, None, "tensor"),
            P("tensor"),
            P("tensor"),
            P("tensor", None),
            P(),
            P(None, "tensor"),
            P("tensor"),
            P("tensor", None),
            P(),
            P(),
            P(),
            P(),
            P(),
        ),
        check_vma=False,
    )
```
